128 devices in a mesh: blk: 16 (over z, y_lo, core), exp: 8 (over y_hi, x).
Axes of the slice: x: 4, y: 4 (y_hi: 2, y_lo: 2; y = y_hi * 2 + y_lo), z: 4, core: 2. Of those that a mesh axis runs over, the one named last changes fastest.
Arguments:
- nodes: bfloat16 [24576, 512], P('blk'), may hold values from -8 to 8
- attention_weights: bfloat16 [3, 256, 512], P(None, 'exp'), may hold values from -1.5 to 1.5
- output_weight: bfloat16 [256, 512], P('exp'), may hold values from -2 to 2
- router_weight: bfloat16 [8, 512], replicated, may hold values from -1.25 to 1.25
- gain_first: float32 [512], replicated, may hold values from 0.1 to 1.9
- gain_second: float32 [512], replicated, may hold values from 0.1 to 1.9
- expert_in: bfloat16 [8, 2048, 512], P('exp', 'blk'), may hold values from -0.25 to 0.25
- expert_out: bfloat16 [8, 2048, 512], P('exp', 'blk'), may hold values from -0.125 to 0.125
- routes: int32 [24576, 2], P(('blk', 'exp')), may hold values from 0 to 7, all different within a row; in each aligned block of 192 rows (0 to 191, 192 to 383, ...) at most 96 rows name the same one
- cotangent: bfloat16 [24576, 512], P(('blk', 'exp')), may hold values from -6 to 6
Outputs:
- layer_out: bfloat16 [24576, 512], P(('blk', 'exp'))
- stream_grad: bfloat16 [24576, 512], P(('blk', 'exp'))
- expert_in_grad: float32 [8, 2048, 512], P('exp', 'blk')
- expert_out_grad: float32 [8, 2048, 512], P('exp', 'blk')
- router_grad: float32 [8, 512], replicated
- gain_grad: float32 [512], replicated
The draws below stay inside these ranges and needn't reach their ends.
Inputs may be any that keep to these rules, and one draw needn't show every extreme that they name: `routes`: each row names two different experts. Among the rows of one device (aligned blocks of 192 rows) no expert is named by more than 96 rows, and in some block one expert is named by exactly 96 rows.
All inputs are finite; a program needn't handle non-finite values.
Results may differ from the reference program's by a relative error of at most 0.04.
The reference program's roundings to bfloat16 on the way count: a program that leaves them out, or rounds other values in their place, can miss the bound.
Values may be sent and summed in bfloat16 or wider, within the bound.
No kernel may reach another device: no remote copies, remote signals or barrier semaphores. Data moves between devices by JAX's collectives and lax.ppermute only.
A program may use at most 64 MiB of HBM per device.

```python
import math
import jax
import jax.numpy as jnp
import numpy as np
from jax import lax

D = 512
HEADS = 8
HD = 32
HID = 2048
NODES = 24576
EXPERTS = 8
SUB = 192
CAP = 96


def draw_nodes(key, part):
    second = jax.random.fold_in(key, 1)
    result = jnp.clip(jax.random.normal(second, (NODES, D), jnp.float32), -6.0, 6.0)
    return result.astype(jnp.bfloat16)


def draw_attention_weights(key, part):
    first = jax.random.fold_in(key, 0)
    second = jax.random.fold_in(key, 1)
    fourth = jax.random.fold_in(key, 3)
    spread = 1.0 / math.sqrt(D)
    query_part = 1.7 * spread * jax.random.normal(first, (HEADS * HD, D), jnp.float32)
    key_part = 1.7 * spread * jax.random.normal(second, (HEADS * HD, D), jnp.float32)
    value_part = spread * jax.random.normal(fourth, (HEADS * HD, D), jnp.float32)
    return jnp.clip(jnp.stack([query_part, key_part, value_part]), -1.5, 1.5).astype(jnp.bfloat16)


def levels(stream_key, shape, cuts, low, largest):
    def one(dim, shards_of):
        heights = jax.random.uniform(jax.random.fold_in(jax.random.fold_in(stream_key, 6), dim), (shards_of,), jnp.float32, low / len(cuts), largest / len(cuts))
        return jnp.repeat(jnp.exp(heights), shape[dim] // shards_of).reshape((-1,) + (1,) * (len(shape) - dim - 1))

    factor_of = one(*cuts[0])
    for cut in cuts[1:]:
        factor_of = factor_of * one(*cut)
    return factor_of


def deal_out(own_key, own, number, rows, count, top, limit, slope):
    sequence = jax.random.permutation(own_key, count)
    packed, common = portions_of(count, rows * top, limit, slope, True), portions_of(count, rows * top, limit, slope, False)
    places = jnp.arange(count)

    def named(lengths, rotation):
        used = int((lengths > 0).sum())
        fixed = max(1, used // 4)
        moved = fixed + (places - fixed + rotation * (used - fixed)) % max(1, count - fixed)
        return jnp.zeros((count,), jnp.int32).at[sequence[jnp.where(places < fixed, places, moved)]].set(jnp.asarray(lengths, jnp.int32))

    lengths = jnp.where(number % 4 == 0, named(packed, number // 4), named(common, number - number // 4 - 1))
    mixed = jax.random.permutation(jax.random.fold_in(own, 3), count)
    source_of, sink = mixed[0:count // 2 * 2:2], mixed[1:count // 2 * 2:2]
    slack = jnp.minimum(lengths[source_of] - 1, limit - lengths[sink]) // 2
    slack = jnp.where((source_of == sequence[0]) | (sink == sequence[0]) | (lengths[sink] == 0), 0, jnp.maximum(slack, 0))
    moved = jax.random.randint(jax.random.fold_in(own, 4), (count // 2,), 0, 1 << 20) % (slack + 1)
    lengths = lengths.at[source_of].add(-moved).at[sink].add(moved)
    items = jnp.searchsorted(jnp.cumsum(lengths), jnp.arange(rows * top), side="right").astype(jnp.int32)
    table = items.reshape(top, rows).T
    table = table[jax.random.permutation(jax.random.fold_in(own, 1), rows)]
    rotation = jax.random.randint(jax.random.fold_in(own, 2), (rows, 1), 0, top)
    return jnp.take_along_axis(table, (jnp.arange(top)[None, :] + rotation) % top, axis=1)


def portions_of(number_of, total, limit, slope, full):
    portions = [(1 << 20) // math.isqrt(rank ** slope) + 1 for rank in range(1, number_of + 1)]
    largest = limit if full else min(limit, max(-(-total // number_of), total * portions[0] // sum(portions)))
    least = 1 if total - largest >= number_of - 1 else 0
    given, rest = [largest] + [least] * (number_of - 1), total - largest - least * (number_of - 1)
    while rest > 0:
        movable = [i for i in range(1, number_of) if given[i] < largest] or [i for i in range(1, number_of) if given[i] < limit]
        mass, remaining = sum([portions[i] for i in movable]), rest
        for i in movable:
            extra = min(limit - given[i], max(1, remaining * portions[i] // mass), rest)
            given[i] = given[i] + extra
            rest = rest - extra
    return np.array(given)


def gaussian(rng, dims, width, limit, shards=(), kind=jnp.bfloat16):
    drawn = width * jax.random.normal(rng, dims, jnp.float32)
    if shards:
        drawn = drawn * levels(rng, dims, shards, -0.22, 0.18)
    return jnp.clip(drawn, -limit, limit).astype(kind)


def setup_inputs(seed: int = 0) -> dict:
    streams_of = jax.random.split(jax.random.key(seed), 11)
    nodes = draw_nodes(jax.random.fold_in(streams_of[10], 71), 0)
    attention_weights = draw_attention_weights(jax.random.fold_in(streams_of[10], 71), 0)
    output_weight = gaussian(streams_of[2], (HEADS * HD, D), (2.0 * (HEADS * HD) ** -0.5), 2.0, ((0, 8),))
    router_weight = gaussian(streams_of[3], (EXPERTS, D), (2.0 * D ** -0.5), 1.25)
    gain_first = jnp.clip(1.0 + 0.18 * jax.random.normal(streams_of[4], (D,), jnp.float32), 0.1, 1.9)
    gain_second = jnp.clip(1.0 + 0.18 * jax.random.normal(streams_of[5], (D,), jnp.float32), 0.1, 1.9)
    expert_in = gaussian(streams_of[6], (EXPERTS, HID, D), D ** -0.5, 0.25, ((0, 8), (1, 16)))
    expert_out = gaussian(streams_of[7], (EXPERTS, HID, D), HID ** -0.5, 0.125, ((0, 8), (1, 16)))
    routes_keys = jax.random.split(jax.random.fold_in(streams_of[8], 1), NODES // SUB)
    routes_turns = jax.random.permutation(jax.random.fold_in(streams_of[8], 3), NODES // SUB)
    routes = jax.vmap(lambda own, number: deal_out(jax.random.fold_in(streams_of[8], 2), own, number, SUB, EXPERTS, 2, CAP, 2))(routes_keys, routes_turns).reshape((NODES, 2))
    cotangent = gaussian(streams_of[9], (NODES, D), 1.0, 6.0, ((0, 128),))
    return {"nodes": nodes, "attention_weights": attention_weights, "output_weight": output_weight, "router_weight": router_weight, "gain_first": gain_first, "gain_second": gain_second, "expert_in": expert_in, "expert_out": expert_out, "routes": routes, "cotangent": cotangent}


EPSILON = 1e-06

def rms_gain(stream, gain):
    return stream * lax.rsqrt(lax.optimization_barrier(jnp.mean(stream * stream, axis=-1, keepdims=True)) + EPSILON) * gain

def gelu_tanh(values):
    return jax.nn.gelu(values, approximate=True)

def head_attention(query_rows, key_rows, value_rows):
    scores = jnp.dot(query_rows, key_rows.T, preferred_element_type=jnp.float32) * (1.0 / math.sqrt(HD))
    row_max = lax.optimization_barrier(jnp.max(scores, axis=-1, keepdims=True))
    weights = jnp.exp(scores - row_max)
    totals = lax.optimization_barrier(jnp.sum(weights, axis=-1, keepdims=True))
    summed = jnp.dot(weights.astype(jnp.bfloat16), value_rows, preferred_element_type=jnp.float32)
    return (summed / totals).astype(jnp.bfloat16)

def attention(query, key_all, value_all):
    query_block = math.gcd(NODES, 1024)
    query_count = NODES // query_block
    query_heads = query.reshape(query_count, query_block, HEADS, HD).transpose(2, 0, 1, 3)
    key_heads = key_all.reshape(NODES, HEADS, HD).transpose(1, 0, 2)
    value_heads = value_all.reshape(NODES, HEADS, HD).transpose(1, 0, 2)

    def per_head(operands):
        queries, key_rows, value_rows = operands
        return lax.map(lambda query_rows: head_attention(query_rows, key_rows, value_rows), queries)
    result = lax.map(per_head, (query_heads, key_heads, value_heads))
    return result.transpose(1, 2, 0, 3).reshape(NODES, HEADS * HD)

def reference(nodes, attention_weights, output_weight, router_weight, gain_first, gain_second, expert_in, expert_out, routes, cotangent):
    blocks = NODES // SUB
    grad_scale = 1.0 / math.sqrt(NODES)
    query = jnp.dot(nodes, attention_weights[0].T, preferred_element_type=jnp.float32).astype(jnp.bfloat16)
    key_all = jnp.dot(nodes, attention_weights[1].T, preferred_element_type=jnp.float32).astype(jnp.bfloat16)
    value_all = jnp.dot(nodes, attention_weights[2].T, preferred_element_type=jnp.float32).astype(jnp.bfloat16)
    head_outputs = attention(query, key_all, value_all)
    attn_out = jnp.dot(head_outputs, output_weight, preferred_element_type=jnp.float32)
    stream = rms_gain(nodes.astype(jnp.float32) + attn_out, gain_first).astype(jnp.bfloat16)
    logits = jnp.dot(stream, router_weight.T, preferred_element_type=jnp.float32)

    def gate_values(values):
        picked = jnp.take_along_axis(jax.nn.sigmoid(values), routes, axis=1)
        return picked / lax.optimization_barrier(jnp.sum(picked, axis=-1, keepdims=True))
    gates, gate_back = jax.vjp(gate_values, logits)
    flat_routes = routes.reshape(blocks, 2 * SUB)
    choose = (flat_routes[..., None] == jnp.arange(EXPERTS, dtype=jnp.int32)).astype(jnp.int32)
    before = jnp.cumsum(choose, axis=1) - choose
    position = (flat_routes * CAP + lax.optimization_barrier(jnp.sum(before * choose, axis=-1))).astype(jnp.int32)
    block_ids = jnp.arange(blocks, dtype=jnp.int32)[:, None]

    def to_experts(assigned):
        buffer = jnp.zeros((blocks, EXPERTS * CAP, D), jnp.bfloat16).at[block_ids, position].set(assigned)
        return buffer.reshape(blocks, EXPERTS, CAP, D).transpose(1, 0, 2, 3).reshape(EXPERTS, blocks * CAP, D)

    def from_experts(buffer):
        regrouped = buffer.reshape(EXPERTS, blocks, CAP, D).transpose(1, 0, 2, 3).reshape(blocks, EXPERTS * CAP, D)
        return regrouped[block_ids, position].reshape(NODES, 2, D).astype(jnp.float32)
    tokens_in = to_experts(jnp.repeat(stream, 2, axis=0).reshape(blocks, 2 * SUB, D))

    def forward_one(operands):
        rows_in, weight_in, weight_out = operands
        pre_act = jnp.dot(rows_in, weight_in.T, preferred_element_type=jnp.float32)
        hidden = gelu_tanh(pre_act).astype(jnp.bfloat16)
        return jnp.dot(hidden, weight_out, preferred_element_type=jnp.float32).astype(jnp.bfloat16)
    results = lax.map(forward_one, (tokens_in, expert_in, expert_out))
    expert_rows = from_experts(results)
    mixture = gates[:, 0:1] * expert_rows[:, 0] + gates[:, 1:2] * expert_rows[:, 1]
    stream_two = stream.astype(jnp.float32) + mixture
    normed, norm_back = jax.vjp(rms_gain, stream_two, gain_second)
    layer_out = normed.astype(jnp.bfloat16)
    grad_two, gain_sum = norm_back(cotangent.astype(jnp.float32))
    gate_grads = lax.optimization_barrier(jnp.sum(expert_rows * grad_two[:, None, :], axis=-1))
    assigned_grads = (gates[..., None] * grad_two[:, None, :]).astype(jnp.bfloat16)
    grads_in = to_experts(assigned_grads.reshape(blocks, 2 * SUB, D))

    def backward_one(operands):
        rows_in, rows_grad, weight_in, weight_out = operands
        pre_act = jnp.dot(rows_in, weight_in.T, preferred_element_type=jnp.float32)
        hidden_full, gelu_back = jax.vjp(gelu_tanh, pre_act)
        hidden = hidden_full.astype(jnp.bfloat16)
        hidden_grad = jnp.dot(rows_grad, weight_out.T, preferred_element_type=jnp.float32)
        pre_grad = gelu_back(hidden_grad)[0].astype(jnp.bfloat16)
        in_grad = jnp.dot(pre_grad.T, rows_in, preferred_element_type=jnp.float32) * grad_scale
        out_grad = jnp.dot(hidden.T, rows_grad, preferred_element_type=jnp.float32) * grad_scale
        rows_back = jnp.dot(pre_grad, weight_in, preferred_element_type=jnp.float32).astype(jnp.bfloat16)
        return (in_grad, out_grad, rows_back)
    expert_in_grad, expert_out_grad, rows_back = lax.map(backward_one, (tokens_in, grads_in, expert_in, expert_out))
    back_rows = from_experts(rows_back)
    logit_grad = gate_back(gate_grads)[0]
    router_grad = jnp.dot(logit_grad.T, stream.astype(jnp.float32), precision=lax.Precision.HIGHEST) * grad_scale
    router_term = jnp.dot(logit_grad, router_weight.astype(jnp.float32), precision=lax.Precision.HIGHEST)
    stream_grad = (grad_two + (back_rows[:, 0] + back_rows[:, 1]) + router_term).astype(jnp.bfloat16)
    return (layer_out, stream_grad, expert_in_grad, expert_out_grad, router_grad, gain_sum * grad_scale)
```

```python
import math

import jax
import jax.numpy as jnp
from jax import lax
from jax.experimental import pallas as pl
from jax.experimental.pallas import tpu as pltpu
from jax.sharding import PartitionSpec as P

HD = 32

EPSILON = 1e-06
LOG2_SCALE = math.log2(math.e) / math.sqrt(HD)
SHIFT_KEYS = 256
SUM_LIMIT = 2.0**100
VMEM_LIMIT = 60 * 2**20


def rms_gain(stream, gain):
    return stream * lax.rsqrt(jnp.mean(stream * stream, axis=-1, keepdims=True) + EPSILON) * gain


def gelu_tanh(values):
    return jax.nn.gelu(values, approximate=True)


def to_sources(buffer):
    return lax.all_to_all(buffer, "exp", split_axis=0, concat_axis=0, tiled=True)


def hop(value, axis, target):
    count = lax.axis_size(axis)
    return lax.ppermute(value, axis, [(i, target(i) % count) for i in range(count)])


def split_terms(value, terms):
    pieces = []
    for _ in range(terms):
        piece = value.astype(jnp.bfloat16)
        pieces.append(piece)
        value = value - piece.astype(jnp.float32)
    return pieces


def key_blocks(refs):
    return [
        (ref, start) for ref in refs for start in range(0, ref.shape[0], 2 * HD)
    ]


def load_keys(blocks, keys, values):
    width = blocks[0][0].shape[1]
    ones = (lax.broadcasted_iota(jnp.int32, (HD, width), 0) < 3).astype(jnp.bfloat16)
    one = (lax.broadcasted_iota(jnp.int32, (HD // 2, width), 0) < 1).astype(jnp.bfloat16)
    for index, (ref, start) in enumerate(blocks):
        block = ref[start : start + HD, :]
        span = slice(index * width, (index + 1) * width)
        keys[span, :] = jnp.concatenate([block, block, block, ones], axis=0).T
        values[:, span] = jnp.concatenate([ref[start + HD : start + 2 * HD, :], one], axis=0)


def group_blocks(refs, count):
    blocks = key_blocks(refs)
    return [blocks[start : start + count] for start in range(0, len(blocks), count)]


def add_blocks(count, width, query, keys, values, total):
    chunk = width // 2

    def step(index, running):
        span = pl.ds(pl.multiple_of(index * chunk, chunk), chunk)
        exponents = jnp.dot(keys[span, :], query, preferred_element_type=jnp.float32)
        weights = jnp.exp2(exponents).astype(jnp.bfloat16)
        return running + jnp.dot(values[:, span], weights, preferred_element_type=jnp.float32)

    return lax.fori_loop(0, 2 * count, step, total)


def first_keys_kernel(count, query_ref, *refs):
    blocks, (wide_ref, total_ref, keys, values) = refs[:-4], refs[-4:]
    load_keys(key_blocks(blocks), keys, values)
    width = query_ref.shape[1]
    scaled = query_ref[...].astype(jnp.float32) * LOG2_SCALE
    pieces = split_terms(scaled, 3)
    wide_ref[...] = jnp.concatenate(pieces + [jnp.zeros_like(pieces[0])], axis=0)
    some = jnp.dot(keys[:SHIFT_KEYS, :], wide_ref[...], preferred_element_type=jnp.float32)
    shift = split_terms(-jnp.max(some, axis=0, keepdims=True), 3)
    row = lax.broadcasted_iota(jnp.int32, (HD, width), 0)
    rows = jnp.zeros((HD, width), jnp.float32)
    for index, piece in enumerate(shift):
        rows = jnp.where(row == index, piece.astype(jnp.float32), rows)
    wide_ref[3 * HD :, :] = rows.astype(jnp.bfloat16)
    total_ref[...] = add_blocks(
        count, width, wide_ref[...], keys, values, jnp.zeros(total_ref.shape, jnp.float32)
    )


def more_keys_kernel(count, wide_ref, before_ref, *refs):
    blocks, (total_ref, keys, values) = refs[:-3], refs[-3:]
    load_keys(key_blocks(blocks), keys, values)
    total_ref[...] = add_blocks(
        count, wide_ref.shape[1], wide_ref[...], keys, values, before_ref[...]
    )


def last_keys_kernel(count, fresh, wide_ref, before_ref, query_ref, *refs):
    blocks, (out_ref, keys, values, total) = refs[:-4], refs[-4:]
    load_keys(key_blocks(blocks[:fresh]), keys, values)
    width = wide_ref.shape[1]
    total[...] = add_blocks(count, width, wide_ref[...], keys, values, before_ref[...])
    sums = total[HD : HD + 1, :]
    inside = jnp.logical_and(sums <= SUM_LIMIT, sums >= 1.0 / SUM_LIMIT)
    outside = jnp.sum(jnp.where(inside, 0, 1))

    @pl.when(outside > 0)
    def _():
        query = query_ref[...]
        query = jnp.concatenate([query, jnp.zeros((3 * HD, width), query.dtype)], axis=0)
        total[...] = jnp.zeros(total.shape, jnp.float32)

        def step(index, top):
            span = pl.ds(pl.multiple_of(index * SHIFT_KEYS, SHIFT_KEYS), SHIFT_KEYS)
            scores = LOG2_SCALE * jnp.dot(
                keys[span, :], query, preferred_element_type=jnp.float32
            )
            new_top = jnp.maximum(top, jnp.max(scores, axis=0, keepdims=True))
            weights = jnp.exp2(scores - new_top).astype(jnp.bfloat16)
            total[...] = total[...] * jnp.exp2(top - new_top) + jnp.dot(
                values[:, span], weights, preferred_element_type=jnp.float32
            )
            return new_top

        top = jnp.full((1, width), -1e30, jnp.float32)
        for group in group_blocks(blocks, count):
            load_keys(group, keys, values)
            top = lax.fori_loop(0, len(group) * (width // SHIFT_KEYS), step, top)

    attended = (total[:HD, :] / total[HD : HD + 1, :]).astype(jnp.bfloat16)
    rows = out_ref.shape[2]
    for index in range(out_ref.shape[0]):
        out_ref[index] = attended[:, index * rows : (index + 1) * rows]


def block_count(arrays):
    return sum(array.shape[0] for array in arrays) // (2 * HD)


def attention_call(kernel, out_shape, operands, count, width, extra=(), aliases=None):
    specs = [pl.BlockSpec(memory_space=pltpu.VMEM)]
    return pl.pallas_call(
        kernel,
        out_shape=out_shape,
        in_specs=specs * len(operands),
        out_specs=jax.tree.map(lambda _: specs[0], out_shape),
        scratch_shapes=[
            pltpu.VMEM((count * width, 4 * HD), jnp.bfloat16),
            pltpu.VMEM((HD + HD // 2, count * width), jnp.bfloat16),
            *extra,
        ],
        input_output_aliases=aliases or {},
        compiler_params=pltpu.CompilerParams(vmem_limit_bytes=VMEM_LIMIT),
        cost_estimate=pl.CostEstimate(
            flops=count * width * width * 1200,
            transcendentals=count * width * width,
            bytes_accessed=count * width * 4 * HD,
        ),
    )(*operands)


def attention(query, keys_values, owners):
    width = query.shape[1]
    partner = hop(keys_values, "blk", lambda i: i ^ 1)
    near = [
        hop(keys_values, "blk", lambda i: i ^ 2),
        hop(keys_values, "blk", lambda i: i + 4),
        hop(keys_values, "blk", lambda i: i + 12),
        hop(keys_values, "blk", lambda i: i + 8),
    ]
    beyond = hop(jnp.concatenate(near[1:], axis=0), "blk", lambda i: i ^ 2)
    near_partner = hop(jnp.concatenate(near, axis=0), "blk", lambda i: i ^ 1)
    beyond_partner = hop(beyond, "blk", lambda i: i ^ 1)
    total_shape = jax.ShapeDtypeStruct((HD + HD // 2, width), jnp.float32)
    wide_shape = jax.ShapeDtypeStruct((4 * HD, width), jnp.bfloat16)
    first = [keys_values, partner]
    wide, total = attention_call(
        lambda *refs: first_keys_kernel(2, *refs), (wide_shape, total_shape), [query, *first], 2, width
    )
    for group in (near, [near_partner]):
        count = block_count(group)
        total = attention_call(
            lambda *refs, count=count: more_keys_kernel(count, *refs),
            total_shape,
            [wide, total, *group],
            count,
            width,
            aliases={1: 0},
        )
    last = [beyond, beyond_partner]
    count = block_count(last)
    attended = attention_call(
        lambda *refs: last_keys_kernel(count, len(last), *refs),
        jax.ShapeDtypeStruct((owners, HD, width // owners), jnp.bfloat16),
        [wide, total, query, *last, *first, *near, near_partner],
        count,
        width,
        extra=[pltpu.VMEM(total_shape.shape, jnp.float32)],
    )
    return attended, beyond_partner


def gather_by_halves(rows, axis):
    index = lax.axis_index(axis)
    distance = 1
    while distance < lax.axis_size(axis):
        other = hop(rows, axis, lambda i, distance=distance: i ^ distance)
        upper = (index // distance) % 2 == 1
        rows = jnp.concatenate(
            [jnp.where(upper, other, rows), jnp.where(upper, rows, other)], axis=0
        )
        distance *= 2
    return rows


def sum_by_halves(value, axes):
    for axis in axes:
        distance = 1
        while distance < lax.axis_size(axis):
            value = value + hop(value, axis, lambda i, distance=distance: i ^ distance)
            distance *= 2
    return value


def local(
    nodes,
    attention_weights,
    output_weight,
    router_weight,
    gain_first,
    gain_second,
    expert_in,
    expert_out,
    routes,
    cotangent,
):
    exp_count = lax.axis_size("exp")
    blk_count = lax.axis_size("blk")
    block_rows = nodes.shape[0]
    width = nodes.shape[1]
    features = attention_weights.shape[1]
    own_rows = block_rows // exp_count
    capacity = 4 * block_rows // (exp_count * exp_count)
    experts = router_weight.shape[0]
    grad_scale = 1.0 / math.sqrt(block_rows * blk_count)
    keys_values = jnp.einsum(
        "fd,td->ft",
        attention_weights[1:].reshape(2 * features, width),
        nodes,
        preferred_element_type=jnp.float32,
    ).astype(jnp.bfloat16)
    query = jnp.einsum(
        "fd,td->ft", attention_weights[0], nodes, preferred_element_type=jnp.float32
    ).astype(jnp.bfloat16)
    attended, last_arrived = attention(query, keys_values, exp_count)
    full_output_weight = gather_by_halves(output_weight, "exp")
    both_weights, _ = lax.optimization_barrier(
        (jnp.concatenate([expert_in, expert_out], axis=0), last_arrived)
    )
    all_weights = lax.all_gather(both_weights, "blk", axis=1, tiled=True)
    weight_rows_in, weight_rows_out = all_weights[0], all_weights[1]
    by_feature = to_sources(attended).reshape(exp_count * features, own_rows)
    attn_out = jnp.einsum(
        "fr,fd->rd", by_feature, full_output_weight, preferred_element_type=jnp.float32
    )
    own_nodes = lax.dynamic_slice_in_dim(
        nodes, lax.axis_index("exp") * own_rows, own_rows, 0
    ).astype(jnp.float32)
    stream = rms_gain(own_nodes + attn_out, gain_first).astype(jnp.bfloat16)
    logits = jnp.dot(stream, router_weight.T, preferred_element_type=jnp.float32)
    flat_routes = routes.reshape(2 * own_rows)
    choose = (flat_routes[:, None] == jnp.arange(experts, dtype=jnp.int32)[None, :]).astype(
        jnp.int32
    )
    before = jnp.cumsum(choose, axis=0) - choose
    slot_index = jnp.sum(before * choose, axis=1)
    position = flat_routes * capacity + slot_index
    dispatch_table = (
        jnp.arange(experts * capacity, dtype=jnp.int32)[:, None] == position[None, :]
    ).astype(jnp.bfloat16)
    selected = choose.reshape(own_rows, 2, experts).astype(jnp.float32)

    def gate_values(values):
        picked = jnp.sum(jax.nn.sigmoid(values)[:, None, :] * selected, axis=-1)
        return picked / jnp.sum(picked, axis=-1, keepdims=True)

    gates, gate_back = jax.vjp(gate_values, logits)
    repeated = jnp.repeat(stream, 2, axis=0)
    outgoing = jnp.dot(dispatch_table, repeated, preferred_element_type=jnp.float32).astype(
        jnp.bfloat16
    )
    outgoing = outgoing.reshape(experts, capacity, width)
    arrived = lax.all_to_all(outgoing, "exp", split_axis=0, concat_axis=0, tiled=True)
    pre_act = jnp.einsum("scd,hd->sch", arrived, weight_rows_in, preferred_element_type=jnp.float32)
    expert_hidden = gelu_tanh(pre_act).astype(jnp.bfloat16)
    result = jnp.einsum(
        "sch,hd->scd", expert_hidden, weight_rows_out, preferred_element_type=jnp.float32
    ).astype(jnp.bfloat16)
    received, pre_act, returned = (arrived, pre_act, to_sources(result))
    expert_rows = jnp.einsum(
        "ps,pd->sd",
        dispatch_table,
        returned.reshape(experts * capacity, width),
        preferred_element_type=jnp.float32,
    )
    expert_rows = expert_rows.reshape(own_rows, 2, width)
    mixture = gates[:, 0:1] * expert_rows[:, 0] + gates[:, 1:2] * expert_rows[:, 1]
    stream_two = stream.astype(jnp.float32) + mixture
    normed, norm_back = jax.vjp(rms_gain, stream_two, gain_second)
    layer_out = normed.astype(jnp.bfloat16)
    grad_two, gain_part = norm_back(cotangent.astype(jnp.float32))
    gate_grads = jnp.sum(expert_rows * grad_two[:, None, :], axis=-1)
    logit_grad = gate_back(gate_grads)[0]
    router_part = jnp.dot(
        logit_grad.T, stream.astype(jnp.float32), precision=lax.Precision.HIGHEST
    )
    small_sums = sum_by_halves(
        jnp.concatenate([router_part, gain_part[None, :]], axis=0) * grad_scale, ("exp", "blk")
    )
    router_grad, gain_grad = small_sums[:-1], small_sums[-1]
    assigned_grads = (
        (gates[..., None] * grad_two[:, None, :]).astype(jnp.bfloat16).reshape(2 * own_rows, width)
    )
    grad_outgoing = jnp.dot(
        dispatch_table, assigned_grads, preferred_element_type=jnp.float32
    ).astype(jnp.bfloat16)
    grad_arrived = lax.all_to_all(
        grad_outgoing.reshape(experts, capacity, width),
        "exp",
        split_axis=0,
        concat_axis=0,
        tiled=True,
    )
    hidden_full, gelu_back = jax.vjp(gelu_tanh, pre_act)
    hidden = hidden_full.astype(jnp.bfloat16)
    hidden_grad = jnp.einsum(
        "scd,hd->sch", grad_arrived, weight_rows_out, preferred_element_type=jnp.float32
    )
    pre_grad = gelu_back(hidden_grad)[0].astype(jnp.bfloat16)
    term_in = jnp.einsum("sch,scd->hd", pre_grad, received, preferred_element_type=jnp.float32)
    term_out = jnp.einsum("sch,scd->hd", hidden, grad_arrived, preferred_element_type=jnp.float32)
    summed_grads = lax.psum_scatter(
        (jnp.concatenate([term_in, term_out], axis=1) * grad_scale).astype(jnp.bfloat16),
        "blk",
        scatter_dimension=0,
        tiled=True,
    ).astype(jnp.float32)
    expert_in_grad = summed_grads[None, :, :width]
    expert_out_grad = summed_grads[None, :, width:]
    rows_back = jnp.einsum(
        "sch,hd->scd", pre_grad, weight_rows_in, preferred_element_type=jnp.float32
    ).astype(jnp.bfloat16)
    back_home = to_sources(rows_back)
    back_rows = jnp.einsum(
        "ps,pd->sd",
        dispatch_table,
        back_home.reshape(experts * capacity, width),
        preferred_element_type=jnp.float32,
    )
    back_rows = back_rows.reshape(own_rows, 2, width)
    router_term = jnp.dot(
        logit_grad, router_weight.astype(jnp.float32), precision=lax.Precision.HIGHEST
    )
    stream_grad = (grad_two + (back_rows[:, 0] + back_rows[:, 1]) + router_term).astype(
        jnp.bfloat16
    )
    return (layer_out, stream_grad, expert_in_grad, expert_out_grad, router_grad, gain_grad)


def solution(mesh):
    placed = (
        P("blk", None),
        P(None, "exp", None),
        P("exp", None),
        P(),
        P(),
        P(),
        P("exp", "blk", None),
        P("exp", "blk", None),
        P(("blk", "exp"), None),
        P(("blk", "exp"), None),
    )
    return jax.shard_map(
        local,
        mesh=mesh,
        in_specs=placed,
        out_specs=(
            P(("blk", "exp"), None),
            P(("blk", "exp"), None),
            P("exp", "blk", None),
            P("exp", "blk", None),
            P(),
            P(),
        ),
        check_vma=False,
    )
```

```python
import math

import jax
import jax.numpy as jnp
from jax import lax
from jax.experimental import pallas as pl
from jax.experimental.pallas import tpu as pltpu
from jax.sharding import PartitionSpec as P

HD = 32

EPSILON = 1e-06
LOG2_SCALE = math.log2(math.e) / math.sqrt(HD)
SHIFT_KEYS = 256
SUM_LIMIT = 2.0**100
VMEM_LIMIT = 60 * 2**20
TANH_SCALE = math.sqrt(2.0 / math.pi)
CUBE = 0.044715


def rms_gain(stream, gain):
    return stream * lax.rsqrt(jnp.mean(stream * stream, axis=-1, keepdims=True) + EPSILON) * gain


def exchange(buffer):
    return lax.all_to_all(buffer, "exp", split_axis=0, concat_axis=0, tiled=True)


def hop(value, axis, target):
    count = lax.axis_size(axis)
    return lax.ppermute(value, axis, [(i, target(i) % count) for i in range(count)])


def split_terms(value, terms):
    pieces = []
    for _ in range(terms):
        piece = value.astype(jnp.bfloat16)
        pieces.append(piece)
        value = value - piece.astype(jnp.float32)
    return pieces


def key_blocks(refs):
    return [
        (ref, start) for ref in refs for start in range(0, ref.shape[0], 2 * HD)
    ]


def load_keys(blocks, keys, values):
    width = blocks[0][0].shape[1]
    ones = (lax.broadcasted_iota(jnp.int32, (HD, width), 0) < 3).astype(jnp.bfloat16)
    one = (lax.broadcasted_iota(jnp.int32, (HD // 2, width), 0) < 1).astype(jnp.bfloat16)
    for index, (ref, start) in enumerate(blocks):
        block = ref[start : start + HD, :]
        span = slice(index * width, (index + 1) * width)
        keys[span, :] = jnp.concatenate([block, block, block, ones], axis=0).T
        values[:, span] = jnp.concatenate([ref[start + HD : start + 2 * HD, :], one], axis=0)


def group_blocks(refs, count):
    blocks = key_blocks(refs)
    return [blocks[start : start + count] for start in range(0, len(blocks), count)]


def add_blocks(count, width, query, keys, values, total):
    chunk = width // 2

    def step(index, running):
        span = pl.ds(pl.multiple_of(index * chunk, chunk), chunk)
        exponents = jnp.dot(keys[span, :], query, preferred_element_type=jnp.float32)
        weights = jnp.exp2(exponents).astype(jnp.bfloat16)
        return running + jnp.dot(values[:, span], weights, preferred_element_type=jnp.float32)

    return lax.fori_loop(0, 2 * count, step, total)


def first_keys_kernel(count, query_ref, *refs):
    blocks, (wide_ref, total_ref, keys, values) = refs[:-4], refs[-4:]
    load_keys(key_blocks(blocks), keys, values)
    width = query_ref.shape[1]
    scaled = query_ref[...].astype(jnp.float32) * LOG2_SCALE
    pieces = split_terms(scaled, 3)
    wide_ref[...] = jnp.concatenate(pieces + [jnp.zeros_like(pieces[0])], axis=0)
    some = jnp.dot(keys[:SHIFT_KEYS, :], wide_ref[...], preferred_element_type=jnp.float32)
    shift = split_terms(-jnp.max(some, axis=0, keepdims=True), 3)
    row = lax.broadcasted_iota(jnp.int32, (HD, width), 0)
    rows = jnp.zeros((HD, width), jnp.float32)
    for index, piece in enumerate(shift):
        rows = jnp.where(row == index, piece.astype(jnp.float32), rows)
    wide_ref[3 * HD :, :] = rows.astype(jnp.bfloat16)
    total_ref[...] = add_blocks(
        count, width, wide_ref[...], keys, values, jnp.zeros(total_ref.shape, jnp.float32)
    )


def more_keys_kernel(count, wide_ref, before_ref, *refs):
    blocks, (total_ref, keys, values) = refs[:-3], refs[-3:]
    load_keys(key_blocks(blocks), keys, values)
    total_ref[...] = add_blocks(
        count, wide_ref.shape[1], wide_ref[...], keys, values, before_ref[...]
    )


def last_keys_kernel(count, fresh, wide_ref, before_ref, query_ref, *refs):
    blocks, (out_ref, keys, values, total) = refs[:-4], refs[-4:]
    load_keys(key_blocks(blocks[:fresh]), keys, values)
    width = wide_ref.shape[1]
    total[...] = add_blocks(count, width, wide_ref[...], keys, values, before_ref[...])
    sums = total[HD : HD + 1, :]
    inside = jnp.logical_and(sums <= SUM_LIMIT, sums >= 1.0 / SUM_LIMIT)
    outside = jnp.sum(jnp.where(inside, 0, 1))

    @pl.when(outside > 0)
    def _():
        query = query_ref[...]
        query = jnp.concatenate([query, jnp.zeros((3 * HD, width), query.dtype)], axis=0)
        total[...] = jnp.zeros(total.shape, jnp.float32)

        def step(index, top):
            span = pl.ds(pl.multiple_of(index * SHIFT_KEYS, SHIFT_KEYS), SHIFT_KEYS)
            scores = LOG2_SCALE * jnp.dot(
                keys[span, :], query, preferred_element_type=jnp.float32
            )
            new_top = jnp.maximum(top, jnp.max(scores, axis=0, keepdims=True))
            weights = jnp.exp2(scores - new_top).astype(jnp.bfloat16)
            total[...] = total[...] * jnp.exp2(top - new_top) + jnp.dot(
                values[:, span], weights, preferred_element_type=jnp.float32
            )
            return new_top

        top = jnp.full((1, width), -1e30, jnp.float32)
        for group in group_blocks(blocks, count):
            load_keys(group, keys, values)
            top = lax.fori_loop(0, len(group) * (width // SHIFT_KEYS), step, top)

    attended = (total[:HD, :] / total[HD : HD + 1, :]).astype(jnp.bfloat16)
    rows = out_ref.shape[2]
    for index in range(out_ref.shape[0]):
        out_ref[index] = attended[:, index * rows : (index + 1) * rows]


def block_count(arrays):
    return sum(array.shape[0] for array in arrays) // (2 * HD)


def attention_call(kernel, out_shape, operands, count, width, extra=(), aliases=None):
    specs = [pl.BlockSpec(memory_space=pltpu.VMEM)]
    return pl.pallas_call(
        kernel,
        out_shape=out_shape,
        in_specs=specs * len(operands),
        out_specs=jax.tree.map(lambda _: specs[0], out_shape),
        scratch_shapes=[
            pltpu.VMEM((count * width, 4 * HD), jnp.bfloat16),
            pltpu.VMEM((HD + HD // 2, count * width), jnp.bfloat16),
            *extra,
        ],
        input_output_aliases=aliases or {},
        compiler_params=pltpu.CompilerParams(vmem_limit_bytes=VMEM_LIMIT),
        cost_estimate=pl.CostEstimate(
            flops=count * width * width * 1200,
            transcendentals=count * width * width,
            bytes_accessed=count * width * 4 * HD,
        ),
    )(*operands)


def double_by_exchange(rows, axis, distance):
    other = hop(rows, axis, lambda i: i ^ distance)
    upper = (lax.axis_index(axis) // distance) % 2 == 1
    return jnp.concatenate(
        [jnp.where(upper, other, rows), jnp.where(upper, rows, other)], axis=0
    )


def attention(query, keys_values, output_weight, expert_weights, owners):
    width = query.shape[1]
    partner = hop(keys_values, "blk", lambda i: i ^ 1)
    near = [
        hop(keys_values, "blk", lambda i: i ^ 2),
        hop(keys_values, "blk", lambda i: i + 4),
        hop(keys_values, "blk", lambda i: i + 12),
        hop(keys_values, "blk", lambda i: i + 8),
    ]
    total_shape = jax.ShapeDtypeStruct((HD + HD // 2, width), jnp.float32)
    wide_shape = jax.ShapeDtypeStruct((4 * HD, width), jnp.bfloat16)
    first = [keys_values, partner]
    wide, total = attention_call(
        lambda *refs: first_keys_kernel(2, *refs),
        (wide_shape, total_shape),
        [query, *first],
        2,
        width,
    )

    def more(total, group):
        count = block_count(group)
        return attention_call(
            lambda *refs: more_keys_kernel(count, *refs),
            total_shape,
            [wide, total, *group],
            count,
            width,
            aliases={1: 0},
        )

    near, output_weight, total = lax.optimization_barrier((near, output_weight, total))
    beyond = hop(jnp.concatenate(near[1:], axis=0), "blk", lambda i: i ^ 2)
    near_partner = hop(jnp.concatenate(near, axis=0), "blk", lambda i: i ^ 1)
    output_weight = double_by_exchange(output_weight, "exp", 1)
    total = more(total, near)
    beyond, output_weight, expert_weights, total = lax.optimization_barrier(
        (beyond, output_weight, expert_weights, total)
    )
    beyond_partner = hop(beyond, "blk", lambda i: i ^ 1)
    output_weight = double_by_exchange(output_weight, "exp", 2)
    expert_weights = lax.all_gather(expert_weights, "blk", axis=1, tiled=True)
    total = more(total, [near_partner])
    output_weight, total = lax.optimization_barrier((output_weight, total))
    output_weight = double_by_exchange(output_weight, "exp", 4)
    last = [beyond, beyond_partner]
    count = block_count(last)
    attended = attention_call(
        lambda *refs: last_keys_kernel(count, len(last), *refs),
        jax.ShapeDtypeStruct((owners, HD, width // owners), jnp.bfloat16),
        [wide, total, query, *last, *first, *near, near_partner],
        count,
        width,
        extra=[pltpu.VMEM(total_shape.shape, jnp.float32)],
    )
    return attended, output_weight, expert_weights


def sum_near(value, axis, distance):
    first, second, both = [
        hop(value, axis, lambda i, step=step: i ^ step)
        for step in (distance, 2 * distance, 3 * distance)
    ]
    return (value + first) + (second + both)


def sum_pair(value, axis, distance):
    return value + hop(value, axis, lambda i: i ^ distance)


def dot_rows(first, second):
    return lax.dot_general(
        first, second, (((1,), (1,)), ((), ())), preferred_element_type=jnp.float32
    )


def tanh_part(values):
    return jnp.tanh(TANH_SCALE * (values + CUBE * (values * values * values)))


def expert_forward_kernel(rows_ref, in_ref, out_ref, result_ref, total):
    step = pl.program_id(0)
    pre_act = dot_rows(rows_ref[...], in_ref[...])
    hidden = (pre_act * (0.5 * (1.0 + tanh_part(pre_act)))).astype(jnp.bfloat16)
    part = jnp.dot(hidden, out_ref[...], preferred_element_type=jnp.float32)

    @pl.when(step == 0)
    def _():
        total[...] = part

    @pl.when(step > 0)
    def _():
        total[...] += part

    @pl.when(step == pl.num_programs(0) - 1)
    def _():
        result_ref[...] = total[...].astype(result_ref.dtype)


def expert_forward(rows, weights):
    count, width = rows.shape
    hidden = weights.shape[1]
    tile = 512
    return pl.pallas_call(
        expert_forward_kernel,
        grid=(hidden // tile,),
        out_shape=jax.ShapeDtypeStruct((count, width), jnp.bfloat16),
        in_specs=[
            pl.BlockSpec((count, width), lambda i: (0, 0)),
            pl.BlockSpec((None, tile, width), lambda i: (0, i, 0)),
            pl.BlockSpec((None, tile, width), lambda i: (1, i, 0)),
        ],
        out_specs=pl.BlockSpec((count, width), lambda i: (0, 0)),
        scratch_shapes=[pltpu.VMEM((count, width), jnp.float32)],
        compiler_params=pltpu.CompilerParams(vmem_limit_bytes=VMEM_LIMIT),
        cost_estimate=pl.CostEstimate(
            flops=4 * count * width * hidden,
            transcendentals=count * hidden,
            bytes_accessed=4 * hidden * width,
        ),
    )(rows, weights, weights)


def expert_slopes_kernel(place_ref, rows_ref, *refs):
    ins, outs = refs[:4], refs[4:8]
    hidden_ref, slope_ref, out_weight_ref, in_weight_ref = refs[8:]
    weight_in = jnp.concatenate([ref[...] for ref in ins], axis=0)
    out_weight_ref[...] = jnp.concatenate([ref[...] for ref in outs], axis=0)
    in_weight_ref[...] = weight_in.T
    pre_act = dot_rows(weight_in, rows_ref[...])
    tanh = tanh_part(pre_act)
    half = 0.5 * (1.0 + tanh)
    hidden_ref[...] = (pre_act * half).astype(hidden_ref.dtype)
    slope_ref[...] = half + pre_act * (0.5 * (1.0 - tanh * tanh)) * (
        TANH_SCALE * (1.0 + 3.0 * CUBE * (pre_act * pre_act))
    )


def expert_slopes(place, rows, weights):
    count, width = rows.shape
    hidden = weights.shape[1]
    share = hidden // 16
    tile = 4 * share

    def weight_spec(which, quarter):
        def index(step, place):
            z = jnp.bitwise_xor(step, place[0])
            y = jnp.bitwise_xor(quarter // 2, place[1])
            core = jnp.bitwise_xor(quarter % 2, place[2])
            return (which, z * 4 + y * 2 + core, 0)

        return pl.BlockSpec((None, share, width), index)

    specs = [weight_spec(which, quarter) for which in range(2) for quarter in range(4)]
    return pl.pallas_call(
        expert_slopes_kernel,
        out_shape=(
            jax.ShapeDtypeStruct((hidden, count), jnp.bfloat16),
            jax.ShapeDtypeStruct((hidden, count), jnp.float32),
            jax.ShapeDtypeStruct((hidden, width), jnp.bfloat16),
            jax.ShapeDtypeStruct((width, hidden), jnp.bfloat16),
        ),
        grid_spec=pltpu.PrefetchScalarGridSpec(
            num_scalar_prefetch=1,
            grid=(hidden // tile,),
            in_specs=[pl.BlockSpec((count, width), lambda i, place: (0, 0)), *specs],
            out_specs=(
                pl.BlockSpec((tile, count), lambda i, place: (i, 0)),
                pl.BlockSpec((tile, count), lambda i, place: (i, 0)),
                pl.BlockSpec((tile, width), lambda i, place: (i, 0)),
                pl.BlockSpec((width, tile), lambda i, place: (0, i)),
            ),
        ),
        compiler_params=pltpu.CompilerParams(vmem_limit_bytes=VMEM_LIMIT),
        cost_estimate=pl.CostEstimate(
            flops=2 * count * width * hidden,
            transcendentals=count * hidden,
            bytes_accessed=6 * count * hidden + 8 * hidden * width,
        ),
    )(place, rows, *([weights] * 8))


def store_shares(term, mine_ref, theirs_ref):
    share = mine_ref.shape[2]
    for y in range(2):
        start = 2 * y * share
        mine_ref[0, y] = term[start : start + share]
        theirs_ref[0, y] = term[start + share : start + 2 * share].astype(theirs_ref.dtype)


def expert_out_grad_kernel(scale, hidden_ref, grads_ref, mine_ref, theirs_ref):
    term = jnp.dot(hidden_ref[...], grads_ref[...], preferred_element_type=jnp.float32)
    store_shares(term * scale, mine_ref, theirs_ref)


def expert_in_grad_kernel(
    scale,
    slope_ref,
    out_weight_ref,
    in_weight_ref,
    rows_ref,
    grads_ref,
    mine_ref,
    theirs_ref,
    back_ref,
    total,
):
    step = pl.program_id(0)
    hidden_grad = dot_rows(out_weight_ref[...], grads_ref[...])
    pre_grad = (hidden_grad * slope_ref[...]).astype(jnp.bfloat16)
    part = jnp.dot(in_weight_ref[...], pre_grad, preferred_element_type=jnp.float32)

    @pl.when(step == 0)
    def _():
        total[...] = part

    @pl.when(step > 0)
    def _():
        total[...] += part

    term = jnp.dot(pre_grad, rows_ref[...], preferred_element_type=jnp.float32)
    store_shares(term * scale, mine_ref, theirs_ref)

    @pl.when(step == pl.num_programs(0) - 1)
    def _():
        back_ref[...] = total[...].T.astype(back_ref.dtype)


def share_shapes(hidden, width):
    shape = (4, 2, hidden // 16, width)
    spec = pl.BlockSpec((1, *shape[1:]), lambda i: (i, 0, 0, 0))
    shapes = (
        jax.ShapeDtypeStruct(shape, jnp.float32),
        jax.ShapeDtypeStruct(shape, jnp.bfloat16),
    )
    return shapes, (spec, spec)


def expert_out_grad(hidden, grads, scale):
    units, count = hidden.shape
    width = grads.shape[1]
    shapes, specs = share_shapes(units, width)
    return pl.pallas_call(
        lambda *refs: expert_out_grad_kernel(scale, *refs),
        grid=(4,),
        out_shape=shapes,
        in_specs=[
            pl.BlockSpec((units // 4, count), lambda i: (i, 0)),
            pl.BlockSpec((count, width), lambda i: (0, 0)),
        ],
        out_specs=specs,
        compiler_params=pltpu.CompilerParams(vmem_limit_bytes=VMEM_LIMIT),
        cost_estimate=pl.CostEstimate(
            flops=2 * units * count * width, transcendentals=0, bytes_accessed=2 * units * count
        ),
    )(hidden, grads)


def expert_in_grad(slopes, out_weight, in_weight, rows, grads, scale):
    units, count = slopes.shape
    width = grads.shape[1]
    shapes, specs = share_shapes(units, width)
    return pl.pallas_call(
        lambda *refs: expert_in_grad_kernel(scale, *refs),
        grid=(4,),
        out_shape=(*shapes, jax.ShapeDtypeStruct((count, width), jnp.bfloat16)),
        in_specs=[
            pl.BlockSpec((units // 4, count), lambda i: (i, 0)),
            pl.BlockSpec((units // 4, width), lambda i: (i, 0)),
            pl.BlockSpec((width, units // 4), lambda i: (0, i)),
            pl.BlockSpec((count, width), lambda i: (0, 0)),
            pl.BlockSpec((count, width), lambda i: (0, 0)),
        ],
        out_specs=(*specs, pl.BlockSpec((count, width), lambda i: (0, 0))),
        scratch_shapes=[pltpu.VMEM((width, count), jnp.float32)],
        compiler_params=pltpu.CompilerParams(vmem_limit_bytes=VMEM_LIMIT),
        cost_estimate=pl.CostEstimate(
            flops=6 * units * count * width, transcendentals=0, bytes_accessed=4 * units * count
        ),
    )(slopes, out_weight, in_weight, rows, grads)


def swap(block, distance):
    return hop(block.astype(jnp.bfloat16), "blk", lambda i: i ^ distance).astype(jnp.float32)


def sum_over_z(blocks):
    return blocks[0] + (swap(blocks[1], 4) + (swap(blocks[2], 8) + swap(blocks[3], 12)))


def local(
    nodes,
    attention_weights,
    output_weight,
    router_weight,
    gain_first,
    gain_second,
    expert_in,
    expert_out,
    routes,
    cotangent,
):
    exp_count = lax.axis_size("exp")
    blk_count = lax.axis_size("blk")
    block_rows = nodes.shape[0]
    width = nodes.shape[1]
    features = attention_weights.shape[1]
    own_rows = block_rows // exp_count
    capacity = 4 * block_rows // (exp_count * exp_count)
    experts = router_weight.shape[0]
    grad_scale = 1.0 / math.sqrt(block_rows * blk_count)
    block = lax.axis_index("blk")
    place = jnp.stack([block // 4, (block // 2) % 2, block % 2]).astype(jnp.int32)
    keys_values = jnp.einsum(
        "fd,td->ft",
        attention_weights[1:].reshape(2 * features, width),
        nodes,
        preferred_element_type=jnp.float32,
    ).astype(jnp.bfloat16)
    query = jnp.einsum(
        "fd,td->ft", attention_weights[0], nodes, preferred_element_type=jnp.float32
    ).astype(jnp.bfloat16)
    attended, full_output_weight, all_weights = attention(
        query,
        keys_values,
        output_weight,
        jnp.concatenate([expert_in, expert_out], axis=0),
        exp_count,
    )
    by_feature = exchange(attended).reshape(exp_count * features, own_rows)
    attn_out = jnp.einsum(
        "fr,fd->rd", by_feature, full_output_weight, preferred_element_type=jnp.float32
    )
    own_nodes = lax.dynamic_slice_in_dim(
        nodes, lax.axis_index("exp") * own_rows, own_rows, 0
    ).astype(jnp.float32)
    stream = rms_gain(own_nodes + attn_out, gain_first).astype(jnp.bfloat16)
    logits = jnp.dot(stream, router_weight.T, preferred_element_type=jnp.float32)
    flat_routes = routes.reshape(2 * own_rows)
    choose = (flat_routes[:, None] == jnp.arange(experts, dtype=jnp.int32)[None, :]).astype(
        jnp.int32
    )
    before = jnp.cumsum(choose, axis=0) - choose
    slot_index = jnp.sum(before * choose, axis=1)
    position = flat_routes * capacity + slot_index
    dispatch_table = (
        jnp.arange(experts * capacity, dtype=jnp.int32)[:, None] == position[None, :]
    ).astype(jnp.bfloat16)
    selected = choose.reshape(own_rows, 2, experts).astype(jnp.float32)

    def gate_values(values):
        picked = jnp.sum(jax.nn.sigmoid(values)[:, None, :] * selected, axis=-1)
        return picked / jnp.sum(picked, axis=-1, keepdims=True)

    gates, gate_back = jax.vjp(gate_values, logits)
    repeated = jnp.repeat(stream, 2, axis=0)
    outgoing = jnp.dot(dispatch_table, repeated, preferred_element_type=jnp.float32).astype(
        jnp.bfloat16
    )
    outgoing = outgoing.reshape(experts, capacity, width)
    arrived = exchange(outgoing).reshape(experts * capacity, width)
    result = expert_forward(arrived, all_weights)
    returned = exchange(result.reshape(experts, capacity, width))
    kept, result = lax.optimization_barrier((arrived, result))
    hidden, slopes, out_weight, in_weight = expert_slopes(place, kept, all_weights)
    expert_rows = jnp.einsum(
        "ps,pd->sd",
        dispatch_table,
        returned.reshape(experts * capacity, width),
        preferred_element_type=jnp.float32,
    )
    expert_rows = expert_rows.reshape(own_rows, 2, width)
    mixture = gates[:, 0:1] * expert_rows[:, 0] + gates[:, 1:2] * expert_rows[:, 1]
    stream_two = stream.astype(jnp.float32) + mixture
    normed, norm_back = jax.vjp(rms_gain, stream_two, gain_second)
    layer_out = normed.astype(jnp.bfloat16)
    grad_two, gain_part = norm_back(cotangent.astype(jnp.float32))
    gate_grads = jnp.sum(expert_rows * grad_two[:, None, :], axis=-1)
    logit_grad = gate_back(gate_grads)[0]
    router_part = jnp.dot(
        logit_grad.T, stream.astype(jnp.float32), precision=lax.Precision.HIGHEST
    )
    small = jnp.concatenate([router_part, gain_part[None, :]], axis=0) * grad_scale
    small = sum_pair(sum_near(small, "exp", 1), "exp", 4)
    small = sum_pair(sum_pair(sum_near(small, "blk", 4), "blk", 2), "blk", 1)
    router_grad, gain_grad = small[:-1], small[-1]
    assigned_grads = (
        (gates[..., None] * grad_two[:, None, :]).astype(jnp.bfloat16).reshape(2 * own_rows, width)
    )
    grad_outgoing = jnp.dot(
        dispatch_table, assigned_grads, preferred_element_type=jnp.float32
    ).astype(jnp.bfloat16)
    grad_arrived = exchange(grad_outgoing.reshape(experts, capacity, width)).reshape(
        experts * capacity, width
    )
    out_mine, out_theirs = expert_out_grad(hidden, grad_arrived, grad_scale)
    in_mine, in_theirs, rows_back = expert_in_grad(
        slopes, out_weight, in_weight, kept, grad_arrived, grad_scale
    )
    out_sums = out_mine + swap(out_theirs, 1)
    out_sums = out_sums[:, 0] + swap(out_sums[:, 1], 2)
    expert_out_grads = sum_over_z(out_sums)[None]
    in_sums = sum_over_z(in_mine + swap(in_theirs, 1))
    expert_in_grads = (in_sums[0] + swap(in_sums[1], 2))[None]
    back_home = exchange(rows_back.reshape(experts, capacity, width))
    back_rows = jnp.einsum(
        "ps,pd->sd",
        dispatch_table,
        back_home.reshape(experts * capacity, width),
        preferred_element_type=jnp.float32,
    )
    back_rows = back_rows.reshape(own_rows, 2, width)
    router_term = jnp.dot(
        logit_grad, router_weight.astype(jnp.float32), precision=lax.Precision.HIGHEST
    )
    stream_grad = (grad_two + (back_rows[:, 0] + back_rows[:, 1]) + router_term).astype(
        jnp.bfloat16
    )
    return (layer_out, stream_grad, expert_in_grads, expert_out_grads, router_grad, gain_grad)


def solution(mesh):
    placed = (
        P("blk", None),
        P(None, "exp", None),
        P("exp", None),
        P(),
        P(),
        P(),
        P("exp", "blk", None),
        P("exp", "blk", None),
        P(("blk", "exp"), None),
        P(("blk", "exp"), None),
    )
    return jax.shard_map(
        local,
        mesh=mesh,
        in_specs=placed,
        out_specs=(
            P(("blk", "exp"), None),
            P(("blk", "exp"), None),
            P("exp", "blk", None),
            P("exp", "blk", None),
            P(),
            P(),
        ),
        check_vma=False,
    )
```

```python
import math

import jax
import jax.numpy as jnp
from jax import lax
from jax.experimental import pallas as pl
from jax.experimental.pallas import tpu as pltpu
from jax.sharding import PartitionSpec as P

HD = 32

EPSILON = 1e-06
LOG2_SCALE = math.log2(math.e) / math.sqrt(HD)
SHIFT_KEYS = 256
SUM_LIMIT = 2.0**100
VMEM_LIMIT = 60 * 2**20
TANH_SCALE = math.sqrt(2.0 / math.pi)
CUBE = 0.044715


def rms_gain(stream, gain):
    return stream * lax.rsqrt(jnp.mean(stream * stream, axis=-1, keepdims=True) + EPSILON) * gain


def exchange(buffer):
    return lax.all_to_all(buffer, "exp", split_axis=0, concat_axis=0, tiled=True)


def hop(value, axis, target):
    count = lax.axis_size(axis)
    return lax.ppermute(value, axis, [(i, target(i) % count) for i in range(count)])


def split_terms(value, terms):
    pieces = []
    for _ in range(terms):
        piece = value.astype(jnp.bfloat16)
        pieces.append(piece)
        value = value - piece.astype(jnp.float32)
    return pieces


def key_blocks(refs):
    return [
        (ref, start) for ref in refs for start in range(0, ref.shape[0], 2 * HD)
    ]


def own_blocks(own_ref):
    return [(own_ref, HD)]


def load_keys(blocks, keys, values):
    width = blocks[0][0].shape[1]
    ones = (lax.broadcasted_iota(jnp.int32, (HD, width), 0) < 3).astype(jnp.bfloat16)
    one = (lax.broadcasted_iota(jnp.int32, (HD // 2, width), 0) < 1).astype(jnp.bfloat16)
    for index, (ref, start) in enumerate(blocks):
        block = ref[start : start + HD, :]
        span = slice(index * width, (index + 1) * width)
        keys[span, :] = jnp.concatenate([block, block, block, ones], axis=0).T
        values[:, span] = jnp.concatenate([ref[start + HD : start + 2 * HD, :], one], axis=0)


def add_blocks(count, width, query, keys, values, total):
    def step(index, running):
        span = pl.ds(pl.multiple_of(index * width, width), width)
        exponents = jnp.dot(keys[span, :], query, preferred_element_type=jnp.float32)
        weights = jnp.exp2(exponents).astype(jnp.bfloat16)
        return running + jnp.dot(values[:, span], weights, preferred_element_type=jnp.float32)

    return lax.fori_loop(0, count, step, total)


def first_keys_kernel(count, own_ref, *refs):
    blocks, (wide_ref, total_ref, keys, values) = refs[:-4], refs[-4:]
    load_keys(own_blocks(own_ref) + key_blocks(blocks), keys, values)
    width = own_ref.shape[1]
    scaled = own_ref[:HD, :].astype(jnp.float32) * LOG2_SCALE
    pieces = split_terms(scaled, 3)
    wide_ref[...] = jnp.concatenate(pieces + [jnp.zeros_like(pieces[0])], axis=0)
    some = jnp.dot(keys[:SHIFT_KEYS, :], wide_ref[...], preferred_element_type=jnp.float32)
    shift = split_terms(-jnp.max(some, axis=0, keepdims=True), 3)
    row = lax.broadcasted_iota(jnp.int32, (HD, width), 0)
    rows = jnp.zeros((HD, width), jnp.float32)
    for index, piece in enumerate(shift):
        rows = jnp.where(row == index, piece.astype(jnp.float32), rows)
    wide_ref[3 * HD :, :] = rows.astype(jnp.bfloat16)
    total_ref[...] = add_blocks(
        count, width, wide_ref[...], keys, values, jnp.zeros(total_ref.shape, jnp.float32)
    )


def more_keys_kernel(count, wide_ref, before_ref, *refs):
    blocks, (total_ref, keys, values) = refs[:-3], refs[-3:]
    load_keys(key_blocks(blocks), keys, values)
    total_ref[...] = add_blocks(
        count, wide_ref.shape[1], wide_ref[...], keys, values, before_ref[...]
    )


def last_keys_kernel(count, fresh, wide_ref, before_ref, own_ref, output_weight_ref, *refs):
    blocks, (out_ref, keys, values, total) = refs[:-4], refs[-4:]
    load_keys(key_blocks(blocks[:fresh]), keys, values)
    width = wide_ref.shape[1]
    total[...] = add_blocks(count, width, wide_ref[...], keys, values, before_ref[...])
    sums = total[HD : HD + 1, :]
    inside = jnp.logical_and(sums <= SUM_LIMIT, sums >= 1.0 / SUM_LIMIT)
    outside = jnp.sum(jnp.where(inside, 0, 1))

    @pl.when(outside > 0)
    def _():
        query = own_ref[:HD, :]
        query = jnp.concatenate([query, jnp.zeros((3 * HD, width), query.dtype)], axis=0)
        total[...] = jnp.zeros(total.shape, jnp.float32)

        def step(index, top):
            span = pl.ds(pl.multiple_of(index * SHIFT_KEYS, SHIFT_KEYS), SHIFT_KEYS)
            scores = LOG2_SCALE * jnp.dot(
                keys[span, :], query, preferred_element_type=jnp.float32
            )
            new_top = jnp.maximum(top, jnp.max(scores, axis=0, keepdims=True))
            weights = jnp.exp2(scores - new_top).astype(jnp.bfloat16)
            total[...] = total[...] * jnp.exp2(top - new_top) + jnp.dot(
                values[:, span], weights, preferred_element_type=jnp.float32
            )
            return new_top

        top = jnp.full((1, width), -1e30, jnp.float32)
        every = own_blocks(own_ref) + key_blocks(blocks)
        for group in [every[i : i + count] for i in range(0, len(every), count)]:
            load_keys(group, keys, values)
            top = lax.fori_loop(0, len(group) * (width // SHIFT_KEYS), step, top)

    attended = (total[:HD, :] / total[HD : HD + 1, :]).astype(jnp.bfloat16)
    weight = output_weight_ref[...]
    features = weight.shape[1]
    rows = out_ref.shape[2] - features
    for index in range(out_ref.shape[0]):
        out_ref[index, :, :features] = weight
        out_ref[index, :, features:] = attended[:, index * rows : (index + 1) * rows]


def block_count(arrays):
    return sum(array.shape[0] for array in arrays) // (2 * HD)


def attention_call(kernel, out_shape, operands, count, width, extra=(), aliases=None):
    specs = [pl.BlockSpec(memory_space=pltpu.VMEM)]
    return pl.pallas_call(
        kernel,
        out_shape=out_shape,
        in_specs=specs * len(operands),
        out_specs=jax.tree.map(lambda _: specs[0], out_shape),
        scratch_shapes=[
            pltpu.VMEM((count * width, 4 * HD), jnp.bfloat16),
            pltpu.VMEM((HD + HD // 2, count * width), jnp.bfloat16),
            *extra,
        ],
        input_output_aliases=aliases or {},
        compiler_params=pltpu.CompilerParams(vmem_limit_bytes=VMEM_LIMIT),
        cost_estimate=pl.CostEstimate(
            flops=count * width * width * 1200,
            transcendentals=count * width * width,
            bytes_accessed=count * width * 4 * HD,
        ),
    )(*operands)


def near_hops(value):
    return [hop(value, "blk", lambda i, step=step: i ^ step) for step in (2, 4, 12, 8)]


def attention(projected, output_weight, expert_weights, owners):
    width = projected.shape[1]
    keys_values = projected[HD:]
    partner = hop(keys_values, "blk", lambda i: i ^ 1)
    near = near_hops(keys_values)
    total_shape = jax.ShapeDtypeStruct((HD + HD // 2, width), jnp.float32)
    wide_shape = jax.ShapeDtypeStruct((4 * HD, width), jnp.bfloat16)
    wide, total = attention_call(
        lambda *refs: first_keys_kernel(2, *refs),
        (wide_shape, total_shape),
        [projected, partner],
        2,
        width,
    )

    def more(total, group):
        count = block_count(group)
        return attention_call(
            lambda *refs: more_keys_kernel(count, *refs),
            total_shape,
            [wide, total, *group],
            count,
            width,
            aliases={1: 0},
        )

    near, total = lax.optimization_barrier((near, total))
    beyond = hop(jnp.concatenate(near[1:], axis=0), "blk", lambda i: i ^ 2)
    near_partner = hop(jnp.concatenate(near, axis=0), "blk", lambda i: i ^ 1)
    total = more(total, near)
    beyond, expert_weights, total = lax.optimization_barrier((beyond, expert_weights, total))
    beyond_partner = hop(beyond, "blk", lambda i: i ^ 1)
    beside = hop(expert_weights, "blk", lambda i: i ^ 2)
    total = more(total, [near_partner])
    beside, beyond_partner, total = lax.optimization_barrier((beside, beyond_partner, total))
    pair = jnp.stack([expert_weights, beside])
    lane = [pair, *[hop(pair, "blk", lambda i, step=step: i ^ step) for step in (4, 8, 12)]]
    last = [beyond, beyond_partner]
    count = block_count(last)
    features = output_weight.shape[1]
    attended = attention_call(
        lambda *refs: last_keys_kernel(count, len(last), *refs),
        jax.ShapeDtypeStruct((owners, HD, features + width // owners), jnp.bfloat16),
        [wide, total, projected, output_weight, *last, partner, *near, near_partner],
        count,
        width,
        extra=[pltpu.VMEM(total_shape.shape, jnp.float32)],
    )
    return attended, lane


def sum_near(value, axis, distance):
    first, second, both = [
        hop(value, axis, lambda i, step=step: i ^ step)
        for step in (distance, 2 * distance, 3 * distance)
    ]
    return (value + first) + (second + both)


def sum_pair(value, axis, distance):
    return value + hop(value, axis, lambda i: i ^ distance)


def dot_rows(first, second):
    return lax.dot_general(
        first, second, (((1,), (1,)), ((), ())), preferred_element_type=jnp.float32
    )


def tanh_part(values):
    return jnp.tanh(TANH_SCALE * (values + CUBE * (values * values * values)))


def tile_rows(lane_ref, partner_ref):
    share, width = lane_ref.shape[1:]
    return jnp.concatenate(
        [ref[...].reshape(2 * share, width) for ref in (lane_ref, partner_ref)], axis=0
    )


def weight_specs(weights):
    _, _, _, share, width = weights.shape
    return [
        pl.BlockSpec((None, 2, None, share, width), lambda i, which=which: (i, 0, which, 0, 0))
        for which in (0, 0, 1, 1)
    ]


def expert_forward_kernel(rows_ref, in_lane, in_partner, out_lane, out_partner, result_ref, total):
    step = pl.program_id(0)
    pre_act = dot_rows(rows_ref[...], tile_rows(in_lane, in_partner))
    hidden = (pre_act * (0.5 * (1.0 + tanh_part(pre_act)))).astype(jnp.bfloat16)
    part = jnp.dot(
        hidden, tile_rows(out_lane, out_partner), preferred_element_type=jnp.float32
    )

    @pl.when(step == 0)
    def _():
        total[...] = part

    @pl.when(step > 0)
    def _():
        total[...] += part

    @pl.when(step == pl.num_programs(0) - 1)
    def _():
        result_ref[...] = total[...].astype(result_ref.dtype)


def expert_forward(rows, lane, partner):
    count, width = rows.shape
    hidden = lane.size // width
    return pl.pallas_call(
        expert_forward_kernel,
        grid=(lane.shape[0],),
        out_shape=jax.ShapeDtypeStruct((count, width), jnp.bfloat16),
        in_specs=[pl.BlockSpec((count, width), lambda i: (0, 0)), *weight_specs(lane)],
        out_specs=pl.BlockSpec((count, width), lambda i: (0, 0)),
        scratch_shapes=[pltpu.VMEM((count, width), jnp.float32)],
        compiler_params=pltpu.CompilerParams(vmem_limit_bytes=VMEM_LIMIT),
        cost_estimate=pl.CostEstimate(
            flops=4 * count * width * hidden,
            transcendentals=count * hidden,
            bytes_accessed=4 * hidden * width,
        ),
    )(rows, lane, partner, lane, partner)


def expert_slopes_kernel(
    rows_ref,
    in_lane,
    in_partner,
    out_lane,
    out_partner,
    hidden_ref,
    slope_ref,
    out_weight_ref,
    in_weight_ref,
):
    weight_in = tile_rows(in_lane, in_partner)
    out_weight_ref[...] = tile_rows(out_lane, out_partner)
    in_weight_ref[...] = weight_in.T
    pre_act = dot_rows(weight_in, rows_ref[...])
    tanh = tanh_part(pre_act)
    half = 0.5 * (1.0 + tanh)
    hidden_ref[...] = (pre_act * half).astype(hidden_ref.dtype)
    slope_ref[...] = half + pre_act * (0.5 * (1.0 - tanh * tanh)) * (
        TANH_SCALE * (1.0 + 3.0 * CUBE * (pre_act * pre_act))
    )


def expert_slopes(rows, lane, partner):
    count, width = rows.shape
    hidden = lane.size // width
    tile = hidden // lane.shape[0]
    return pl.pallas_call(
        expert_slopes_kernel,
        grid=(lane.shape[0],),
        out_shape=(
            jax.ShapeDtypeStruct((hidden, count), jnp.bfloat16),
            jax.ShapeDtypeStruct((hidden, count), jnp.float32),
            jax.ShapeDtypeStruct((hidden, width), jnp.bfloat16),
            jax.ShapeDtypeStruct((width, hidden), jnp.bfloat16),
        ),
        in_specs=[pl.BlockSpec((count, width), lambda i: (0, 0)), *weight_specs(lane)],
        out_specs=(
            pl.BlockSpec((tile, count), lambda i: (i, 0)),
            pl.BlockSpec((tile, count), lambda i: (i, 0)),
            pl.BlockSpec((tile, width), lambda i: (i, 0)),
            pl.BlockSpec((width, tile), lambda i: (0, i)),
        ),
        compiler_params=pltpu.CompilerParams(vmem_limit_bytes=VMEM_LIMIT),
        cost_estimate=pl.CostEstimate(
            flops=2 * count * width * hidden,
            transcendentals=count * hidden,
            bytes_accessed=6 * count * hidden + 8 * hidden * width,
        ),
    )(rows, lane, partner, lane, partner)


def store_shares(term, mine_ref, theirs_ref):
    share = mine_ref.shape[2]
    for y in range(2):
        mine_ref[0, y] = term[y * share : (y + 1) * share]
        theirs_ref[0, y] = term[(y + 2) * share : (y + 3) * share].astype(theirs_ref.dtype)


def expert_out_grad_kernel(scale, hidden_ref, grads_ref, mine_ref, theirs_ref):
    term = jnp.dot(hidden_ref[...], grads_ref[...], preferred_element_type=jnp.float32)
    store_shares(term * scale, mine_ref, theirs_ref)


def expert_in_grad_kernel(
    scale,
    slope_ref,
    out_weight_ref,
    rows_ref,
    grads_ref,
    mine_ref,
    theirs_ref,
    pre_grad_ref,
):
    hidden_grad = dot_rows(out_weight_ref[...], grads_ref[...])
    pre_grad = (hidden_grad * slope_ref[...]).astype(jnp.bfloat16)
    pre_grad_ref[...] = pre_grad
    term = jnp.dot(pre_grad, rows_ref[...], preferred_element_type=jnp.float32)
    store_shares(term * scale, mine_ref, theirs_ref)


def rows_back_kernel(pre_grad_ref, in_weight_ref, back_ref, total):
    step = pl.program_id(0)
    part = jnp.dot(in_weight_ref[...], pre_grad_ref[...], preferred_element_type=jnp.float32)

    @pl.when(step == 0)
    def _():
        total[...] = part

    @pl.when(step > 0)
    def _():
        total[...] += part

    @pl.when(step == pl.num_programs(0) - 1)
    def _():
        back_ref[...] = total[...].T.astype(back_ref.dtype)


def share_shapes(hidden, width):
    shape = (4, 2, hidden // 16, width)
    spec = pl.BlockSpec((1, *shape[1:]), lambda i: (i, 0, 0, 0))
    shapes = (
        jax.ShapeDtypeStruct(shape, jnp.float32),
        jax.ShapeDtypeStruct(shape, jnp.bfloat16),
    )
    return shapes, (spec, spec)


def expert_out_grad(hidden, grads, scale):
    units, count = hidden.shape
    width = grads.shape[1]
    shapes, specs = share_shapes(units, width)
    return pl.pallas_call(
        lambda *refs: expert_out_grad_kernel(scale, *refs),
        grid=(4,),
        out_shape=shapes,
        in_specs=[
            pl.BlockSpec((units // 4, count), lambda i: (i, 0)),
            pl.BlockSpec((count, width), lambda i: (0, 0)),
        ],
        out_specs=specs,
        compiler_params=pltpu.CompilerParams(vmem_limit_bytes=VMEM_LIMIT),
        cost_estimate=pl.CostEstimate(
            flops=2 * units * count * width, transcendentals=0, bytes_accessed=2 * units * count
        ),
    )(hidden, grads)


def expert_in_grad(slopes, out_weight, rows, grads, scale):
    units, count = slopes.shape
    width = grads.shape[1]
    shapes, specs = share_shapes(units, width)
    return pl.pallas_call(
        lambda *refs: expert_in_grad_kernel(scale, *refs),
        grid=(4,),
        out_shape=(*shapes, jax.ShapeDtypeStruct((units, count), jnp.bfloat16)),
        in_specs=[
            pl.BlockSpec((units // 4, count), lambda i: (i, 0)),
            pl.BlockSpec((units // 4, width), lambda i: (i, 0)),
            pl.BlockSpec((count, width), lambda i: (0, 0)),
            pl.BlockSpec((count, width), lambda i: (0, 0)),
        ],
        out_specs=(*specs, pl.BlockSpec((units // 4, count), lambda i: (i, 0))),
        compiler_params=pltpu.CompilerParams(vmem_limit_bytes=VMEM_LIMIT),
        cost_estimate=pl.CostEstimate(
            flops=4 * units * count * width, transcendentals=0, bytes_accessed=6 * units * count
        ),
    )(slopes, out_weight, rows, grads)


def rows_back(pre_grad, in_weight):
    units, count = pre_grad.shape
    width = in_weight.shape[0]
    return pl.pallas_call(
        rows_back_kernel,
        grid=(4,),
        out_shape=jax.ShapeDtypeStruct((count, width), jnp.bfloat16),
        in_specs=[
            pl.BlockSpec((units // 4, count), lambda i: (i, 0)),
            pl.BlockSpec((width, units // 4), lambda i: (0, i)),
        ],
        out_specs=pl.BlockSpec((count, width), lambda i: (0, 0)),
        scratch_shapes=[pltpu.VMEM((width, count), jnp.float32)],
        compiler_params=pltpu.CompilerParams(vmem_limit_bytes=VMEM_LIMIT),
        cost_estimate=pl.CostEstimate(
            flops=units * count, transcendentals=0, bytes_accessed=count * width
        ),
    )(pre_grad, in_weight)


def swap(block, distance):
    return hop(block.astype(jnp.bfloat16), "blk", lambda i: i ^ distance)


def swap_over_z(blocks):
    return [swap(blocks[d], 4 * d) for d in (1, 2, 3)]


def add_swapped(own, swapped):
    first, second, third = [block.astype(jnp.float32) for block in swapped]
    return own + (first + (second + third))


def local(
    nodes,
    attention_weights,
    output_weight,
    router_weight,
    gain_first,
    gain_second,
    expert_in,
    expert_out,
    routes,
    cotangent,
):
    exp_count = lax.axis_size("exp")
    blk_count = lax.axis_size("blk")
    block_rows = nodes.shape[0]
    width = nodes.shape[1]
    features = attention_weights.shape[1]
    own_rows = block_rows // exp_count
    capacity = 4 * block_rows // (exp_count * exp_count)
    experts = router_weight.shape[0]
    grad_scale = 1.0 / math.sqrt(block_rows * blk_count)
    projected = jnp.einsum(
        "fd,td->ft",
        attention_weights.reshape(3 * features, width),
        nodes,
        preferred_element_type=jnp.float32,
    ).astype(jnp.bfloat16)
    attended, lane_parts = attention(
        projected, output_weight, jnp.concatenate([expert_in, expert_out], axis=0), exp_count
    )
    from_heads = exchange(attended)
    from_heads, lane_parts = lax.optimization_barrier((from_heads, lane_parts))
    lane = jnp.stack(lane_parts)
    lane_partner = hop(lane, "blk", lambda i: i ^ 1)
    attn_out = jnp.einsum(
        "hfr,hfd->rd",
        from_heads[:, :, width:],
        from_heads[:, :, :width],
        preferred_element_type=jnp.float32,
    )
    own_nodes = lax.dynamic_slice_in_dim(
        nodes, lax.axis_index("exp") * own_rows, own_rows, 0
    ).astype(jnp.float32)
    stream = rms_gain(own_nodes + attn_out, gain_first).astype(jnp.bfloat16)
    logits = jnp.dot(stream, router_weight.T, preferred_element_type=jnp.float32)
    flat_routes = routes.reshape(2 * own_rows)
    choose = (flat_routes[:, None] == jnp.arange(experts, dtype=jnp.int32)[None, :]).astype(
        jnp.int32
    )
    before = jnp.cumsum(choose, axis=0) - choose
    slot_index = jnp.sum(before * choose, axis=1)
    position = flat_routes * capacity + slot_index
    dispatch_table = (
        jnp.arange(experts * capacity, dtype=jnp.int32)[:, None] == position[None, :]
    ).astype(jnp.bfloat16)
    selected = choose.reshape(own_rows, 2, experts).astype(jnp.float32)

    def gate_values(values):
        picked = jnp.sum(jax.nn.sigmoid(values)[:, None, :] * selected, axis=-1)
        return picked / jnp.sum(picked, axis=-1, keepdims=True)

    gates, gate_back = jax.vjp(gate_values, logits)
    repeated = jnp.repeat(stream, 2, axis=0)
    outgoing = jnp.dot(dispatch_table, repeated, preferred_element_type=jnp.float32).astype(
        jnp.bfloat16
    )
    outgoing = outgoing.reshape(experts, capacity, width)
    arrived = exchange(outgoing).reshape(experts * capacity, width)
    result = expert_forward(arrived, lane, lane_partner)
    returned = exchange(result.reshape(experts, capacity, width))
    kept, result = lax.optimization_barrier((arrived, result))
    hidden, slopes, out_weight, in_weight = expert_slopes(kept, lane, lane_partner)
    returned, hidden, slopes = lax.optimization_barrier((returned, hidden, slopes))
    expert_rows = jnp.einsum(
        "ps,pd->sd",
        dispatch_table,
        returned.reshape(experts * capacity, width),
        preferred_element_type=jnp.float32,
    )
    expert_rows = expert_rows.reshape(own_rows, 2, width)
    mixture = gates[:, 0:1] * expert_rows[:, 0] + gates[:, 1:2] * expert_rows[:, 1]
    stream_two = stream.astype(jnp.float32) + mixture
    normed, norm_back = jax.vjp(rms_gain, stream_two, gain_second)
    layer_out = normed.astype(jnp.bfloat16)
    grad_two, gain_part = norm_back(cotangent.astype(jnp.float32))
    gate_grads = jnp.sum(expert_rows * grad_two[:, None, :], axis=-1)
    logit_grad = gate_back(gate_grads)[0]
    router_part = jnp.dot(
        logit_grad.T, stream.astype(jnp.float32), precision=lax.Precision.HIGHEST
    )
    small = jnp.concatenate([router_part, gain_part[None, :]], axis=0) * grad_scale
    small = sum_pair(sum_near(small, "exp", 1), "exp", 4)
    small = sum_near(small, "blk", 4)
    assigned_grads = (
        (gates[..., None] * grad_two[:, None, :]).astype(jnp.bfloat16).reshape(2 * own_rows, width)
    )
    grad_outgoing = jnp.dot(
        dispatch_table, assigned_grads, preferred_element_type=jnp.float32
    ).astype(jnp.bfloat16)
    grad_arrived = exchange(grad_outgoing.reshape(experts, capacity, width)).reshape(
        experts * capacity, width
    )
    grad_arrived, small = lax.optimization_barrier((grad_arrived, small))
    out_mine, out_theirs = expert_out_grad(hidden, grad_arrived, grad_scale)
    out_sums = out_mine + swap(out_theirs, 1).astype(jnp.float32)
    out_sent = out_sums[:, 1].astype(jnp.bfloat16)
    out_beside = swap(out_sent, 2)
    small = sum_pair(small, "blk", 2)
    grad_arrived, out_sums, out_sent = lax.optimization_barrier(
        (grad_arrived, out_sums, out_sent)
    )
    in_mine, in_theirs, pre_grad = expert_in_grad(
        slopes, out_weight, kept, grad_arrived, grad_scale
    )
    in_swapped = swap(in_theirs, 1)
    pre_grad, in_mine, small = lax.optimization_barrier((pre_grad, in_mine, small))
    row_grads = rows_back(pre_grad, in_weight)
    small = sum_pair(small, "blk", 1)
    router_grad, gain_grad = small[:-1], small[-1]
    in_mine, in_swapped, row_grads, out_beside = lax.optimization_barrier(
        (in_mine, in_swapped, row_grads, out_beside)
    )
    in_sums = in_mine + in_swapped.astype(jnp.float32)
    in_parts = swap_over_z(in_sums)
    out_sums = out_sums[:, 0] + out_beside.astype(jnp.float32)
    expert_out_grads = add_swapped(out_sums[0], swap_over_z(out_sums))[None]
    in_sums = add_swapped(in_sums[0], in_parts)
    expert_in_grads = (in_sums[0] + swap(in_sums[1], 2).astype(jnp.float32))[None]
    back_home = exchange(row_grads.reshape(experts, capacity, width))
    back_rows = jnp.einsum(
        "ps,pd->sd",
        dispatch_table,
        back_home.reshape(experts * capacity, width),
        preferred_element_type=jnp.float32,
    )
    back_rows = back_rows.reshape(own_rows, 2, width)
    router_term = jnp.dot(
        logit_grad, router_weight.astype(jnp.float32), precision=lax.Precision.HIGHEST
    )
    stream_grad = (grad_two + (back_rows[:, 0] + back_rows[:, 1]) + router_term).astype(
        jnp.bfloat16
    )
    return (layer_out, stream_grad, expert_in_grads, expert_out_grads, router_grad, gain_grad)


def solution(mesh):
    placed = (
        P("blk", None),
        P(None, "exp", None),
        P("exp", None),
        P(),
        P(),
        P(),
        P("exp", "blk", None),
        P("exp", "blk", None),
        P(("blk", "exp"), None),
        P(("blk", "exp"), None),
    )
    return jax.shard_map(
        local,
        mesh=mesh,
        in_specs=placed,
        out_specs=(
            P(("blk", "exp"), None),
            P(("blk", "exp"), None),
            P("exp", "blk", None),
            P("exp", "blk", None),
            P(),
            P(),
        ),
        check_vma=False,
    )
```

```python
import math

import jax
import jax.numpy as jnp
from jax import lax
from jax.experimental import pallas as pl
from jax.experimental.pallas import tpu as pltpu
from jax.sharding import PartitionSpec as P

HD = 32

EPSILON = 1e-06
LOG2_SCALE = math.log2(math.e) / math.sqrt(HD)
SHIFT_KEYS = 256
SUM_LIMIT = 2.0**100
ATTENTION_VMEM = 40 * 2**20
EXPERT_VMEM = 24 * 2**20
SUM_ROWS = 16
TANH_SCALE = math.sqrt(2.0 / math.pi)
CUBE = 0.044715


def rms_gain(stream, gain):
    return stream * lax.rsqrt(jnp.mean(stream * stream, axis=-1, keepdims=True) + EPSILON) * gain


def exchange(buffer):
    return lax.all_to_all(buffer, "exp", split_axis=0, concat_axis=0, tiled=True)


def hop(value, axis, target):
    count = lax.axis_size(axis)
    return lax.ppermute(value, axis, [(i, target(i) % count) for i in range(count)])


def split_terms(value, terms):
    pieces = []
    for _ in range(terms):
        piece = value.astype(jnp.bfloat16)
        pieces.append(piece)
        value = value - piece.astype(jnp.float32)
    return pieces


def key_blocks(refs):
    return [
        (ref, start) for ref in refs for start in range(0, ref.shape[0], 2 * HD)
    ]


def own_blocks(own_ref):
    return [(own_ref, HD)]


def load_keys(blocks, keys, values):
    width = blocks[0][0].shape[1]
    ones = (lax.broadcasted_iota(jnp.int32, (HD, width), 0) < 3).astype(jnp.bfloat16)
    one = (lax.broadcasted_iota(jnp.int32, (HD // 2, width), 0) < 1).astype(jnp.bfloat16)
    for index, (ref, start) in enumerate(blocks):
        block = ref[start : start + HD, :]
        span = slice(index * width, (index + 1) * width)
        keys[span, :] = jnp.concatenate([block, block, block, ones], axis=0).T
        values[:, span] = jnp.concatenate([ref[start + HD : start + 2 * HD, :], one], axis=0)


def add_blocks(count, width, query, keys, values, total):
    def step(index, running):
        span = pl.ds(pl.multiple_of(index * width, width), width)
        exponents = jnp.dot(keys[span, :], query, preferred_element_type=jnp.float32)
        weights = jnp.exp2(exponents).astype(jnp.bfloat16)
        return running + jnp.dot(values[:, span], weights, preferred_element_type=jnp.float32)

    return lax.fori_loop(0, count, step, total)


def first_keys_kernel(count, own_ref, *refs):
    blocks, (wide_ref, total_ref, keys, values) = refs[:-4], refs[-4:]
    load_keys(own_blocks(own_ref) + key_blocks(blocks), keys, values)
    width = own_ref.shape[1]
    scaled = own_ref[:HD, :].astype(jnp.float32) * LOG2_SCALE
    pieces = split_terms(scaled, 3)
    wide_ref[...] = jnp.concatenate(pieces + [jnp.zeros_like(pieces[0])], axis=0)
    some = jnp.dot(keys[:SHIFT_KEYS, :], wide_ref[...], preferred_element_type=jnp.float32)
    shift = split_terms(-jnp.max(some, axis=0, keepdims=True), 3)
    row = lax.broadcasted_iota(jnp.int32, (HD, width), 0)
    rows = jnp.zeros((HD, width), jnp.float32)
    for index, piece in enumerate(shift):
        rows = jnp.where(row == index, piece.astype(jnp.float32), rows)
    wide_ref[3 * HD :, :] = rows.astype(jnp.bfloat16)
    total_ref[...] = add_blocks(
        count, width, wide_ref[...], keys, values, jnp.zeros(total_ref.shape, jnp.float32)
    )


def more_keys_kernel(count, wide_ref, before_ref, *refs):
    blocks, (total_ref, keys, values) = refs[:-3], refs[-3:]
    load_keys(key_blocks(blocks), keys, values)
    total_ref[...] = add_blocks(
        count, wide_ref.shape[1], wide_ref[...], keys, values, before_ref[...]
    )


def last_keys_kernel(count, fresh, wide_ref, before_ref, own_ref, output_weight_ref, *refs):
    blocks, (out_ref, keys, values, total) = refs[:-4], refs[-4:]
    load_keys(key_blocks(blocks[:fresh]), keys, values)
    width = wide_ref.shape[1]
    total[...] = add_blocks(count, width, wide_ref[...], keys, values, before_ref[...])
    sums = total[HD : HD + 1, :]
    inside = jnp.logical_and(sums <= SUM_LIMIT, sums >= 1.0 / SUM_LIMIT)
    outside = jnp.sum(jnp.where(inside, 0, 1))

    @pl.when(outside > 0)
    def _():
        query = own_ref[:HD, :]
        query = jnp.concatenate([query, jnp.zeros((3 * HD, width), query.dtype)], axis=0)
        total[...] = jnp.zeros(total.shape, jnp.float32)

        def step(index, top):
            span = pl.ds(pl.multiple_of(index * SHIFT_KEYS, SHIFT_KEYS), SHIFT_KEYS)
            scores = LOG2_SCALE * jnp.dot(
                keys[span, :], query, preferred_element_type=jnp.float32
            )
            new_top = jnp.maximum(top, jnp.max(scores, axis=0, keepdims=True))
            weights = jnp.exp2(scores - new_top).astype(jnp.bfloat16)
            total[...] = total[...] * jnp.exp2(top - new_top) + jnp.dot(
                values[:, span], weights, preferred_element_type=jnp.float32
            )
            return new_top

        top = jnp.full((1, width), -1e30, jnp.float32)
        every = own_blocks(own_ref) + key_blocks(blocks)
        for group in [every[i : i + count] for i in range(0, len(every), count)]:
            load_keys(group, keys, values)
            top = lax.fori_loop(0, len(group) * (width // SHIFT_KEYS), step, top)

    attended = (total[:HD, :] / total[HD : HD + 1, :]).astype(jnp.bfloat16)
    weight = output_weight_ref[...]
    features = weight.shape[1]
    rows = out_ref.shape[2] - features
    for index in range(out_ref.shape[0]):
        out_ref[index, :, :features] = weight
        out_ref[index, :, features:] = attended[:, index * rows : (index + 1) * rows]


def block_count(arrays):
    return sum(array.shape[0] for array in arrays) // (2 * HD)


def attention_call(kernel, out_shape, operands, count, width, extra=(), aliases=None):
    specs = [pl.BlockSpec(memory_space=pltpu.VMEM)]
    return pl.pallas_call(
        kernel,
        out_shape=out_shape,
        in_specs=specs * len(operands),
        out_specs=jax.tree.map(lambda _: specs[0], out_shape),
        scratch_shapes=[
            pltpu.VMEM((count * width, 4 * HD), jnp.bfloat16),
            pltpu.VMEM((HD + HD // 2, count * width), jnp.bfloat16),
            *extra,
        ],
        input_output_aliases=aliases or {},
        compiler_params=pltpu.CompilerParams(vmem_limit_bytes=ATTENTION_VMEM),
        cost_estimate=pl.CostEstimate(
            flops=count * width * width * 1200,
            transcendentals=count * width * width,
            bytes_accessed=count * width * 4 * HD,
        ),
    )(*operands)


def near_hops(value):
    return [hop(value, "blk", lambda i, step=step: i ^ step) for step in (2, 4, 12, 8)]


def attention(projected, output_weight, expert_weights, owners):
    width = projected.shape[1]
    keys_values = projected[HD:]
    partner = hop(keys_values, "blk", lambda i: i ^ 1)
    near = near_hops(keys_values)
    total_shape = jax.ShapeDtypeStruct((HD + HD // 2, width), jnp.float32)
    wide_shape = jax.ShapeDtypeStruct((4 * HD, width), jnp.bfloat16)
    wide, total = attention_call(
        lambda *refs: first_keys_kernel(2, *refs),
        (wide_shape, total_shape),
        [projected, partner],
        2,
        width,
    )

    def more(total, group):
        count = block_count(group)
        return attention_call(
            lambda *refs: more_keys_kernel(count, *refs),
            total_shape,
            [wide, total, *group],
            count,
            width,
            aliases={1: 0},
        )

    near, total = lax.optimization_barrier((near, total))
    beyond = hop(jnp.concatenate(near[1:], axis=0), "blk", lambda i: i ^ 2)
    near_partner = hop(jnp.concatenate(near, axis=0), "blk", lambda i: i ^ 1)
    total = more(total, near)
    near_partner, expert_weights, total = lax.optimization_barrier(
        (near_partner, expert_weights, total)
    )
    beside = hop(expert_weights, "blk", lambda i: i ^ 2)
    total = more(total, [near_partner])
    beyond, beside, total = lax.optimization_barrier((beyond, beside, total))
    beyond_partner = hop(beyond, "blk", lambda i: i ^ 1)
    pair = jnp.stack([expert_weights, beside])
    lane = [pair, *[hop(pair, "blk", lambda i, step=step: i ^ step) for step in (4, 8, 12)]]
    total = more(total, [beyond])
    beyond_partner, total = lax.optimization_barrier((beyond_partner, total))
    last = [beyond_partner]
    count = block_count(last)
    features = output_weight.shape[1]
    attended = attention_call(
        lambda *refs: last_keys_kernel(count, len(last), *refs),
        jax.ShapeDtypeStruct((owners, HD, features + width // owners), jnp.bfloat16),
        [wide, total, projected, output_weight, *last, partner, *near, near_partner, beyond],
        count,
        width,
        extra=[pltpu.VMEM(total_shape.shape, jnp.float32)],
    )
    return attended, lane


def add_rows(block, rows):
    return jnp.concatenate([block.reshape(-1, block.shape[-1]), rows], axis=0)


def dot_rows(first, second):
    return lax.dot_general(
        first, second, (((1,), (1,)), ((), ())), preferred_element_type=jnp.float32
    )


def tanh_part(values):
    return jnp.tanh(TANH_SCALE * (values + CUBE * (values * values * values)))


def tile_rows(lane_ref, partner_ref):
    share, width = lane_ref.shape[1:]
    return jnp.concatenate(
        [ref[...].reshape(2 * share, width) for ref in (lane_ref, partner_ref)], axis=0
    )


def weight_specs(weights):
    _, _, _, share, width = weights.shape
    return [
        pl.BlockSpec((None, 2, None, share, width), lambda i, which=which: (i, 0, which, 0, 0))
        for which in (0, 0, 1, 1)
    ]


def expert_forward_kernel(rows_ref, in_lane, in_partner, out_lane, out_partner, result_ref, total):
    step = pl.program_id(0)
    pre_act = dot_rows(rows_ref[...], tile_rows(in_lane, in_partner))
    hidden = (pre_act * (0.5 * (1.0 + tanh_part(pre_act)))).astype(jnp.bfloat16)
    part = jnp.dot(
        hidden, tile_rows(out_lane, out_partner), preferred_element_type=jnp.float32
    )

    @pl.when(step == 0)
    def _():
        total[...] = part

    @pl.when(step > 0)
    def _():
        total[...] += part

    @pl.when(step == pl.num_programs(0) - 1)
    def _():
        result_ref[...] = total[...].astype(result_ref.dtype)


def expert_forward(rows, lane, partner):
    count, width = rows.shape
    hidden = lane.size // width
    return pl.pallas_call(
        expert_forward_kernel,
        grid=(lane.shape[0],),
        out_shape=jax.ShapeDtypeStruct((count, width), jnp.bfloat16),
        in_specs=[pl.BlockSpec((count, width), lambda i: (0, 0)), *weight_specs(lane)],
        out_specs=pl.BlockSpec((count, width), lambda i: (0, 0)),
        scratch_shapes=[pltpu.VMEM((count, width), jnp.float32)],
        compiler_params=pltpu.CompilerParams(vmem_limit_bytes=EXPERT_VMEM),
        cost_estimate=pl.CostEstimate(
            flops=4 * count * width * hidden,
            transcendentals=count * hidden,
            bytes_accessed=4 * hidden * width,
        ),
    )(rows, lane, partner, lane, partner)


def expert_slopes_kernel(
    rows_ref,
    in_lane,
    in_partner,
    out_lane,
    out_partner,
    hidden_ref,
    slope_ref,
    out_weight_ref,
    in_weight_ref,
):
    weight_in = tile_rows(in_lane, in_partner)
    out_weight_ref[...] = tile_rows(out_lane, out_partner)
    in_weight_ref[...] = weight_in.T
    pre_act = dot_rows(weight_in, rows_ref[...])
    tanh = tanh_part(pre_act)
    half = 0.5 * (1.0 + tanh)
    hidden_ref[...] = (pre_act * half).astype(hidden_ref.dtype)
    slope_ref[...] = half + pre_act * (0.5 * (1.0 - tanh * tanh)) * (
        TANH_SCALE * (1.0 + 3.0 * CUBE * (pre_act * pre_act))
    )


def expert_slopes(rows, lane, partner):
    count, width = rows.shape
    hidden = lane.size // width
    tile = hidden // lane.shape[0]
    return pl.pallas_call(
        expert_slopes_kernel,
        grid=(lane.shape[0],),
        out_shape=(
            jax.ShapeDtypeStruct((hidden, count), jnp.bfloat16),
            jax.ShapeDtypeStruct((hidden, count), jnp.float32),
            jax.ShapeDtypeStruct((hidden, width), jnp.bfloat16),
            jax.ShapeDtypeStruct((width, hidden), jnp.bfloat16),
        ),
        in_specs=[pl.BlockSpec((count, width), lambda i: (0, 0)), *weight_specs(lane)],
        out_specs=(
            pl.BlockSpec((tile, count), lambda i: (i, 0)),
            pl.BlockSpec((tile, count), lambda i: (i, 0)),
            pl.BlockSpec((tile, width), lambda i: (i, 0)),
            pl.BlockSpec((width, tile), lambda i: (0, i)),
        ),
        compiler_params=pltpu.CompilerParams(vmem_limit_bytes=EXPERT_VMEM),
        cost_estimate=pl.CostEstimate(
            flops=2 * count * width * hidden,
            transcendentals=count * hidden,
            bytes_accessed=6 * count * hidden + 8 * hidden * width,
        ),
    )(rows, lane, partner, lane, partner)


def store_shares(term, mine_ref, theirs_ref):
    share = mine_ref.shape[2]
    for y in range(2):
        mine_ref[0, y] = term[y * share : (y + 1) * share]
        theirs_ref[0, y] = term[(y + 2) * share : (y + 3) * share].astype(theirs_ref.dtype)


def routed_rows(grads_ref):
    sources, rows, width = grads_ref.shape
    rows = rows - SUM_ROWS
    return grads_ref[:, :rows, :].reshape(sources * rows, width)


def expert_out_grad_kernel(scale, hidden_ref, grads_ref, mine_ref, theirs_ref):
    term = jnp.dot(hidden_ref[...], routed_rows(grads_ref), preferred_element_type=jnp.float32)
    store_shares(term * scale, mine_ref, theirs_ref)


def expert_in_grad_kernel(
    scale,
    slope_ref,
    out_weight_ref,
    rows_ref,
    grads_ref,
    mine_ref,
    theirs_ref,
    pre_grad_ref,
):
    hidden_grad = dot_rows(out_weight_ref[...], routed_rows(grads_ref))
    pre_grad = (hidden_grad * slope_ref[...]).astype(jnp.bfloat16)
    pre_grad_ref[...] = pre_grad
    term = jnp.dot(pre_grad, rows_ref[...], preferred_element_type=jnp.float32)
    store_shares(term * scale, mine_ref, theirs_ref)


def rows_back_kernel(pre_grad_ref, in_weight_ref, back_ref, total):
    step = pl.program_id(0)
    part = jnp.dot(in_weight_ref[...], pre_grad_ref[...], preferred_element_type=jnp.float32)

    @pl.when(step == 0)
    def _():
        total[...] = part

    @pl.when(step > 0)
    def _():
        total[...] += part

    @pl.when(step == pl.num_programs(0) - 1)
    def _():
        back_ref[...] = total[...].T.astype(back_ref.dtype)


def share_shapes(hidden, width):
    shape = (4, 2, hidden // 16, width)
    spec = pl.BlockSpec((1, *shape[1:]), lambda i: (i, 0, 0, 0))
    shapes = (
        jax.ShapeDtypeStruct(shape, jnp.float32),
        jax.ShapeDtypeStruct(shape, jnp.bfloat16),
    )
    return shapes, (spec, spec)


def expert_out_grad(hidden, grads, scale):
    units, count = hidden.shape
    width = grads.shape[2]
    shapes, specs = share_shapes(units, width)
    return pl.pallas_call(
        lambda *refs: expert_out_grad_kernel(scale, *refs),
        grid=(4,),
        out_shape=shapes,
        in_specs=[
            pl.BlockSpec((units // 4, count), lambda i: (i, 0)),
            pl.BlockSpec(grads.shape, lambda i: (0, 0, 0)),
        ],
        out_specs=specs,
        compiler_params=pltpu.CompilerParams(vmem_limit_bytes=EXPERT_VMEM),
        cost_estimate=pl.CostEstimate(
            flops=2 * units * count * width, transcendentals=0, bytes_accessed=2 * units * count
        ),
    )(hidden, grads)


def expert_in_grad(slopes, out_weight, rows, grads, scale):
    units, count = slopes.shape
    width = grads.shape[2]
    shapes, specs = share_shapes(units, width)
    return pl.pallas_call(
        lambda *refs: expert_in_grad_kernel(scale, *refs),
        grid=(4,),
        out_shape=(*shapes, jax.ShapeDtypeStruct((units, count), jnp.bfloat16)),
        in_specs=[
            pl.BlockSpec((units // 4, count), lambda i: (i, 0)),
            pl.BlockSpec((units // 4, width), lambda i: (i, 0)),
            pl.BlockSpec((count, width), lambda i: (0, 0)),
            pl.BlockSpec(grads.shape, lambda i: (0, 0, 0)),
        ],
        out_specs=(*specs, pl.BlockSpec((units // 4, count), lambda i: (i, 0))),
        compiler_params=pltpu.CompilerParams(vmem_limit_bytes=EXPERT_VMEM),
        cost_estimate=pl.CostEstimate(
            flops=4 * units * count * width, transcendentals=0, bytes_accessed=6 * units * count
        ),
    )(slopes, out_weight, rows, grads)


def rows_back(pre_grad, in_weight):
    units, count = pre_grad.shape
    width = in_weight.shape[0]
    return pl.pallas_call(
        rows_back_kernel,
        grid=(4,),
        out_shape=jax.ShapeDtypeStruct((count, width), jnp.bfloat16),
        in_specs=[
            pl.BlockSpec((units // 4, count), lambda i: (i, 0)),
            pl.BlockSpec((width, units // 4), lambda i: (0, i)),
        ],
        out_specs=pl.BlockSpec((count, width), lambda i: (0, 0)),
        scratch_shapes=[pltpu.VMEM((width, count), jnp.float32)],
        compiler_params=pltpu.CompilerParams(vmem_limit_bytes=EXPERT_VMEM),
        cost_estimate=pl.CostEstimate(
            flops=units * count, transcendentals=0, bytes_accessed=count * width
        ),
    )(pre_grad, in_weight)


def swap(block, distance):
    return hop(block.astype(jnp.bfloat16), "blk", lambda i: i ^ distance)


def swap_over_z(blocks):
    return [swap(blocks[d], 4 * d) for d in (1, 2, 3)]


def add_swapped(own, swapped):
    first, second, third = [block.astype(jnp.float32) for block in swapped]
    return own + (first + (second + third))


def local(
    nodes,
    attention_weights,
    output_weight,
    router_weight,
    gain_first,
    gain_second,
    expert_in,
    expert_out,
    routes,
    cotangent,
):
    exp_count = lax.axis_size("exp")
    blk_count = lax.axis_size("blk")
    block_rows = nodes.shape[0]
    width = nodes.shape[1]
    features = attention_weights.shape[1]
    own_rows = block_rows // exp_count
    capacity = 4 * block_rows // (exp_count * exp_count)
    experts = router_weight.shape[0]
    grad_scale = 1.0 / math.sqrt(block_rows * blk_count)
    projected = jnp.einsum(
        "fd,td->ft",
        attention_weights.reshape(3 * features, width),
        nodes,
        preferred_element_type=jnp.float32,
    ).astype(jnp.bfloat16)
    attended, lane_parts = attention(
        projected, output_weight, jnp.concatenate([expert_in, expert_out], axis=0), exp_count
    )
    from_heads = exchange(attended)
    from_heads, lane_parts = lax.optimization_barrier((from_heads, lane_parts))
    attn_out = jnp.einsum(
        "hfr,hfd->rd",
        from_heads[:, :, width:],
        from_heads[:, :, :width],
        preferred_element_type=jnp.float32,
    )
    own_nodes = lax.dynamic_slice_in_dim(
        nodes, lax.axis_index("exp") * own_rows, own_rows, 0
    ).astype(jnp.float32)
    stream = rms_gain(own_nodes + attn_out, gain_first).astype(jnp.bfloat16)
    lane_parts, late_stream = lax.optimization_barrier((lane_parts, stream))
    lane = jnp.stack(lane_parts)
    lane_partner = hop(lane, "blk", lambda i: i ^ 1)
    logits = jnp.dot(late_stream, router_weight.T, preferred_element_type=jnp.float32)
    flat_routes = routes.reshape(2 * own_rows)
    choose = (flat_routes[:, None] == jnp.arange(experts, dtype=jnp.int32)[None, :]).astype(
        jnp.int32
    )
    before = jnp.cumsum(choose, axis=0) - choose
    slot_index = jnp.sum(before * choose, axis=1)
    position = flat_routes * capacity + slot_index
    dispatch_table = (
        jnp.arange(experts * capacity, dtype=jnp.int32)[:, None] == position[None, :]
    ).astype(jnp.bfloat16)
    selected = choose.reshape(own_rows, 2, experts).astype(jnp.float32)

    def gate_values(values):
        picked = jnp.sum(jax.nn.sigmoid(values)[:, None, :] * selected, axis=-1)
        return picked / jnp.sum(picked, axis=-1, keepdims=True)

    gates, gate_back = jax.vjp(gate_values, logits)
    repeated = jnp.repeat(stream, 2, axis=0)
    outgoing = jnp.dot(dispatch_table, repeated, preferred_element_type=jnp.float32).astype(
        jnp.bfloat16
    )
    outgoing = outgoing.reshape(experts, capacity, width)
    arrived = exchange(outgoing).reshape(experts * capacity, width)
    result = expert_forward(arrived, lane, lane_partner)
    returned = exchange(result.reshape(experts, capacity, width))
    kept, result = lax.optimization_barrier((arrived, result))
    hidden, slopes, out_weight, in_weight = expert_slopes(kept, lane, lane_partner)
    returned, hidden, slopes = lax.optimization_barrier((returned, hidden, slopes))
    expert_rows = jnp.einsum(
        "ps,pd->sd",
        dispatch_table,
        returned.reshape(experts * capacity, width),
        preferred_element_type=jnp.float32,
    )
    expert_rows = expert_rows.reshape(own_rows, 2, width)
    mixture = gates[:, 0:1] * expert_rows[:, 0] + gates[:, 1:2] * expert_rows[:, 1]
    stream_two = stream.astype(jnp.float32) + mixture
    normed, norm_back = jax.vjp(rms_gain, stream_two, gain_second)
    layer_out = normed.astype(jnp.bfloat16)
    grad_two, gain_part = norm_back(cotangent.astype(jnp.float32))
    gate_grads = jnp.sum(expert_rows * grad_two[:, None, :], axis=-1)
    logit_grad = gate_back(gate_grads)[0]
    router_part = jnp.dot(
        logit_grad.T, stream.astype(jnp.float32), precision=lax.Precision.HIGHEST
    )
    small = jnp.concatenate([router_part, gain_part[None, :]], axis=0) * grad_scale
    sum_rows = jnp.pad(small, ((0, SUM_ROWS - small.shape[0]), (0, 0))).astype(jnp.bfloat16)
    assigned_grads = (
        (gates[..., None] * grad_two[:, None, :]).astype(jnp.bfloat16).reshape(2 * own_rows, width)
    )
    padded = capacity + SUM_ROWS
    place = jnp.arange(experts * padded, dtype=jnp.int32)[:, None]
    row_experts = jnp.concatenate([flat_routes, jnp.full((SUM_ROWS,), -1, jnp.int32)])
    row_slots = jnp.concatenate([slot_index, capacity + jnp.arange(SUM_ROWS, dtype=jnp.int32)])
    anywhere = jnp.logical_or(place // padded == row_experts[None, :], row_experts[None, :] < 0)
    spread = jnp.logical_and(anywhere, place % padded == row_slots[None, :])
    grad_outgoing = jnp.dot(
        spread.astype(jnp.bfloat16),
        jnp.concatenate([assigned_grads, sum_rows], axis=0),
        preferred_element_type=jnp.float32,
    ).astype(jnp.bfloat16)
    grad_arrived = exchange(grad_outgoing.reshape(experts, padded, width))
    out_mine, out_theirs = expert_out_grad(hidden, grad_arrived, grad_scale)
    out_mine, out_theirs, grad_arrived = lax.optimization_barrier(
        (out_mine, out_theirs, grad_arrived)
    )
    sum_rows = jnp.sum(grad_arrived[:, capacity:].astype(jnp.float32), axis=0)
    sum_rows = sum_rows.astype(jnp.bfloat16)
    sums_swapped = swap(sum_rows, 1)
    out_swapped = swap(out_theirs, 1)
    in_mine, in_theirs, pre_grad = expert_in_grad(
        slopes, out_weight, kept, grad_arrived, grad_scale
    )
    in_swapped = swap(in_theirs, 1)
    sums_swapped, out_swapped, in_mine, pre_grad = lax.optimization_barrier(
        (sums_swapped, out_swapped, in_mine, pre_grad)
    )
    sum_rows = (sum_rows.astype(jnp.float32) + sums_swapped.astype(jnp.float32)).astype(
        jnp.bfloat16
    )
    out_sums = out_mine + out_swapped.astype(jnp.float32)
    out_sent = add_rows(out_sums[:, 1].astype(jnp.bfloat16), sum_rows)
    out_beside = swap(out_sent, 2)
    out_sent, out_sums, pre_grad = lax.optimization_barrier((out_sent, out_sums, pre_grad))
    row_grads = rows_back(pre_grad, in_weight)
    in_mine, in_swapped, row_grads = lax.optimization_barrier((in_mine, in_swapped, row_grads))
    back_home = exchange(row_grads.reshape(experts, capacity, width))
    in_sums = in_mine + in_swapped.astype(jnp.float32)
    in_parts = swap_over_z(in_sums)
    out_beside, in_sums = lax.optimization_barrier((out_beside, in_sums))
    sum_rows = (
        out_sent[-SUM_ROWS:].astype(jnp.float32) + out_beside[-SUM_ROWS:].astype(jnp.float32)
    ).astype(jnp.bfloat16)
    out_sums = out_sums[:, 0] + out_beside[:-SUM_ROWS].reshape(out_sums.shape[:1] + out_sums.shape[2:])
    out_parts = [
        swap(add_rows(out_sums[d].astype(jnp.bfloat16), sum_rows), 4 * d) for d in (1, 2, 3)
    ]
    expert_out_grads = add_swapped(out_sums[0], [part[:-SUM_ROWS] for part in out_parts])[None]
    first, second, third = [part[-SUM_ROWS:].astype(jnp.float32) for part in out_parts]
    sums = (sum_rows.astype(jnp.float32) + first) + (second + third)
    router_grad, gain_grad = sums[:experts], sums[experts]
    in_sums = add_swapped(in_sums[0], in_parts)
    back_home, in_sums = lax.optimization_barrier((back_home, in_sums))
    expert_in_grads = (in_sums[0] + swap(in_sums[1], 2).astype(jnp.float32))[None]
    back_rows = jnp.einsum(
        "ps,pd->sd",
        dispatch_table,
        back_home.reshape(experts * capacity, width),
        preferred_element_type=jnp.float32,
    )
    back_rows = back_rows.reshape(own_rows, 2, width)
    router_term = jnp.dot(
        logit_grad, router_weight.astype(jnp.float32), precision=lax.Precision.HIGHEST
    )
    stream_grad = (grad_two + (back_rows[:, 0] + back_rows[:, 1]) + router_term).astype(
        jnp.bfloat16
    )
    return (layer_out, stream_grad, expert_in_grads, expert_out_grads, router_grad, gain_grad)


def solution(mesh):
    placed = (
        P("blk", None),
        P(None, "exp", None),
        P("exp", None),
        P(),
        P(),
        P(),
        P("exp", "blk", None),
        P("exp", "blk", None),
        P(("blk", "exp"), None),
        P(("blk", "exp"), None),
    )
    return jax.shard_map(
        local,
        mesh=mesh,
        in_specs=placed,
        out_specs=(
            P(("blk", "exp"), None),
            P(("blk", "exp"), None),
            P("exp", "blk", None),
            P("exp", "blk", None),
            P(),
            P(),
        ),
        check_vma=False,
    )
```

```python
import math

import jax
import jax.numpy as jnp
from jax import lax
from jax.experimental import pallas as pl
from jax.experimental.pallas import tpu as pltpu
from jax.sharding import PartitionSpec as P

HD = 32

EPSILON = 1e-06
LOG2_SCALE = math.log2(math.e) / math.sqrt(HD)
SHIFT_KEYS = 256
SUM_LIMIT = 2.0**100
ATTENTION_VMEM = 40 * 2**20
EXPERT_VMEM = 24 * 2**20
SUM_ROWS = 16
TANH_SCALE = math.sqrt(2.0 / math.pi)
CUBE = 0.044715


def rms_gain(stream, gain):
    return stream * lax.rsqrt(jnp.mean(stream * stream, axis=-1, keepdims=True) + EPSILON) * gain


def exchange(buffer):
    return lax.all_to_all(buffer, "exp", split_axis=0, concat_axis=0, tiled=True)


def hop(value, axis, target):
    count = lax.axis_size(axis)
    return lax.ppermute(value, axis, [(i, target(i) % count) for i in range(count)])


def split_terms(value, terms):
    pieces = []
    for _ in range(terms):
        piece = value.astype(jnp.bfloat16)
        pieces.append(piece)
        value = value - piece.astype(jnp.float32)
    return pieces


def key_blocks(refs):
    return [
        (ref, start) for ref in refs for start in range(0, ref.shape[0], 2 * HD)
    ]


def own_blocks(own_ref):
    return [(own_ref, HD)]


def load_keys(blocks, keys, values):
    width = blocks[0][0].shape[1]
    ones = (lax.broadcasted_iota(jnp.int32, (HD, width), 0) < 3).astype(jnp.bfloat16)
    one = (lax.broadcasted_iota(jnp.int32, (HD // 2, width), 0) < 1).astype(jnp.bfloat16)
    for index, (ref, start) in enumerate(blocks):
        block = ref[start : start + HD, :]
        span = slice(index * width, (index + 1) * width)
        keys[span, :] = jnp.concatenate([block, block, block, ones], axis=0).T
        values[:, span] = jnp.concatenate([ref[start + HD : start + 2 * HD, :], one], axis=0)


def add_blocks(count, width, query, keys, values, total):
    chunk = width // 2

    def step(index, running):
        span = pl.ds(pl.multiple_of(index * chunk, chunk), chunk)
        exponents = jnp.dot(keys[span, :], query, preferred_element_type=jnp.float32)
        weights = jnp.exp2(exponents).astype(jnp.bfloat16)
        return running + jnp.dot(values[:, span], weights, preferred_element_type=jnp.float32)

    return lax.fori_loop(0, 2 * count, step, total)


def first_keys_kernel(count, own_ref, *refs):
    blocks, (wide_ref, total_ref, keys, values) = refs[:-4], refs[-4:]
    load_keys(own_blocks(own_ref) + key_blocks(blocks), keys, values)
    width = own_ref.shape[1]
    scaled = own_ref[:HD, :].astype(jnp.float32) * LOG2_SCALE
    pieces = split_terms(scaled, 3)
    wide_ref[...] = jnp.concatenate(pieces + [jnp.zeros_like(pieces[0])], axis=0)
    some = jnp.dot(keys[:SHIFT_KEYS, :], wide_ref[...], preferred_element_type=jnp.float32)
    shift = split_terms(-jnp.max(some, axis=0, keepdims=True), 3)
    row = lax.broadcasted_iota(jnp.int32, (HD, width), 0)
    rows = jnp.zeros((HD, width), jnp.float32)
    for index, piece in enumerate(shift):
        rows = jnp.where(row == index, piece.astype(jnp.float32), rows)
    wide_ref[3 * HD :, :] = rows.astype(jnp.bfloat16)
    total_ref[...] = add_blocks(
        count, width, wide_ref[...], keys, values, jnp.zeros(total_ref.shape, jnp.float32)
    )


def more_keys_kernel(count, wide_ref, before_ref, *refs):
    blocks, (total_ref, keys, values) = refs[:-3], refs[-3:]
    load_keys(key_blocks(blocks), keys, values)
    total_ref[...] = add_blocks(
        count, wide_ref.shape[1], wide_ref[...], keys, values, before_ref[...]
    )


def last_keys_kernel(count, fresh, wide_ref, before_ref, own_ref, output_weight_ref, *refs):
    blocks, (out_ref, keys, values, total) = refs[:-4], refs[-4:]
    load_keys(key_blocks(blocks[:fresh]), keys, values)
    width = wide_ref.shape[1]
    total[...] = add_blocks(count, width, wide_ref[...], keys, values, before_ref[...])
    sums = total[HD : HD + 1, :]
    inside = jnp.logical_and(sums <= SUM_LIMIT, sums >= 1.0 / SUM_LIMIT)
    outside = jnp.sum(jnp.where(inside, 0, 1))

    @pl.when(outside > 0)
    def _():
        query = own_ref[:HD, :]
        query = jnp.concatenate([query, jnp.zeros((3 * HD, width), query.dtype)], axis=0)
        total[...] = jnp.zeros(total.shape, jnp.float32)

        def step(index, top):
            span = pl.ds(pl.multiple_of(index * SHIFT_KEYS, SHIFT_KEYS), SHIFT_KEYS)
            scores = LOG2_SCALE * jnp.dot(
                keys[span, :], query, preferred_element_type=jnp.float32
            )
            new_top = jnp.maximum(top, jnp.max(scores, axis=0, keepdims=True))
            weights = jnp.exp2(scores - new_top).astype(jnp.bfloat16)
            total[...] = total[...] * jnp.exp2(top - new_top) + jnp.dot(
                values[:, span], weights, preferred_element_type=jnp.float32
            )
            return new_top

        top = jnp.full((1, width), -1e30, jnp.float32)
        every = own_blocks(own_ref) + key_blocks(blocks)
        for group in [every[i : i + count] for i in range(0, len(every), count)]:
            load_keys(group, keys, values)
            top = lax.fori_loop(0, len(group) * (width // SHIFT_KEYS), step, top)

    attended = (total[:HD, :] / total[HD : HD + 1, :]).astype(jnp.bfloat16)
    weight = output_weight_ref[...]
    features = weight.shape[1]
    rows = out_ref.shape[2] - features
    for index in range(out_ref.shape[0]):
        out_ref[index, :, :features] = weight
        out_ref[index, :, features:] = attended[:, index * rows : (index + 1) * rows]


def block_count(arrays):
    return sum(array.shape[0] for array in arrays) // (2 * HD)


def attention_call(kernel, out_shape, operands, count, width, extra=(), aliases=None):
    specs = [pl.BlockSpec(memory_space=pltpu.VMEM)]
    return pl.pallas_call(
        kernel,
        out_shape=out_shape,
        in_specs=specs * len(operands),
        out_specs=jax.tree.map(lambda _: specs[0], out_shape),
        scratch_shapes=[
            pltpu.VMEM((count * width, 4 * HD), jnp.bfloat16),
            pltpu.VMEM((HD + HD // 2, count * width), jnp.bfloat16),
            *extra,
        ],
        input_output_aliases=aliases or {},
        compiler_params=pltpu.CompilerParams(vmem_limit_bytes=ATTENTION_VMEM),
        cost_estimate=pl.CostEstimate(
            flops=count * width * width * 1200,
            transcendentals=count * width * width,
            bytes_accessed=count * width * 4 * HD,
        ),
    )(*operands)


def near_hops(value):
    return [hop(value, "blk", lambda i, step=step: i ^ step) for step in (2, 4, 12, 8)]


def attention(projected, output_weight, expert_weights, owners):
    width = projected.shape[1]
    keys_values = projected[HD:]
    partner = hop(keys_values, "blk", lambda i: i ^ 1)
    near = near_hops(keys_values)
    total_shape = jax.ShapeDtypeStruct((HD + HD // 2, width), jnp.float32)
    wide_shape = jax.ShapeDtypeStruct((4 * HD, width), jnp.bfloat16)
    wide, total = attention_call(
        lambda *refs: first_keys_kernel(2, *refs),
        (wide_shape, total_shape),
        [projected, partner],
        2,
        width,
    )

    def more(total, group):
        count = block_count(group)
        return attention_call(
            lambda *refs: more_keys_kernel(count, *refs),
            total_shape,
            [wide, total, *group],
            count,
            width,
            aliases={1: 0},
        )

    near, total = lax.optimization_barrier((near, total))
    beyond = hop(jnp.concatenate(near[1:], axis=0), "blk", lambda i: i ^ 2)
    near_partner = hop(jnp.concatenate(near, axis=0), "blk", lambda i: i ^ 1)
    total = more(total, near)
    near_partner, expert_weights, total = lax.optimization_barrier(
        (near_partner, expert_weights, total)
    )
    beside = hop(expert_weights, "blk", lambda i: i ^ 2)
    total = more(total, [near_partner])
    beyond, beside, total = lax.optimization_barrier((beyond, beside, total))
    beyond_partner = hop(beyond, "blk", lambda i: i ^ 1)
    pair = jnp.stack([expert_weights, beside])
    lane = [pair, *[hop(pair, "blk", lambda i, step=step: i ^ step) for step in (4, 8, 12)]]
    total = more(total, [beyond])
    beyond_partner, total = lax.optimization_barrier((beyond_partner, total))
    last = [beyond_partner]
    count = block_count(last)
    features = output_weight.shape[1]
    attended = attention_call(
        lambda *refs: last_keys_kernel(count, len(last), *refs),
        jax.ShapeDtypeStruct((owners, HD, features + width // owners), jnp.bfloat16),
        [wide, total, projected, output_weight, *last, partner, *near, near_partner, beyond],
        count,
        width,
        extra=[pltpu.VMEM(total_shape.shape, jnp.float32)],
    )
    return attended, lane


def add_rows(block, rows):
    return jnp.concatenate([block.reshape(-1, block.shape[-1]), rows], axis=0)


def dot_rows(first, second):
    return lax.dot_general(
        first, second, (((1,), (1,)), ((), ())), preferred_element_type=jnp.float32
    )


def tanh_part(values):
    return jnp.tanh(TANH_SCALE * (values + CUBE * (values * values * values)))


def tile_rows(lane_ref, partner_ref):
    share, width = lane_ref.shape[1:]
    return jnp.concatenate(
        [ref[...].reshape(2 * share, width) for ref in (lane_ref, partner_ref)], axis=0
    )


def weight_specs(weights):
    _, _, _, share, width = weights.shape
    return [
        pl.BlockSpec((None, 2, None, share, width), lambda i, which=which: (i, 0, which, 0, 0))
        for which in (0, 0, 1, 1)
    ]


def expert_forward_kernel(rows_ref, in_lane, in_partner, out_lane, out_partner, result_ref, total):
    step = pl.program_id(0)
    pre_act = dot_rows(rows_ref[...], tile_rows(in_lane, in_partner))
    hidden = (pre_act * (0.5 * (1.0 + tanh_part(pre_act)))).astype(jnp.bfloat16)
    part = jnp.dot(
        hidden, tile_rows(out_lane, out_partner), preferred_element_type=jnp.float32
    )

    @pl.when(step == 0)
    def _():
        total[...] = part

    @pl.when(step > 0)
    def _():
        total[...] += part

    @pl.when(step == pl.num_programs(0) - 1)
    def _():
        result_ref[...] = total[...].astype(result_ref.dtype)


def expert_forward(rows, lane, partner):
    count, width = rows.shape
    hidden = lane.size // width
    return pl.pallas_call(
        expert_forward_kernel,
        grid=(lane.shape[0],),
        out_shape=jax.ShapeDtypeStruct((count, width), jnp.bfloat16),
        in_specs=[pl.BlockSpec((count, width), lambda i: (0, 0)), *weight_specs(lane)],
        out_specs=pl.BlockSpec((count, width), lambda i: (0, 0)),
        scratch_shapes=[pltpu.VMEM((count, width), jnp.float32)],
        compiler_params=pltpu.CompilerParams(vmem_limit_bytes=EXPERT_VMEM),
        cost_estimate=pl.CostEstimate(
            flops=4 * count * width * hidden,
            transcendentals=count * hidden,
            bytes_accessed=4 * hidden * width,
        ),
    )(rows, lane, partner, lane, partner)


def expert_slopes_kernel(
    rows_ref,
    in_lane,
    in_partner,
    out_lane,
    out_partner,
    hidden_ref,
    slope_ref,
    out_weight_ref,
    in_weight_ref,
):
    weight_in = tile_rows(in_lane, in_partner)
    out_weight_ref[...] = tile_rows(out_lane, out_partner)
    in_weight_ref[...] = weight_in.T
    pre_act = dot_rows(weight_in, rows_ref[...])
    tanh = tanh_part(pre_act)
    half = 0.5 * (1.0 + tanh)
    hidden_ref[...] = (pre_act * half).astype(hidden_ref.dtype)
    slope_ref[...] = half + pre_act * (0.5 * (1.0 - tanh * tanh)) * (
        TANH_SCALE * (1.0 + 3.0 * CUBE * (pre_act * pre_act))
    )


def expert_slopes(rows, lane, partner):
    count, width = rows.shape
    hidden = lane.size // width
    tile = hidden // lane.shape[0]
    return pl.pallas_call(
        expert_slopes_kernel,
        grid=(lane.shape[0],),
        out_shape=(
            jax.ShapeDtypeStruct((hidden, count), jnp.bfloat16),
            jax.ShapeDtypeStruct((hidden, count), jnp.float32),
            jax.ShapeDtypeStruct((hidden, width), jnp.bfloat16),
            jax.ShapeDtypeStruct((width, hidden), jnp.bfloat16),
        ),
        in_specs=[pl.BlockSpec((count, width), lambda i: (0, 0)), *weight_specs(lane)],
        out_specs=(
            pl.BlockSpec((tile, count), lambda i: (i, 0)),
            pl.BlockSpec((tile, count), lambda i: (i, 0)),
            pl.BlockSpec((tile, width), lambda i: (i, 0)),
            pl.BlockSpec((width, tile), lambda i: (0, i)),
        ),
        compiler_params=pltpu.CompilerParams(vmem_limit_bytes=EXPERT_VMEM),
        cost_estimate=pl.CostEstimate(
            flops=2 * count * width * hidden,
            transcendentals=count * hidden,
            bytes_accessed=6 * count * hidden + 8 * hidden * width,
        ),
    )(rows, lane, partner, lane, partner)


def store_shares(term, mine_ref, theirs_ref):
    share = mine_ref.shape[2]
    for y in range(2):
        mine_ref[0, y] = term[y * share : (y + 1) * share]
        theirs_ref[0, y] = term[(y + 2) * share : (y + 3) * share].astype(theirs_ref.dtype)


def routed_rows(grads_ref):
    sources, rows, width = grads_ref.shape
    rows = rows - SUM_ROWS
    return grads_ref[:, :rows, :].reshape(sources * rows, width)


def expert_out_grad_kernel(scale, hidden_ref, grads_ref, mine_ref, theirs_ref):
    term = jnp.dot(hidden_ref[...], routed_rows(grads_ref), preferred_element_type=jnp.float32)
    store_shares(term * scale, mine_ref, theirs_ref)


def expert_in_grad_kernel(
    scale,
    slope_ref,
    out_weight_ref,
    rows_ref,
    grads_ref,
    mine_ref,
    theirs_ref,
    pre_grad_ref,
):
    hidden_grad = dot_rows(out_weight_ref[...], routed_rows(grads_ref))
    pre_grad = (hidden_grad * slope_ref[...]).astype(jnp.bfloat16)
    pre_grad_ref[...] = pre_grad
    term = jnp.dot(pre_grad, rows_ref[...], preferred_element_type=jnp.float32)
    store_shares(term * scale, mine_ref, theirs_ref)


def rows_back_kernel(pre_grad_ref, in_weight_ref, back_ref, total):
    step = pl.program_id(0)
    part = jnp.dot(in_weight_ref[...], pre_grad_ref[...], preferred_element_type=jnp.float32)

    @pl.when(step == 0)
    def _():
        total[...] = part

    @pl.when(step > 0)
    def _():
        total[...] += part

    @pl.when(step == pl.num_programs(0) - 1)
    def _():
        back_ref[...] = total[...].T.astype(back_ref.dtype)


def share_shapes(hidden, width):
    shape = (4, 2, hidden // 16, width)
    spec = pl.BlockSpec((1, *shape[1:]), lambda i: (i, 0, 0, 0))
    shapes = (
        jax.ShapeDtypeStruct(shape, jnp.float32),
        jax.ShapeDtypeStruct(shape, jnp.bfloat16),
    )
    return shapes, (spec, spec)


def expert_out_grad(hidden, grads, scale):
    units, count = hidden.shape
    width = grads.shape[2]
    shapes, specs = share_shapes(units, width)
    return pl.pallas_call(
        lambda *refs: expert_out_grad_kernel(scale, *refs),
        grid=(4,),
        out_shape=shapes,
        in_specs=[
            pl.BlockSpec((units // 4, count), lambda i: (i, 0)),
            pl.BlockSpec(grads.shape, lambda i: (0, 0, 0)),
        ],
        out_specs=specs,
        compiler_params=pltpu.CompilerParams(vmem_limit_bytes=EXPERT_VMEM),
        cost_estimate=pl.CostEstimate(
            flops=2 * units * count * width, transcendentals=0, bytes_accessed=2 * units * count
        ),
    )(hidden, grads)


def expert_in_grad(slopes, out_weight, rows, grads, scale):
    units, count = slopes.shape
    width = grads.shape[2]
    shapes, specs = share_shapes(units, width)
    return pl.pallas_call(
        lambda *refs: expert_in_grad_kernel(scale, *refs),
        grid=(4,),
        out_shape=(*shapes, jax.ShapeDtypeStruct((units, count), jnp.bfloat16)),
        in_specs=[
            pl.BlockSpec((units // 4, count), lambda i: (i, 0)),
            pl.BlockSpec((units // 4, width), lambda i: (i, 0)),
            pl.BlockSpec((count, width), lambda i: (0, 0)),
            pl.BlockSpec(grads.shape, lambda i: (0, 0, 0)),
        ],
        out_specs=(*specs, pl.BlockSpec((units // 4, count), lambda i: (i, 0))),
        compiler_params=pltpu.CompilerParams(vmem_limit_bytes=EXPERT_VMEM),
        cost_estimate=pl.CostEstimate(
            flops=4 * units * count * width, transcendentals=0, bytes_accessed=6 * units * count
        ),
    )(slopes, out_weight, rows, grads)


def rows_back(pre_grad, in_weight):
    units, count = pre_grad.shape
    width = in_weight.shape[0]
    return pl.pallas_call(
        rows_back_kernel,
        grid=(4,),
        out_shape=jax.ShapeDtypeStruct((count, width), jnp.bfloat16),
        in_specs=[
            pl.BlockSpec((units // 4, count), lambda i: (i, 0)),
            pl.BlockSpec((width, units // 4), lambda i: (0, i)),
        ],
        out_specs=pl.BlockSpec((count, width), lambda i: (0, 0)),
        scratch_shapes=[pltpu.VMEM((width, count), jnp.float32)],
        compiler_params=pltpu.CompilerParams(vmem_limit_bytes=EXPERT_VMEM),
        cost_estimate=pl.CostEstimate(
            flops=units * count, transcendentals=0, bytes_accessed=count * width
        ),
    )(pre_grad, in_weight)


def swap(block, distance):
    return hop(block.astype(jnp.bfloat16), "blk", lambda i: i ^ distance)


def swap_over_z(blocks):
    return [swap(blocks[d], 4 * d) for d in (1, 2, 3)]


def add_swapped(own, swapped):
    first, second, third = [block.astype(jnp.float32) for block in swapped]
    return own + (first + (second + third))


def local(
    nodes,
    attention_weights,
    output_weight,
    router_weight,
    gain_first,
    gain_second,
    expert_in,
    expert_out,
    routes,
    cotangent,
):
    exp_count = lax.axis_size("exp")
    blk_count = lax.axis_size("blk")
    block_rows = nodes.shape[0]
    width = nodes.shape[1]
    features = attention_weights.shape[1]
    own_rows = block_rows // exp_count
    capacity = 4 * block_rows // (exp_count * exp_count)
    experts = router_weight.shape[0]
    grad_scale = 1.0 / math.sqrt(block_rows * blk_count)
    projected = jnp.einsum(
        "fd,td->ft",
        attention_weights.reshape(3 * features, width),
        nodes,
        preferred_element_type=jnp.float32,
    ).astype(jnp.bfloat16)
    attended, lane_parts = attention(
        projected, output_weight, jnp.concatenate([expert_in, expert_out], axis=0), exp_count
    )
    flat_routes = routes.reshape(2 * own_rows)
    choose = (flat_routes[:, None] == jnp.arange(experts, dtype=jnp.int32)[None, :]).astype(
        jnp.int32
    )
    before = jnp.cumsum(choose, axis=0) - choose
    slot_index = jnp.sum(before * choose, axis=1)
    position = flat_routes * capacity + slot_index
    from_heads = exchange(attended)
    lane = jnp.stack(lane_parts)
    from_heads, lane, position = lax.optimization_barrier((from_heads, lane, position))
    attn_out = jnp.einsum(
        "hfr,hfd->rd",
        from_heads[:, :, width:],
        from_heads[:, :, :width],
        preferred_element_type=jnp.float32,
    )
    own_nodes = lax.dynamic_slice_in_dim(
        nodes, lax.axis_index("exp") * own_rows, own_rows, 0
    ).astype(jnp.float32)
    stream = rms_gain(own_nodes + attn_out, gain_first).astype(jnp.bfloat16)
    lane_partner = hop(lane, "blk", lambda i: i ^ 1)
    logits = jnp.dot(stream, router_weight.T, preferred_element_type=jnp.float32)
    dispatch_table = (
        jnp.arange(experts * capacity, dtype=jnp.int32)[:, None] == position[None, :]
    ).astype(jnp.bfloat16)
    selected = choose.reshape(own_rows, 2, experts).astype(jnp.float32)

    def gate_values(values):
        picked = jnp.sum(jax.nn.sigmoid(values)[:, None, :] * selected, axis=-1)
        return picked / jnp.sum(picked, axis=-1, keepdims=True)

    gates, gate_back = jax.vjp(gate_values, logits)
    repeated = jnp.repeat(stream, 2, axis=0)
    outgoing = jnp.dot(dispatch_table, repeated, preferred_element_type=jnp.float32).astype(
        jnp.bfloat16
    )
    outgoing = outgoing.reshape(experts, capacity, width)
    arrived = exchange(outgoing).reshape(experts * capacity, width)
    result = expert_forward(arrived, lane, lane_partner)
    returned = exchange(result.reshape(experts, capacity, width))
    kept, result = lax.optimization_barrier((arrived, result))
    hidden, slopes, out_weight, in_weight = expert_slopes(kept, lane, lane_partner)
    returned, hidden, slopes = lax.optimization_barrier((returned, hidden, slopes))
    expert_rows = jnp.einsum(
        "ps,pd->sd",
        dispatch_table,
        returned.reshape(experts * capacity, width),
        preferred_element_type=jnp.float32,
    )
    expert_rows = expert_rows.reshape(own_rows, 2, width)
    mixture = gates[:, 0:1] * expert_rows[:, 0] + gates[:, 1:2] * expert_rows[:, 1]
    stream_two = stream.astype(jnp.float32) + mixture
    normed, norm_back = jax.vjp(rms_gain, stream_two, gain_second)
    layer_out = normed.astype(jnp.bfloat16)
    grad_two, gain_part = norm_back(cotangent.astype(jnp.float32))
    gate_grads = jnp.sum(expert_rows * grad_two[:, None, :], axis=-1)
    logit_grad = gate_back(gate_grads)[0]
    router_part = jnp.dot(
        logit_grad.T, stream.astype(jnp.float32), precision=lax.Precision.HIGHEST
    )
    small = jnp.concatenate([router_part, gain_part[None, :]], axis=0) * grad_scale
    sum_rows = jnp.pad(small, ((0, SUM_ROWS - small.shape[0]), (0, 0))).astype(jnp.bfloat16)
    assigned_grads = (
        (gates[..., None] * grad_two[:, None, :]).astype(jnp.bfloat16).reshape(2 * own_rows, width)
    )
    padded = capacity + SUM_ROWS
    place = jnp.arange(experts * padded, dtype=jnp.int32)[:, None]
    row_experts = jnp.concatenate([flat_routes, jnp.full((SUM_ROWS,), -1, jnp.int32)])
    row_slots = jnp.concatenate([slot_index, capacity + jnp.arange(SUM_ROWS, dtype=jnp.int32)])
    anywhere = jnp.logical_or(place // padded == row_experts[None, :], row_experts[None, :] < 0)
    spread = jnp.logical_and(anywhere, place % padded == row_slots[None, :])
    grad_outgoing = jnp.dot(
        spread.astype(jnp.bfloat16),
        jnp.concatenate([assigned_grads, sum_rows], axis=0),
        preferred_element_type=jnp.float32,
    ).astype(jnp.bfloat16)
    grad_arrived = exchange(grad_outgoing.reshape(experts, padded, width))
    out_mine, out_theirs = expert_out_grad(hidden, grad_arrived, grad_scale)
    out_mine, out_theirs, grad_arrived = lax.optimization_barrier(
        (out_mine, out_theirs, grad_arrived)
    )
    sum_rows = jnp.sum(grad_arrived[:, capacity:].astype(jnp.float32), axis=0)
    sum_rows = sum_rows.astype(jnp.bfloat16)
    sums_swapped = swap(sum_rows, 1)
    out_swapped = swap(out_theirs, 1)
    in_mine, in_theirs, pre_grad = expert_in_grad(
        slopes, out_weight, kept, grad_arrived, grad_scale
    )
    in_swapped = swap(in_theirs, 1)
    sums_swapped, out_swapped, in_mine, pre_grad = lax.optimization_barrier(
        (sums_swapped, out_swapped, in_mine, pre_grad)
    )
    sum_rows = (sum_rows.astype(jnp.float32) + sums_swapped.astype(jnp.float32)).astype(
        jnp.bfloat16
    )
    out_sums = out_mine + out_swapped.astype(jnp.float32)
    out_sent = add_rows(out_sums[:, 1].astype(jnp.bfloat16), sum_rows)
    out_beside = swap(out_sent, 2)
    out_sent, out_sums, pre_grad = lax.optimization_barrier((out_sent, out_sums, pre_grad))
    row_grads = rows_back(pre_grad, in_weight)
    in_mine, in_swapped, row_grads = lax.optimization_barrier((in_mine, in_swapped, row_grads))
    back_home = exchange(row_grads.reshape(experts, capacity, width))
    in_sums = in_mine + in_swapped.astype(jnp.float32)
    in_parts = swap_over_z(in_sums)
    out_beside, in_sums = lax.optimization_barrier((out_beside, in_sums))
    sum_rows = (
        out_sent[-SUM_ROWS:].astype(jnp.float32) + out_beside[-SUM_ROWS:].astype(jnp.float32)
    ).astype(jnp.bfloat16)
    out_sums = out_sums[:, 0] + out_beside[:-SUM_ROWS].reshape(out_sums.shape[:1] + out_sums.shape[2:])
    out_parts = [
        swap(add_rows(out_sums[d].astype(jnp.bfloat16), sum_rows), 4 * d) for d in (1, 2, 3)
    ]
    expert_out_grads = add_swapped(out_sums[0], [part[:-SUM_ROWS] for part in out_parts])[None]
    first, second, third = [part[-SUM_ROWS:].astype(jnp.float32) for part in out_parts]
    sums = (sum_rows.astype(jnp.float32) + first) + (second + third)
    router_grad, gain_grad = sums[:experts], sums[experts]
    in_sums = add_swapped(in_sums[0], in_parts)
    in_beside = swap(in_sums[1], 2)
    back_home, in_beside, expert_out_grads = lax.optimization_barrier(
        (back_home, in_beside, expert_out_grads)
    )
    expert_in_grads = (in_sums[0] + in_beside.astype(jnp.float32))[None]
    back_rows = jnp.einsum(
        "ps,pd->sd",
        dispatch_table,
        back_home.reshape(experts * capacity, width),
        preferred_element_type=jnp.float32,
    )
    back_rows = back_rows.reshape(own_rows, 2, width)
    router_term = jnp.dot(
        logit_grad, router_weight.astype(jnp.float32), precision=lax.Precision.HIGHEST
    )
    stream_grad = (grad_two + (back_rows[:, 0] + back_rows[:, 1]) + router_term).astype(
        jnp.bfloat16
    )
    return (layer_out, stream_grad, expert_in_grads, expert_out_grads, router_grad, gain_grad)


def solution(mesh):
    placed = (
        P("blk", None),
        P(None, "exp", None),
        P("exp", None),
        P(),
        P(),
        P(),
        P("exp", "blk", None),
        P("exp", "blk", None),
        P(("blk", "exp"), None),
        P(("blk", "exp"), None),
    )
    return jax.shard_map(
        local,
        mesh=mesh,
        in_specs=placed,
        out_specs=(
            P(("blk", "exp"), None),
            P(("blk", "exp"), None),
            P("exp", "blk", None),
            P("exp", "blk", None),
            P(),
            P(),
        ),
        check_vma=False,
    )
```

```python
import math

import jax
import jax.numpy as jnp
from jax import lax
from jax.experimental import pallas as pl
from jax.experimental.pallas import tpu as pltpu
from jax.sharding import PartitionSpec as P

HD = 32

EPSILON = 1e-06
LOG2_SCALE = math.log2(math.e) / math.sqrt(HD)
SHIFT_KEYS = 256
SUM_LIMIT = 2.0**100
ATTENTION_VMEM = 40 * 2**20
EXPERT_VMEM = 24 * 2**20
SUM_ROWS = 16
TANH_SCALE = math.sqrt(2.0 / math.pi)
CUBE = 0.044715


def rms_gain(stream, gain):
    return stream * lax.rsqrt(jnp.mean(stream * stream, axis=-1, keepdims=True) + EPSILON) * gain


def exchange(buffer):
    return lax.all_to_all(buffer, "exp", split_axis=0, concat_axis=0, tiled=True)


def hop(value, axis, target):
    count = lax.axis_size(axis)
    return lax.ppermute(value, axis, [(i, target(i) % count) for i in range(count)])


def split_terms(value, terms):
    pieces = []
    for _ in range(terms):
        piece = value.astype(jnp.bfloat16)
        pieces.append(piece)
        value = value - piece.astype(jnp.float32)
    return pieces


def key_blocks(refs):
    return [
        (ref, start) for ref in refs for start in range(0, ref.shape[0], 2 * HD)
    ]


def own_blocks(own_ref):
    return [(own_ref, HD)]


def load_keys(blocks, keys, values):
    width = blocks[0][0].shape[1]
    ones = (lax.broadcasted_iota(jnp.int32, (HD, width), 0) < 3).astype(jnp.bfloat16)
    one = (lax.broadcasted_iota(jnp.int32, (HD // 2, width), 0) < 1).astype(jnp.bfloat16)
    for index, (ref, start) in enumerate(blocks):
        block = ref[start : start + HD, :]
        span = slice(index * width, (index + 1) * width)
        keys[span, :] = jnp.concatenate([block, block, block, ones], axis=0).T
        values[:, span] = jnp.concatenate([ref[start + HD : start + 2 * HD, :], one], axis=0)


def add_blocks(count, width, query, keys, values, total):
    chunk = width // 2

    def step(index, running):
        span = pl.ds(pl.multiple_of(index * chunk, chunk), chunk)
        exponents = jnp.dot(keys[span, :], query, preferred_element_type=jnp.float32)
        weights = jnp.exp2(exponents).astype(jnp.bfloat16)
        return running + jnp.dot(values[:, span], weights, preferred_element_type=jnp.float32)

    return lax.fori_loop(0, 2 * count, step, total)


def first_keys_kernel(count, own_ref, *refs):
    blocks, (wide_ref, total_ref, keys, values) = refs[:-4], refs[-4:]
    load_keys(own_blocks(own_ref) + key_blocks(blocks), keys, values)
    width = own_ref.shape[1]
    scaled = own_ref[:HD, :].astype(jnp.float32) * LOG2_SCALE
    pieces = split_terms(scaled, 3)
    wide_ref[...] = jnp.concatenate(pieces + [jnp.zeros_like(pieces[0])], axis=0)
    some = jnp.dot(keys[:SHIFT_KEYS, :], wide_ref[...], preferred_element_type=jnp.float32)
    shift = split_terms(-jnp.max(some, axis=0, keepdims=True), 3)
    row = lax.broadcasted_iota(jnp.int32, (HD, width), 0)
    rows = jnp.zeros((HD, width), jnp.float32)
    for index, piece in enumerate(shift):
        rows = jnp.where(row == index, piece.astype(jnp.float32), rows)
    wide_ref[3 * HD :, :] = rows.astype(jnp.bfloat16)
    total_ref[...] = add_blocks(
        count, width, wide_ref[...], keys, values, jnp.zeros(total_ref.shape, jnp.float32)
    )


def more_keys_kernel(count, wide_ref, before_ref, *refs):
    blocks, (total_ref, keys, values) = refs[:-3], refs[-3:]
    load_keys(key_blocks(blocks), keys, values)
    total_ref[...] = add_blocks(
        count, wide_ref.shape[1], wide_ref[...], keys, values, before_ref[...]
    )


def last_keys_kernel(count, fresh, wide_ref, before_ref, own_ref, output_weight_ref, *refs):
    blocks, (out_ref, keys, values, total) = refs[:-4], refs[-4:]
    load_keys(key_blocks(blocks[:fresh]), keys, values)
    width = wide_ref.shape[1]
    total[...] = add_blocks(count, width, wide_ref[...], keys, values, before_ref[...])
    sums = total[HD : HD + 1, :]
    inside = jnp.logical_and(sums <= SUM_LIMIT, sums >= 1.0 / SUM_LIMIT)
    outside = jnp.sum(jnp.where(inside, 0, 1))

    @pl.when(outside > 0)
    def _():
        query = own_ref[:HD, :]
        query = jnp.concatenate([query, jnp.zeros((3 * HD, width), query.dtype)], axis=0)
        total[...] = jnp.zeros(total.shape, jnp.float32)

        def step(index, top):
            span = pl.ds(pl.multiple_of(index * SHIFT_KEYS, SHIFT_KEYS), SHIFT_KEYS)
            scores = LOG2_SCALE * jnp.dot(
                keys[span, :], query, preferred_element_type=jnp.float32
            )
            new_top = jnp.maximum(top, jnp.max(scores, axis=0, keepdims=True))
            weights = jnp.exp2(scores - new_top).astype(jnp.bfloat16)
            total[...] = total[...] * jnp.exp2(top - new_top) + jnp.dot(
                values[:, span], weights, preferred_element_type=jnp.float32
            )
            return new_top

        top = jnp.full((1, width), -1e30, jnp.float32)
        every = own_blocks(own_ref) + key_blocks(blocks)
        for group in [every[i : i + count] for i in range(0, len(every), count)]:
            load_keys(group, keys, values)
            top = lax.fori_loop(0, len(group) * (width // SHIFT_KEYS), step, top)

    attended = (total[:HD, :] / total[HD : HD + 1, :]).astype(jnp.bfloat16)
    weight = output_weight_ref[...]
    features = weight.shape[1]
    rows = out_ref.shape[2] - features
    for index in range(out_ref.shape[0]):
        out_ref[index, :, :features] = weight
        out_ref[index, :, features:] = attended[:, index * rows : (index + 1) * rows]


def block_count(arrays):
    return sum(array.shape[0] for array in arrays) // (2 * HD)


def attention_call(kernel, out_shape, operands, count, width, extra=(), aliases=None):
    specs = [pl.BlockSpec(memory_space=pltpu.VMEM)]
    return pl.pallas_call(
        kernel,
        out_shape=out_shape,
        in_specs=specs * len(operands),
        out_specs=jax.tree.map(lambda _: specs[0], out_shape),
        scratch_shapes=[
            pltpu.VMEM((count * width, 4 * HD), jnp.bfloat16),
            pltpu.VMEM((HD + HD // 2, count * width), jnp.bfloat16),
            *extra,
        ],
        input_output_aliases=aliases or {},
        compiler_params=pltpu.CompilerParams(vmem_limit_bytes=ATTENTION_VMEM),
        cost_estimate=pl.CostEstimate(
            flops=count * width * width * 1200,
            transcendentals=count * width * width,
            bytes_accessed=count * width * 4 * HD,
        ),
    )(*operands)


def near_hops(value):
    return [hop(value, "blk", lambda i, step=step: i ^ step) for step in (8, 12, 4, 2)]


def attention(projected, output_weight, expert_weights, owners):
    width = projected.shape[1]
    keys_values = projected[HD:]
    partner = hop(keys_values, "blk", lambda i: i ^ 1)
    near = near_hops(keys_values)
    total_shape = jax.ShapeDtypeStruct((HD + HD // 2, width), jnp.float32)
    wide_shape = jax.ShapeDtypeStruct((4 * HD, width), jnp.bfloat16)
    wide, total = attention_call(
        lambda *refs: first_keys_kernel(2, *refs),
        (wide_shape, total_shape),
        [projected, partner],
        2,
        width,
    )

    def more(total, group):
        count = block_count(group)
        return attention_call(
            lambda *refs: more_keys_kernel(count, *refs),
            total_shape,
            [wide, total, *group],
            count,
            width,
            aliases={1: 0},
        )

    near, total = lax.optimization_barrier((near, total))
    beyond = hop(jnp.concatenate(near[:3], axis=0), "blk", lambda i: i ^ 2)
    near_partner = hop(jnp.concatenate(near, axis=0), "blk", lambda i: i ^ 1)
    total = more(total, near)
    near_partner, expert_weights, total = lax.optimization_barrier(
        (near_partner, expert_weights, total)
    )
    beside = hop(expert_weights, "blk", lambda i: i ^ 2)
    total = more(total, [near_partner])
    beyond, beside, total = lax.optimization_barrier((beyond, beside, total))
    beyond_partner = hop(beyond, "blk", lambda i: i ^ 1)
    pair = jnp.stack([expert_weights, beside])
    lane = [pair, *[hop(pair, "blk", lambda i, step=step: i ^ step) for step in (4, 8, 12)]]
    total = more(total, [beyond])
    beyond_partner, total = lax.optimization_barrier((beyond_partner, total))
    last = [beyond_partner]
    count = block_count(last)
    features = output_weight.shape[1]
    attended = attention_call(
        lambda *refs: last_keys_kernel(count, len(last), *refs),
        jax.ShapeDtypeStruct((owners, HD, features + width // owners), jnp.bfloat16),
        [wide, total, projected, output_weight, *last, partner, *near, near_partner, beyond],
        count,
        width,
        extra=[pltpu.VMEM(total_shape.shape, jnp.float32)],
    )
    return attended, lane


def add_rows(block, rows):
    return jnp.concatenate([block.reshape(-1, block.shape[-1]), rows], axis=0)


def dot_rows(first, second):
    return lax.dot_general(
        first, second, (((1,), (1,)), ((), ())), preferred_element_type=jnp.float32
    )


def tanh_part(values):
    return jnp.tanh(TANH_SCALE * (values + CUBE * (values * values * values)))


def tile_rows(lane_ref, partner_ref):
    share, width = lane_ref.shape[1:]
    return jnp.concatenate(
        [ref[...].reshape(2 * share, width) for ref in (lane_ref, partner_ref)], axis=0
    )


def weight_specs(weights):
    _, _, _, share, width = weights.shape
    return [
        pl.BlockSpec((None, 2, None, share, width), lambda i, which=which: (i, 0, which, 0, 0))
        for which in (0, 0, 1, 1)
    ]


def expert_forward_kernel(rows_ref, lane_ref, partner_ref, result_ref):
    rows = rows_ref[...]
    total = jnp.zeros(result_ref.shape, jnp.float32)
    for step in range(lane_ref.shape[0]):
        weights = [
            tile_rows(lane_ref.at[step, :, which], partner_ref.at[step, :, which])
            for which in range(2)
        ]
        pre_act = dot_rows(rows, weights[0])
        hidden = (pre_act * (0.5 * (1.0 + tanh_part(pre_act)))).astype(jnp.bfloat16)
        total += jnp.dot(hidden, weights[1], preferred_element_type=jnp.float32)
    result_ref[...] = total.astype(result_ref.dtype)


def expert_forward(rows, lane, partner):
    count, width = rows.shape
    hidden = lane.size // width
    return pl.pallas_call(
        expert_forward_kernel,
        out_shape=jax.ShapeDtypeStruct((count, width), jnp.bfloat16),
        in_specs=[pl.BlockSpec(memory_space=pltpu.VMEM)] * 3,
        out_specs=pl.BlockSpec(memory_space=pltpu.VMEM),
        compiler_params=pltpu.CompilerParams(vmem_limit_bytes=EXPERT_VMEM),
        cost_estimate=pl.CostEstimate(
            flops=4 * count * width * hidden,
            transcendentals=count * hidden,
            bytes_accessed=4 * hidden * width,
        ),
    )(rows, lane, partner)


def expert_slopes_kernel(
    rows_ref,
    in_lane,
    in_partner,
    out_lane,
    out_partner,
    hidden_ref,
    slope_ref,
    out_weight_ref,
    in_weight_ref,
):
    weight_in = tile_rows(in_lane, in_partner)
    out_weight_ref[...] = tile_rows(out_lane, out_partner)
    in_weight_ref[...] = weight_in.T
    pre_act = dot_rows(weight_in, rows_ref[...])
    tanh = tanh_part(pre_act)
    half = 0.5 * (1.0 + tanh)
    hidden_ref[...] = (pre_act * half).astype(hidden_ref.dtype)
    slope = half + pre_act * (0.5 * (1.0 - tanh * tanh)) * (
        TANH_SCALE * (1.0 + 3.0 * CUBE * (pre_act * pre_act))
    )
    slope_ref[...] = slope.astype(slope_ref.dtype)


def expert_slopes(rows, lane, partner):
    count, width = rows.shape
    hidden = lane.size // width
    tile = hidden // lane.shape[0]
    return pl.pallas_call(
        expert_slopes_kernel,
        grid=(lane.shape[0],),
        out_shape=(
            jax.ShapeDtypeStruct((hidden, count), jnp.bfloat16),
            jax.ShapeDtypeStruct((hidden, count), jnp.bfloat16),
            jax.ShapeDtypeStruct((hidden, width), jnp.bfloat16),
            jax.ShapeDtypeStruct((width, hidden), jnp.bfloat16),
        ),
        in_specs=[pl.BlockSpec((count, width), lambda i: (0, 0)), *weight_specs(lane)],
        out_specs=(
            pl.BlockSpec((tile, count), lambda i: (i, 0)),
            pl.BlockSpec((tile, count), lambda i: (i, 0)),
            pl.BlockSpec((tile, width), lambda i: (i, 0)),
            pl.BlockSpec((width, tile), lambda i: (0, i)),
        ),
        compiler_params=pltpu.CompilerParams(vmem_limit_bytes=EXPERT_VMEM),
        cost_estimate=pl.CostEstimate(
            flops=2 * count * width * hidden,
            transcendentals=count * hidden,
            bytes_accessed=6 * count * hidden + 8 * hidden * width,
        ),
    )(rows, lane, partner, lane, partner)


def store_shares(term, mine_ref, theirs_ref):
    share = mine_ref.shape[2]
    for y in range(2):
        mine_ref[0, y] = term[y * share : (y + 1) * share]
        theirs_ref[0, y] = term[(y + 2) * share : (y + 3) * share].astype(theirs_ref.dtype)


def routed_rows(grads_ref):
    sources, rows, width = grads_ref.shape
    rows = rows - SUM_ROWS
    return grads_ref[:, :rows, :].reshape(sources * rows, width)


def expert_out_grad_kernel(scale, hidden_ref, grads_ref, mine_ref, theirs_ref):
    term = jnp.dot(hidden_ref[...], routed_rows(grads_ref), preferred_element_type=jnp.float32)
    store_shares(term * scale, mine_ref, theirs_ref)


def expert_in_grad_kernel(
    scale,
    slope_ref,
    out_weight_ref,
    rows_ref,
    grads_ref,
    mine_ref,
    theirs_ref,
    pre_grad_ref,
):
    hidden_grad = dot_rows(out_weight_ref[...], routed_rows(grads_ref))
    pre_grad = (hidden_grad * slope_ref[...].astype(jnp.float32)).astype(jnp.bfloat16)
    pre_grad_ref[...] = pre_grad
    term = jnp.dot(pre_grad, rows_ref[...], preferred_element_type=jnp.float32)
    store_shares(term * scale, mine_ref, theirs_ref)


def rows_back_kernel(pre_grad_ref, in_weight_ref, back_ref):
    total = jnp.dot(in_weight_ref[...], pre_grad_ref[...], preferred_element_type=jnp.float32)
    back_ref[...] = total.T.astype(back_ref.dtype)


def share_shapes(hidden, width):
    shape = (4, 2, hidden // 16, width)
    spec = pl.BlockSpec((1, *shape[1:]), lambda i: (i, 0, 0, 0))
    shapes = (
        jax.ShapeDtypeStruct(shape, jnp.float32),
        jax.ShapeDtypeStruct(shape, jnp.bfloat16),
    )
    return shapes, (spec, spec)


def expert_out_grad(hidden, grads, scale):
    units, count = hidden.shape
    width = grads.shape[2]
    shapes, specs = share_shapes(units, width)
    return pl.pallas_call(
        lambda *refs: expert_out_grad_kernel(scale, *refs),
        grid=(4,),
        out_shape=shapes,
        in_specs=[
            pl.BlockSpec((units // 4, count), lambda i: (i, 0)),
            pl.BlockSpec(grads.shape, lambda i: (0, 0, 0)),
        ],
        out_specs=specs,
        compiler_params=pltpu.CompilerParams(vmem_limit_bytes=EXPERT_VMEM),
        cost_estimate=pl.CostEstimate(
            flops=2 * units * count * width, transcendentals=0, bytes_accessed=2 * units * count
        ),
    )(hidden, grads)


def expert_in_grad(slopes, out_weight, rows, grads, scale):
    units, count = slopes.shape
    width = grads.shape[2]
    shapes, specs = share_shapes(units, width)
    return pl.pallas_call(
        lambda *refs: expert_in_grad_kernel(scale, *refs),
        grid=(4,),
        out_shape=(*shapes, jax.ShapeDtypeStruct((units, count), jnp.bfloat16)),
        in_specs=[
            pl.BlockSpec((units // 4, count), lambda i: (i, 0)),
            pl.BlockSpec((units // 4, width), lambda i: (i, 0)),
            pl.BlockSpec((count, width), lambda i: (0, 0)),
            pl.BlockSpec(grads.shape, lambda i: (0, 0, 0)),
        ],
        out_specs=(*specs, pl.BlockSpec((units // 4, count), lambda i: (i, 0))),
        compiler_params=pltpu.CompilerParams(vmem_limit_bytes=EXPERT_VMEM),
        cost_estimate=pl.CostEstimate(
            flops=4 * units * count * width, transcendentals=0, bytes_accessed=6 * units * count
        ),
    )(slopes, out_weight, rows, grads)


def rows_back(pre_grad, in_weight):
    units, count = pre_grad.shape
    width = in_weight.shape[0]
    return pl.pallas_call(
        rows_back_kernel,
        out_shape=jax.ShapeDtypeStruct((count, width), jnp.bfloat16),
        in_specs=[pl.BlockSpec(memory_space=pltpu.VMEM)] * 2,
        out_specs=pl.BlockSpec(memory_space=pltpu.VMEM),
        compiler_params=pltpu.CompilerParams(vmem_limit_bytes=EXPERT_VMEM),
        cost_estimate=pl.CostEstimate(
            flops=units * count, transcendentals=0, bytes_accessed=count * width
        ),
    )(pre_grad, in_weight)


def swap(block, distance):
    return hop(block.astype(jnp.bfloat16), "blk", lambda i: i ^ distance)


def swap_over_z(blocks):
    return [swap(blocks[d], 4 * d) for d in (1, 2, 3)]


def add_swapped(own, swapped):
    first, second, third = [block.astype(jnp.float32) for block in swapped]
    return own + (first + (second + third))


def local(
    nodes,
    attention_weights,
    output_weight,
    router_weight,
    gain_first,
    gain_second,
    expert_in,
    expert_out,
    routes,
    cotangent,
):
    exp_count = lax.axis_size("exp")
    blk_count = lax.axis_size("blk")
    block_rows = nodes.shape[0]
    width = nodes.shape[1]
    features = attention_weights.shape[1]
    own_rows = block_rows // exp_count
    capacity = 4 * block_rows // (exp_count * exp_count)
    experts = router_weight.shape[0]
    grad_scale = 1.0 / math.sqrt(block_rows * blk_count)
    projected = jnp.einsum(
        "fd,td->ft",
        attention_weights.reshape(3 * features, width),
        nodes,
        preferred_element_type=jnp.float32,
    ).astype(jnp.bfloat16)
    attended, lane_parts = attention(
        projected, output_weight, jnp.concatenate([expert_in, expert_out], axis=0), exp_count
    )
    flat_routes = routes.reshape(2 * own_rows)
    choose = (flat_routes[:, None] == jnp.arange(experts, dtype=jnp.int32)[None, :]).astype(
        jnp.int32
    )
    before = jnp.cumsum(choose, axis=0) - choose
    slot_index = jnp.sum(before * choose, axis=1)
    position = flat_routes * capacity + slot_index
    from_heads = exchange(attended)
    lane = jnp.stack(lane_parts)
    from_heads, lane, position = lax.optimization_barrier((from_heads, lane, position))
    attn_out = jnp.einsum(
        "hfr,hfd->rd",
        from_heads[:, :, width:],
        from_heads[:, :, :width],
        preferred_element_type=jnp.float32,
    )
    own_nodes = lax.dynamic_slice_in_dim(
        nodes, lax.axis_index("exp") * own_rows, own_rows, 0
    ).astype(jnp.float32)
    stream = rms_gain(own_nodes + attn_out, gain_first).astype(jnp.bfloat16)
    lane_partner = hop(lane, "blk", lambda i: i ^ 1)
    logits = jnp.dot(stream, router_weight.T, preferred_element_type=jnp.float32)
    dispatch_table = (
        jnp.arange(experts * capacity, dtype=jnp.int32)[:, None] == position[None, :]
    ).astype(jnp.bfloat16)
    selected = choose.reshape(own_rows, 2, experts).astype(jnp.float32)

    def gate_values(values):
        picked = jnp.sum(jax.nn.sigmoid(values)[:, None, :] * selected, axis=-1)
        return picked / jnp.sum(picked, axis=-1, keepdims=True)

    gates, gate_back = jax.vjp(gate_values, logits)
    repeated = jnp.repeat(stream, 2, axis=0)
    outgoing = jnp.dot(dispatch_table, repeated, preferred_element_type=jnp.float32).astype(
        jnp.bfloat16
    )
    outgoing = outgoing.reshape(experts, capacity, width)
    arrived = exchange(outgoing).reshape(experts * capacity, width)
    result = expert_forward(arrived, lane, lane_partner)
    returned = exchange(result.reshape(experts, capacity, width))
    kept, result = lax.optimization_barrier((arrived, result))
    hidden, slopes, out_weight, in_weight = expert_slopes(kept, lane, lane_partner)
    returned, hidden, slopes = lax.optimization_barrier((returned, hidden, slopes))
    expert_rows = jnp.einsum(
        "ps,pd->sd",
        dispatch_table,
        returned.reshape(experts * capacity, width),
        preferred_element_type=jnp.float32,
    )
    expert_rows = expert_rows.reshape(own_rows, 2, width)
    mixture = gates[:, 0:1] * expert_rows[:, 0] + gates[:, 1:2] * expert_rows[:, 1]
    stream_two = stream.astype(jnp.float32) + mixture
    normed, norm_back = jax.vjp(rms_gain, stream_two, gain_second)
    layer_out = normed.astype(jnp.bfloat16)
    grad_two, gain_part = norm_back(cotangent.astype(jnp.float32))
    gate_grads = jnp.sum(expert_rows * grad_two[:, None, :], axis=-1)
    logit_grad = gate_back(gate_grads)[0]
    router_part = jnp.dot(
        logit_grad.T, stream.astype(jnp.float32), precision=lax.Precision.HIGHEST
    )
    small = jnp.concatenate([router_part, gain_part[None, :]], axis=0) * grad_scale
    sum_rows = jnp.pad(small, ((0, SUM_ROWS - small.shape[0]), (0, 0))).astype(jnp.bfloat16)
    assigned_grads = (
        (gates[..., None] * grad_two[:, None, :]).astype(jnp.bfloat16).reshape(2 * own_rows, width)
    )
    padded = capacity + SUM_ROWS
    place = jnp.arange(experts * padded, dtype=jnp.int32)[:, None]
    row_experts = jnp.concatenate([flat_routes, jnp.full((SUM_ROWS,), -1, jnp.int32)])
    row_slots = jnp.concatenate([slot_index, capacity + jnp.arange(SUM_ROWS, dtype=jnp.int32)])
    anywhere = jnp.logical_or(place // padded == row_experts[None, :], row_experts[None, :] < 0)
    spread = jnp.logical_and(anywhere, place % padded == row_slots[None, :])
    grad_outgoing = jnp.dot(
        spread.astype(jnp.bfloat16),
        jnp.concatenate([assigned_grads, sum_rows], axis=0),
        preferred_element_type=jnp.float32,
    ).astype(jnp.bfloat16)
    grad_arrived = exchange(grad_outgoing.reshape(experts, padded, width))
    out_mine, out_theirs = expert_out_grad(hidden, grad_arrived, grad_scale)
    out_mine, out_theirs, grad_arrived = lax.optimization_barrier(
        (out_mine, out_theirs, grad_arrived)
    )
    sum_rows = jnp.sum(grad_arrived[:, capacity:].astype(jnp.float32), axis=0)
    sum_rows = sum_rows.astype(jnp.bfloat16)
    sums_swapped = swap(sum_rows, 1)
    out_swapped = swap(out_theirs, 1)
    in_mine, in_theirs, pre_grad = expert_in_grad(
        slopes, out_weight, kept, grad_arrived, grad_scale
    )
    in_swapped = swap(in_theirs, 1)
    sums_swapped, out_swapped, in_mine, pre_grad = lax.optimization_barrier(
        (sums_swapped, out_swapped, in_mine, pre_grad)
    )
    sum_rows = (sum_rows.astype(jnp.float32) + sums_swapped.astype(jnp.float32)).astype(
        jnp.bfloat16
    )
    out_sums = out_mine + out_swapped.astype(jnp.float32)
    out_sent = add_rows(out_sums[:, 1].astype(jnp.bfloat16), sum_rows)
    out_beside = swap(out_sent, 2)
    out_sent, out_sums, pre_grad = lax.optimization_barrier((out_sent, out_sums, pre_grad))
    row_grads = rows_back(pre_grad, in_weight)
    in_mine, in_swapped, row_grads = lax.optimization_barrier((in_mine, in_swapped, row_grads))
    back_home = exchange(row_grads.reshape(experts, capacity, width))
    in_sums = in_mine + in_swapped.astype(jnp.float32)
    in_parts = swap_over_z(in_sums)
    out_beside, in_sums = lax.optimization_barrier((out_beside, in_sums))
    sum_rows = (
        out_sent[-SUM_ROWS:].astype(jnp.float32) + out_beside[-SUM_ROWS:].astype(jnp.float32)
    ).astype(jnp.bfloat16)
    out_sums = out_sums[:, 0] + out_beside[:-SUM_ROWS].reshape(out_sums.shape[:1] + out_sums.shape[2:])
    out_parts = [
        swap(add_rows(out_sums[d].astype(jnp.bfloat16), sum_rows), 4 * d) for d in (1, 2, 3)
    ]
    expert_out_grads = add_swapped(out_sums[0], [part[:-SUM_ROWS] for part in out_parts])[None]
    first, second, third = [part[-SUM_ROWS:].astype(jnp.float32) for part in out_parts]
    sums = (sum_rows.astype(jnp.float32) + first) + (second + third)
    router_grad, gain_grad = sums[:experts], sums[experts]
    in_sums = add_swapped(in_sums[0], in_parts)
    in_beside = swap(in_sums[1], 2)
    back_home, in_beside, expert_out_grads = lax.optimization_barrier(
        (back_home, in_beside, expert_out_grads)
    )
    expert_in_grads = (in_sums[0] + in_beside.astype(jnp.float32))[None]
    back_rows = jnp.einsum(
        "ps,pd->sd",
        dispatch_table,
        back_home.reshape(experts * capacity, width),
        preferred_element_type=jnp.float32,
    )
    back_rows = back_rows.reshape(own_rows, 2, width)
    router_term = jnp.dot(
        logit_grad, router_weight.astype(jnp.float32), precision=lax.Precision.HIGHEST
    )
    stream_grad = (grad_two + (back_rows[:, 0] + back_rows[:, 1]) + router_term).astype(
        jnp.bfloat16
    )
    return (layer_out, stream_grad, expert_in_grads, expert_out_grads, router_grad, gain_grad)


def solution(mesh):
    placed = (
        P("blk", None),
        P(None, "exp", None),
        P("exp", None),
        P(),
        P(),
        P(),
        P("exp", "blk", None),
        P("exp", "blk", None),
        P(("blk", "exp"), None),
        P(("blk", "exp"), None),
    )
    return jax.shard_map(
        local,
        mesh=mesh,
        in_specs=placed,
        out_specs=(
            P(("blk", "exp"), None),
            P(("blk", "exp"), None),
            P("exp", "blk", None),
            P("exp", "blk", None),
            P(),
            P(),
        ),
        check_vma=False,
    )
```

```python
import math

import jax
import jax.numpy as jnp
from jax import lax
from jax.experimental import pallas as pl
from jax.experimental.pallas import tpu as pltpu
from jax.sharding import PartitionSpec as P

HD = 32

EPSILON = 1e-06
LOG2_SCALE = math.log2(math.e) / math.sqrt(HD)
SHIFT_KEYS = 256
SUM_LIMIT = 2.0**100
ATTENTION_VMEM = 40 * 2**20
EXPERT_VMEM = 24 * 2**20
SUM_ROWS = 16
TANH_SCALE = math.sqrt(2.0 / math.pi)
CUBE = 0.044715


def rms_gain(stream, gain):
    return stream * lax.rsqrt(jnp.mean(stream * stream, axis=-1, keepdims=True) + EPSILON) * gain


def exchange(buffer):
    return lax.all_to_all(buffer, "exp", split_axis=0, concat_axis=0, tiled=True)


def hop(value, axis, target):
    count = lax.axis_size(axis)
    return lax.ppermute(value, axis, [(i, target(i) % count) for i in range(count)])


def split_terms(value, terms):
    pieces = []
    for _ in range(terms):
        piece = value.astype(jnp.bfloat16)
        pieces.append(piece)
        value = value - piece.astype(jnp.float32)
    return pieces


def key_blocks(refs):
    return [
        (ref, start) for ref in refs for start in range(0, ref.shape[0], 2 * HD)
    ]


def own_blocks(own_ref):
    return [(own_ref, HD)]


def load_keys(blocks, keys, values):
    width = blocks[0][0].shape[1]
    ones = (lax.broadcasted_iota(jnp.int32, (HD, width), 0) < 3).astype(jnp.bfloat16)
    one = (lax.broadcasted_iota(jnp.int32, (HD // 2, width), 0) < 1).astype(jnp.bfloat16)
    for index, (ref, start) in enumerate(blocks):
        block = ref[start : start + HD, :]
        span = slice(index * width, (index + 1) * width)
        keys[span, :] = jnp.concatenate([block, block, block, ones], axis=0).T
        values[:, span] = jnp.concatenate([ref[start + HD : start + 2 * HD, :], one], axis=0)


def add_blocks(count, width, query, keys, values, total):
    chunk = width // 2

    def step(index, running):
        span = pl.ds(pl.multiple_of(index * chunk, chunk), chunk)
        exponents = jnp.dot(keys[span, :], query, preferred_element_type=jnp.float32)
        weights = jnp.exp2(exponents).astype(jnp.bfloat16)
        return running + jnp.dot(values[:, span], weights, preferred_element_type=jnp.float32)

    return lax.fori_loop(0, 2 * count, step, total)


def first_keys_kernel(count, own_ref, *refs):
    blocks, (wide_ref, total_ref, keys, values) = refs[:-4], refs[-4:]
    load_keys(own_blocks(own_ref) + key_blocks(blocks), keys, values)
    width = own_ref.shape[1]
    scaled = own_ref[:HD, :].astype(jnp.float32) * LOG2_SCALE
    pieces = split_terms(scaled, 3)
    wide_ref[...] = jnp.concatenate(pieces + [jnp.zeros_like(pieces[0])], axis=0)
    some = jnp.dot(keys[:SHIFT_KEYS, :], wide_ref[...], preferred_element_type=jnp.float32)
    shift = split_terms(-jnp.max(some, axis=0, keepdims=True), 3)
    row = lax.broadcasted_iota(jnp.int32, (HD, width), 0)
    rows = jnp.zeros((HD, width), jnp.float32)
    for index, piece in enumerate(shift):
        rows = jnp.where(row == index, piece.astype(jnp.float32), rows)
    wide_ref[3 * HD :, :] = rows.astype(jnp.bfloat16)
    total_ref[...] = add_blocks(
        count, width, wide_ref[...], keys, values, jnp.zeros(total_ref.shape, jnp.float32)
    )


def more_keys_kernel(count, wide_ref, before_ref, *refs):
    blocks, (total_ref, keys, values) = refs[:-3], refs[-3:]
    load_keys(key_blocks(blocks), keys, values)
    total_ref[...] = add_blocks(
        count, wide_ref.shape[1], wide_ref[...], keys, values, before_ref[...]
    )


def last_keys_kernel(count, fresh, wide_ref, before_ref, own_ref, output_weight_ref, *refs):
    blocks, (out_ref, keys, values, total) = refs[:-4], refs[-4:]
    load_keys(key_blocks(blocks[:fresh]), keys, values)
    width = wide_ref.shape[1]
    total[...] = add_blocks(count, width, wide_ref[...], keys, values, before_ref[...])
    sums = total[HD : HD + 1, :]
    inside = jnp.logical_and(sums <= SUM_LIMIT, sums >= 1.0 / SUM_LIMIT)
    outside = jnp.sum(jnp.where(inside, 0, 1))

    @pl.when(outside > 0)
    def _():
        query = own_ref[:HD, :]
        query = jnp.concatenate([query, jnp.zeros((3 * HD, width), query.dtype)], axis=0)
        total[...] = jnp.zeros(total.shape, jnp.float32)

        def step(index, top):
            span = pl.ds(pl.multiple_of(index * SHIFT_KEYS, SHIFT_KEYS), SHIFT_KEYS)
            scores = LOG2_SCALE * jnp.dot(
                keys[span, :], query, preferred_element_type=jnp.float32
            )
            new_top = jnp.maximum(top, jnp.max(scores, axis=0, keepdims=True))
            weights = jnp.exp2(scores - new_top).astype(jnp.bfloat16)
            total[...] = total[...] * jnp.exp2(top - new_top) + jnp.dot(
                values[:, span], weights, preferred_element_type=jnp.float32
            )
            return new_top

        top = jnp.full((1, width), -1e30, jnp.float32)
        every = own_blocks(own_ref) + key_blocks(blocks)
        for group in [every[i : i + count] for i in range(0, len(every), count)]:
            load_keys(group, keys, values)
            top = lax.fori_loop(0, len(group) * (width // SHIFT_KEYS), step, top)

    attended = (total[:HD, :] / total[HD : HD + 1, :]).astype(jnp.bfloat16)
    weight = output_weight_ref[...]
    features = weight.shape[1]
    rows = out_ref.shape[2] - features
    for index in range(out_ref.shape[0]):
        out_ref[index, :, :features] = weight
        out_ref[index, :, features:] = attended[:, index * rows : (index + 1) * rows]


def block_count(arrays):
    return sum(array.shape[0] for array in arrays) // (2 * HD)


def attention_call(kernel, out_shape, operands, count, width, extra=(), aliases=None):
    specs = [pl.BlockSpec(memory_space=pltpu.VMEM)]
    return pl.pallas_call(
        kernel,
        out_shape=out_shape,
        in_specs=specs * len(operands),
        out_specs=jax.tree.map(lambda _: specs[0], out_shape),
        scratch_shapes=[
            pltpu.VMEM((count * width, 4 * HD), jnp.bfloat16),
            pltpu.VMEM((HD + HD // 2, count * width), jnp.bfloat16),
            *extra,
        ],
        input_output_aliases=aliases or {},
        compiler_params=pltpu.CompilerParams(vmem_limit_bytes=ATTENTION_VMEM),
        cost_estimate=pl.CostEstimate(
            flops=count * width * width * 1200,
            transcendentals=count * width * width,
            bytes_accessed=count * width * 4 * HD,
        ),
    )(*operands)


def near_hops(value):
    return [hop(value, "blk", lambda i, step=step: i ^ step) for step in (8, 12, 4, 2)]


def attention(projected, output_weight, expert_weights, owners):
    width = projected.shape[1]
    keys_values = projected[HD:]
    partner = hop(keys_values, "blk", lambda i: i ^ 1)
    near = near_hops(keys_values)
    total_shape = jax.ShapeDtypeStruct((HD + HD // 2, width), jnp.float32)
    wide_shape = jax.ShapeDtypeStruct((4 * HD, width), jnp.bfloat16)
    wide, total = attention_call(
        lambda *refs: first_keys_kernel(2, *refs),
        (wide_shape, total_shape),
        [projected, partner],
        2,
        width,
    )

    def more(total, group):
        count = block_count(group)
        return attention_call(
            lambda *refs: more_keys_kernel(count, *refs),
            total_shape,
            [wide, total, *group],
            count,
            width,
            aliases={1: 0},
        )

    near, total = lax.optimization_barrier((near, total))
    beyond = hop(jnp.concatenate(near[:3], axis=0), "blk", lambda i: i ^ 2)
    near_partner = hop(jnp.concatenate(near, axis=0), "blk", lambda i: i ^ 1)
    total = more(total, near)
    near_partner, expert_weights, total = lax.optimization_barrier(
        (near_partner, expert_weights, total)
    )
    beside = hop(expert_weights, "blk", lambda i: i ^ 2)
    total = more(total, [near_partner])
    beyond, beside, total = lax.optimization_barrier((beyond, beside, total))
    beyond_partner = hop(beyond, "blk", lambda i: i ^ 1)
    pair = jnp.stack([expert_weights, beside])
    lane = [pair, *[hop(pair, "blk", lambda i, step=step: i ^ step) for step in (4, 8, 12)]]
    total = more(total, [beyond])
    beyond_partner, total = lax.optimization_barrier((beyond_partner, total))
    last = [beyond_partner]
    count = block_count(last)
    features = output_weight.shape[1]
    attended = attention_call(
        lambda *refs: last_keys_kernel(count, len(last), *refs),
        jax.ShapeDtypeStruct((owners, HD, features + width // owners), jnp.bfloat16),
        [wide, total, projected, output_weight, *last, partner, *near, near_partner, beyond],
        count,
        width,
        extra=[pltpu.VMEM(total_shape.shape, jnp.float32)],
    )
    return attended, lane


def add_rows(block, rows):
    return jnp.concatenate([block.reshape(-1, block.shape[-1]), rows], axis=0)


def dot_rows(first, second):
    return lax.dot_general(
        first, second, (((1,), (1,)), ((), ())), preferred_element_type=jnp.float32
    )


def tanh_part(values):
    return jnp.tanh(TANH_SCALE * (values + CUBE * (values * values * values)))


def tile_rows(lane_ref, partner_ref):
    share, width = lane_ref.shape[1:]
    return jnp.concatenate(
        [ref[...].reshape(2 * share, width) for ref in (lane_ref, partner_ref)], axis=0
    )


def weight_specs(weights):
    _, _, _, share, width = weights.shape
    return [
        pl.BlockSpec((None, 2, None, share, width), lambda i, which=which: (i, 0, which, 0, 0))
        for which in (0, 0, 1, 1)
    ]


def expert_forward_kernel(rows_ref, lane_ref, partner_ref, result_ref):
    rows = rows_ref[...]
    total = jnp.zeros(result_ref.shape, jnp.float32)
    for step in range(lane_ref.shape[0]):
        weights = [
            tile_rows(lane_ref.at[step, :, which], partner_ref.at[step, :, which])
            for which in range(2)
        ]
        pre_act = dot_rows(rows, weights[0])
        hidden = (pre_act * (0.5 * (1.0 + tanh_part(pre_act)))).astype(jnp.bfloat16)
        total += jnp.dot(hidden, weights[1], preferred_element_type=jnp.float32)
    result_ref[...] = total.astype(result_ref.dtype)


def expert_forward(rows, lane, partner):
    count, width = rows.shape
    hidden = lane.size // width
    return pl.pallas_call(
        expert_forward_kernel,
        out_shape=jax.ShapeDtypeStruct((count, width), jnp.bfloat16),
        in_specs=[pl.BlockSpec(memory_space=pltpu.VMEM)] * 3,
        out_specs=pl.BlockSpec(memory_space=pltpu.VMEM),
        compiler_params=pltpu.CompilerParams(vmem_limit_bytes=EXPERT_VMEM),
        cost_estimate=pl.CostEstimate(
            flops=4 * count * width * hidden,
            transcendentals=count * hidden,
            bytes_accessed=4 * hidden * width,
        ),
    )(rows, lane, partner)


def expert_slopes_kernel(
    rows_ref,
    in_lane,
    in_partner,
    out_lane,
    out_partner,
    hidden_ref,
    slope_ref,
    out_weight_ref,
    in_weight_ref,
):
    weight_in = tile_rows(in_lane, in_partner)
    out_weight_ref[...] = tile_rows(out_lane, out_partner)
    in_weight_ref[...] = weight_in.T
    pre_act = dot_rows(weight_in, rows_ref[...])
    tanh = tanh_part(pre_act)
    half = 0.5 * (1.0 + tanh)
    hidden_ref[...] = (pre_act * half).astype(hidden_ref.dtype)
    slope = half + pre_act * (0.5 * (1.0 - tanh * tanh)) * (
        TANH_SCALE * (1.0 + 3.0 * CUBE * (pre_act * pre_act))
    )
    slope_ref[...] = slope.astype(slope_ref.dtype)


def expert_slopes(rows, lane, partner):
    count, width = rows.shape
    hidden = lane.size // width
    tile = hidden // lane.shape[0]
    return pl.pallas_call(
        expert_slopes_kernel,
        grid=(lane.shape[0],),
        out_shape=(
            jax.ShapeDtypeStruct((hidden, count), jnp.bfloat16),
            jax.ShapeDtypeStruct((hidden, count), jnp.bfloat16),
            jax.ShapeDtypeStruct((hidden, width), jnp.bfloat16),
            jax.ShapeDtypeStruct((width, hidden), jnp.bfloat16),
        ),
        in_specs=[pl.BlockSpec((count, width), lambda i: (0, 0)), *weight_specs(lane)],
        out_specs=(
            pl.BlockSpec((tile, count), lambda i: (i, 0)),
            pl.BlockSpec((tile, count), lambda i: (i, 0)),
            pl.BlockSpec((tile, width), lambda i: (i, 0)),
            pl.BlockSpec((width, tile), lambda i: (0, i)),
        ),
        compiler_params=pltpu.CompilerParams(vmem_limit_bytes=EXPERT_VMEM),
        cost_estimate=pl.CostEstimate(
            flops=2 * count * width * hidden,
            transcendentals=count * hidden,
            bytes_accessed=6 * count * hidden + 8 * hidden * width,
        ),
    )(rows, lane, partner, lane, partner)


def store_shares(term, mine_ref, theirs_ref):
    share = mine_ref.shape[2]
    for y in range(2):
        mine_ref[0, y] = term[y * share : (y + 1) * share]
        theirs_ref[0, y] = term[(y + 2) * share : (y + 3) * share].astype(theirs_ref.dtype)


def routed_rows(grads_ref):
    sources, rows, width = grads_ref.shape
    rows = rows - SUM_ROWS
    return grads_ref[:, :rows, :].reshape(sources * rows, width)


def expert_out_grad_kernel(scale, hidden_ref, grads_ref, mine_ref, theirs_ref):
    term = jnp.dot(hidden_ref[...], routed_rows(grads_ref), preferred_element_type=jnp.float32)
    store_shares(term * scale, mine_ref, theirs_ref)


def expert_in_grad_kernel(
    scale,
    slope_ref,
    out_weight_ref,
    rows_ref,
    grads_ref,
    mine_ref,
    theirs_ref,
    pre_grad_ref,
):
    hidden_grad = dot_rows(out_weight_ref[...], routed_rows(grads_ref))
    pre_grad = (hidden_grad * slope_ref[...].astype(jnp.float32)).astype(jnp.bfloat16)
    pre_grad_ref[...] = pre_grad
    term = jnp.dot(pre_grad, rows_ref[...], preferred_element_type=jnp.float32)
    store_shares(term * scale, mine_ref, theirs_ref)


def rows_back_kernel(pre_grad_ref, in_weight_ref, back_ref):
    total = jnp.dot(in_weight_ref[...], pre_grad_ref[...], preferred_element_type=jnp.float32)
    back_ref[...] = total.T.astype(back_ref.dtype)


def share_shapes(hidden, width):
    shape = (4, 2, hidden // 16, width)
    spec = pl.BlockSpec((1, *shape[1:]), lambda i: (i, 0, 0, 0))
    shapes = (
        jax.ShapeDtypeStruct(shape, jnp.float32),
        jax.ShapeDtypeStruct(shape, jnp.bfloat16),
    )
    return shapes, (spec, spec)


def expert_out_grad(hidden, grads, scale):
    units, count = hidden.shape
    width = grads.shape[2]
    shapes, specs = share_shapes(units, width)
    return pl.pallas_call(
        lambda *refs: expert_out_grad_kernel(scale, *refs),
        grid=(4,),
        out_shape=shapes,
        in_specs=[
            pl.BlockSpec((units // 4, count), lambda i: (i, 0)),
            pl.BlockSpec(grads.shape, lambda i: (0, 0, 0)),
        ],
        out_specs=specs,
        compiler_params=pltpu.CompilerParams(vmem_limit_bytes=EXPERT_VMEM),
        cost_estimate=pl.CostEstimate(
            flops=2 * units * count * width, transcendentals=0, bytes_accessed=2 * units * count
        ),
    )(hidden, grads)


def expert_in_grad(slopes, out_weight, rows, grads, scale):
    units, count = slopes.shape
    width = grads.shape[2]
    shapes, specs = share_shapes(units, width)
    return pl.pallas_call(
        lambda *refs: expert_in_grad_kernel(scale, *refs),
        grid=(4,),
        out_shape=(*shapes, jax.ShapeDtypeStruct((units, count), jnp.bfloat16)),
        in_specs=[
            pl.BlockSpec((units // 4, count), lambda i: (i, 0)),
            pl.BlockSpec((units // 4, width), lambda i: (i, 0)),
            pl.BlockSpec((count, width), lambda i: (0, 0)),
            pl.BlockSpec(grads.shape, lambda i: (0, 0, 0)),
        ],
        out_specs=(*specs, pl.BlockSpec((units // 4, count), lambda i: (i, 0))),
        compiler_params=pltpu.CompilerParams(vmem_limit_bytes=EXPERT_VMEM),
        cost_estimate=pl.CostEstimate(
            flops=4 * units * count * width, transcendentals=0, bytes_accessed=6 * units * count
        ),
    )(slopes, out_weight, rows, grads)


def rows_back(pre_grad, in_weight):
    units, count = pre_grad.shape
    width = in_weight.shape[0]
    return pl.pallas_call(
        rows_back_kernel,
        out_shape=jax.ShapeDtypeStruct((count, width), jnp.bfloat16),
        in_specs=[pl.BlockSpec(memory_space=pltpu.VMEM)] * 2,
        out_specs=pl.BlockSpec(memory_space=pltpu.VMEM),
        compiler_params=pltpu.CompilerParams(vmem_limit_bytes=EXPERT_VMEM),
        cost_estimate=pl.CostEstimate(
            flops=units * count, transcendentals=0, bytes_accessed=count * width
        ),
    )(pre_grad, in_weight)


def swap(block, distance):
    return hop(block.astype(jnp.bfloat16), "blk", lambda i: i ^ distance)


def swap_over_z(blocks):
    return [swap(blocks[d], 4 * d) for d in (1, 2, 3)]


def add_swapped(own, swapped):
    first, second, third = [block.astype(jnp.float32) for block in swapped]
    return own + (first + (second + third))


def local(
    nodes,
    attention_weights,
    output_weight,
    router_weight,
    gain_first,
    gain_second,
    expert_in,
    expert_out,
    routes,
    cotangent,
):
    exp_count = lax.axis_size("exp")
    blk_count = lax.axis_size("blk")
    block_rows = nodes.shape[0]
    width = nodes.shape[1]
    features = attention_weights.shape[1]
    own_rows = block_rows // exp_count
    capacity = 4 * block_rows // (exp_count * exp_count)
    experts = router_weight.shape[0]
    grad_scale = 1.0 / math.sqrt(block_rows * blk_count)
    projected = jnp.einsum(
        "fd,td->ft",
        attention_weights.reshape(3 * features, width),
        nodes,
        preferred_element_type=jnp.float32,
    ).astype(jnp.bfloat16)
    attended, lane_parts = attention(
        projected, output_weight, jnp.concatenate([expert_in, expert_out], axis=0), exp_count
    )
    flat_routes = routes.reshape(2 * own_rows)
    choose = (flat_routes[:, None] == jnp.arange(experts, dtype=jnp.int32)[None, :]).astype(
        jnp.int32
    )
    before = jnp.cumsum(choose, axis=0) - choose
    slot_index = jnp.sum(before * choose, axis=1)
    position = flat_routes * capacity + slot_index
    from_heads = exchange(attended)
    lane = jnp.stack(lane_parts)
    from_heads, lane, position = lax.optimization_barrier((from_heads, lane, position))
    attn_out = jnp.einsum(
        "hfr,hfd->rd",
        from_heads[:, :, width:],
        from_heads[:, :, :width],
        preferred_element_type=jnp.float32,
    )
    own_nodes = lax.dynamic_slice_in_dim(
        nodes, lax.axis_index("exp") * own_rows, own_rows, 0
    ).astype(jnp.float32)
    stream = rms_gain(own_nodes + attn_out, gain_first).astype(jnp.bfloat16)
    lane_partner = hop(lane, "blk", lambda i: i ^ 1)
    logits = jnp.dot(stream, router_weight.T, preferred_element_type=jnp.float32)
    dispatch_table = (
        jnp.arange(experts * capacity, dtype=jnp.int32)[:, None] == position[None, :]
    ).astype(jnp.bfloat16)
    selected = choose.reshape(own_rows, 2, experts).astype(jnp.float32)

    def gate_values(values):
        picked = jnp.sum(jax.nn.sigmoid(values)[:, None, :] * selected, axis=-1)
        return picked / jnp.sum(picked, axis=-1, keepdims=True)

    gates, gate_back = jax.vjp(gate_values, logits)
    repeated = jnp.repeat(stream, 2, axis=0)
    outgoing = jnp.dot(dispatch_table, repeated, preferred_element_type=jnp.float32).astype(
        jnp.bfloat16
    )
    outgoing = outgoing.reshape(experts, capacity, width)
    arrived = exchange(outgoing).reshape(experts * capacity, width)
    result = expert_forward(arrived, lane, lane_partner)
    returned = exchange(result.reshape(experts, capacity, width))
    kept, result = lax.optimization_barrier((arrived, result))
    hidden, slopes, out_weight, in_weight = expert_slopes(kept, lane, lane_partner)
    returned, hidden, slopes = lax.optimization_barrier((returned, hidden, slopes))
    expert_rows = jnp.einsum(
        "ps,pd->sd",
        dispatch_table,
        returned.reshape(experts * capacity, width),
        preferred_element_type=jnp.float32,
    )
    expert_rows = expert_rows.reshape(own_rows, 2, width)
    mixture = gates[:, 0:1] * expert_rows[:, 0] + gates[:, 1:2] * expert_rows[:, 1]
    stream_two = stream.astype(jnp.float32) + mixture
    normed, norm_back = jax.vjp(rms_gain, stream_two, gain_second)
    layer_out = normed.astype(jnp.bfloat16)
    grad_two, gain_part = norm_back(cotangent.astype(jnp.float32))
    gate_grads = jnp.sum(expert_rows * grad_two[:, None, :], axis=-1)
    logit_grad = gate_back(gate_grads)[0]
    router_part = jnp.dot(
        logit_grad.T, stream.astype(jnp.float32), precision=lax.Precision.HIGHEST
    )
    small = jnp.concatenate([router_part, gain_part[None, :]], axis=0) * grad_scale
    sum_rows = jnp.pad(small, ((0, SUM_ROWS - small.shape[0]), (0, 0))).astype(jnp.bfloat16)
    assigned_grads = (
        (gates[..., None] * grad_two[:, None, :]).astype(jnp.bfloat16).reshape(2 * own_rows, width)
    )
    padded = capacity + SUM_ROWS
    place = jnp.arange(experts * padded, dtype=jnp.int32)[:, None]
    row_experts = jnp.concatenate([flat_routes, jnp.full((SUM_ROWS,), -1, jnp.int32)])
    row_slots = jnp.concatenate([slot_index, capacity + jnp.arange(SUM_ROWS, dtype=jnp.int32)])
    anywhere = jnp.logical_or(place // padded == row_experts[None, :], row_experts[None, :] < 0)
    spread = jnp.logical_and(anywhere, place % padded == row_slots[None, :])
    grad_outgoing = jnp.dot(
        spread.astype(jnp.bfloat16),
        jnp.concatenate([assigned_grads, sum_rows], axis=0),
        preferred_element_type=jnp.float32,
    ).astype(jnp.bfloat16)
    grad_arrived = exchange(grad_outgoing.reshape(experts, padded, width))
    out_mine, out_theirs = expert_out_grad(hidden, grad_arrived, grad_scale)
    out_mine, out_theirs, grad_arrived = lax.optimization_barrier(
        (out_mine, out_theirs, grad_arrived)
    )
    sum_rows = jnp.sum(grad_arrived[:, capacity:].astype(jnp.float32), axis=0)
    sum_rows = sum_rows.astype(jnp.bfloat16)
    sums_swapped = swap(sum_rows, 1)
    out_swapped = swap(out_theirs, 1)
    in_mine, in_theirs, pre_grad = expert_in_grad(
        slopes, out_weight, kept, grad_arrived, grad_scale
    )
    in_swapped = swap(in_theirs, 1)
    sums_swapped, out_swapped, in_mine, pre_grad = lax.optimization_barrier(
        (sums_swapped, out_swapped, in_mine, pre_grad)
    )
    sum_rows = (sum_rows.astype(jnp.float32) + sums_swapped.astype(jnp.float32)).astype(
        jnp.bfloat16
    )
    out_sums = out_mine + out_swapped.astype(jnp.float32)
    out_sent = add_rows(out_sums[:, 1].astype(jnp.bfloat16), sum_rows)
    out_beside = swap(out_sent, 2)
    in_sums = in_mine + in_swapped.astype(jnp.float32)
    in_parts = swap_over_z(in_sums)
    out_sent, out_sums, in_sums, pre_grad = lax.optimization_barrier(
        (out_sent, out_sums, in_sums, pre_grad)
    )
    row_grads = rows_back(pre_grad, in_weight)
    back_home = exchange(row_grads.reshape(experts, capacity, width))
    out_beside, in_sums = lax.optimization_barrier((out_beside, in_sums))
    sum_rows = (
        out_sent[-SUM_ROWS:].astype(jnp.float32) + out_beside[-SUM_ROWS:].astype(jnp.float32)
    ).astype(jnp.bfloat16)
    out_sums = out_sums[:, 0] + out_beside[:-SUM_ROWS].reshape(out_sums.shape[:1] + out_sums.shape[2:])
    out_parts = [
        swap(add_rows(out_sums[d].astype(jnp.bfloat16), sum_rows), 4 * d) for d in (1, 2, 3)
    ]
    expert_out_grads = add_swapped(out_sums[0], [part[:-SUM_ROWS] for part in out_parts])[None]
    first, second, third = [part[-SUM_ROWS:].astype(jnp.float32) for part in out_parts]
    sums = (sum_rows.astype(jnp.float32) + first) + (second + third)
    router_grad, gain_grad = sums[:experts], sums[experts]
    in_sums = add_swapped(in_sums[0], in_parts)
    in_beside = swap(in_sums[1], 2)
    back_home, in_beside, expert_out_grads = lax.optimization_barrier(
        (back_home, in_beside, expert_out_grads)
    )
    expert_in_grads = (in_sums[0] + in_beside.astype(jnp.float32))[None]
    back_rows = jnp.einsum(
        "ps,pd->sd",
        dispatch_table,
        back_home.reshape(experts * capacity, width),
        preferred_element_type=jnp.float32,
    )
    back_rows = back_rows.reshape(own_rows, 2, width)
    router_term = jnp.dot(
        logit_grad, router_weight.astype(jnp.float32), precision=lax.Precision.HIGHEST
    )
    stream_grad = (grad_two + (back_rows[:, 0] + back_rows[:, 1]) + router_term).astype(
        jnp.bfloat16
    )
    return (layer_out, stream_grad, expert_in_grads, expert_out_grads, router_grad, gain_grad)


def solution(mesh):
    placed = (
        P("blk", None),
        P(None, "exp", None),
        P("exp", None),
        P(),
        P(),
        P(),
        P("exp", "blk", None),
        P("exp", "blk", None),
        P(("blk", "exp"), None),
        P(("blk", "exp"), None),
    )
    return jax.shard_map(
        local,
        mesh=mesh,
        in_specs=placed,
        out_specs=(
            P(("blk", "exp"), None),
            P(("blk", "exp"), None),
            P("exp", "blk", None),
            P("exp", "blk", None),
            P(),
            P(),
        ),
        check_vma=False,
    )
```

```python
import math

import jax
import jax.numpy as jnp
from jax import lax
from jax.experimental import pallas as pl
from jax.experimental.pallas import tpu as pltpu
from jax.sharding import PartitionSpec as P

HD = 32

EPSILON = 1e-06
LOG2_SCALE = math.log2(math.e) / math.sqrt(HD)
SHIFT_KEYS = 256
SUM_LIMIT = 2.0**100
ATTENTION_VMEM = 40 * 2**20
EXPERT_VMEM = 24 * 2**20
SUM_ROWS = 16
TANH_SCALE = math.sqrt(2.0 / math.pi)
CUBE = 0.044715


def rms_gain(stream, gain):
    return stream * lax.rsqrt(jnp.mean(stream * stream, axis=-1, keepdims=True) + EPSILON) * gain


def exchange(buffer):
    return lax.all_to_all(buffer, "exp", split_axis=0, concat_axis=0, tiled=True)


def hop(value, axis, target):
    count = lax.axis_size(axis)
    return lax.ppermute(value, axis, [(i, target(i) % count) for i in range(count)])


def split_terms(value, terms):
    pieces = []
    for _ in range(terms):
        piece = value.astype(jnp.bfloat16)
        pieces.append(piece)
        value = value - piece.astype(jnp.float32)
    return pieces


def key_blocks(refs):
    return [
        (ref, start) for ref in refs for start in range(0, ref.shape[0], 2 * HD)
    ]


def own_blocks(own_ref):
    return [(own_ref, HD)]


def load_keys(blocks, keys, values):
    width = blocks[0][0].shape[1]
    ones = (lax.broadcasted_iota(jnp.int32, (HD, width), 0) < 3).astype(jnp.bfloat16)
    one = (lax.broadcasted_iota(jnp.int32, (HD // 2, width), 0) < 1).astype(jnp.bfloat16)
    for index, (ref, start) in enumerate(blocks):
        block = ref[start : start + HD, :]
        span = slice(index * width, (index + 1) * width)
        keys[span, :] = jnp.concatenate([block, block, block, ones], axis=0).T
        values[:, span] = jnp.concatenate([ref[start + HD : start + 2 * HD, :], one], axis=0)


def add_blocks(count, width, query, keys, values, total):
    chunk = width // 2

    def step(index, running):
        span = pl.ds(pl.multiple_of(index * chunk, chunk), chunk)
        exponents = jnp.dot(keys[span, :], query, preferred_element_type=jnp.float32)
        weights = jnp.exp2(exponents).astype(jnp.bfloat16)
        return running + jnp.dot(values[:, span], weights, preferred_element_type=jnp.float32)

    return lax.fori_loop(0, 2 * count, step, total)


def first_keys_kernel(count, own_ref, *refs):
    blocks, (wide_ref, total_ref, keys, values) = refs[:-4], refs[-4:]
    load_keys(own_blocks(own_ref) + key_blocks(blocks), keys, values)
    width = own_ref.shape[1]
    scaled = own_ref[:HD, :].astype(jnp.float32) * LOG2_SCALE
    pieces = split_terms(scaled, 3)
    wide_ref[...] = jnp.concatenate(pieces + [jnp.zeros_like(pieces[0])], axis=0)
    some = jnp.dot(keys[:SHIFT_KEYS, :], wide_ref[...], preferred_element_type=jnp.float32)
    shift = split_terms(-jnp.max(some, axis=0, keepdims=True), 3)
    row = lax.broadcasted_iota(jnp.int32, (HD, width), 0)
    rows = jnp.zeros((HD, width), jnp.float32)
    for index, piece in enumerate(shift):
        rows = jnp.where(row == index, piece.astype(jnp.float32), rows)
    wide_ref[3 * HD :, :] = rows.astype(jnp.bfloat16)
    total_ref[...] = add_blocks(
        count, width, wide_ref[...], keys, values, jnp.zeros(total_ref.shape, jnp.float32)
    )


def more_keys_kernel(count, wide_ref, before_ref, *refs):
    blocks, (total_ref, keys, values) = refs[:-3], refs[-3:]
    load_keys(key_blocks(blocks), keys, values)
    total_ref[...] = add_blocks(
        count, wide_ref.shape[1], wide_ref[...], keys, values, before_ref[...]
    )


def last_keys_kernel(count, fresh, wide_ref, before_ref, own_ref, output_weight_ref, *refs):
    blocks, (out_ref, keys, values, total) = refs[:-4], refs[-4:]
    load_keys(key_blocks(blocks[:fresh]), keys, values)
    width = wide_ref.shape[1]
    total[...] = add_blocks(count, width, wide_ref[...], keys, values, before_ref[...])
    sums = total[HD : HD + 1, :]
    inside = jnp.logical_and(sums <= SUM_LIMIT, sums >= 1.0 / SUM_LIMIT)
    outside = jnp.sum(jnp.where(inside, 0, 1))

    @pl.when(outside > 0)
    def _():
        query = own_ref[:HD, :]
        query = jnp.concatenate([query, jnp.zeros((3 * HD, width), query.dtype)], axis=0)
        total[...] = jnp.zeros(total.shape, jnp.float32)

        def step(index, top):
            span = pl.ds(pl.multiple_of(index * SHIFT_KEYS, SHIFT_KEYS), SHIFT_KEYS)
            scores = LOG2_SCALE * jnp.dot(
                keys[span, :], query, preferred_element_type=jnp.float32
            )
            new_top = jnp.maximum(top, jnp.max(scores, axis=0, keepdims=True))
            weights = jnp.exp2(scores - new_top).astype(jnp.bfloat16)
            total[...] = total[...] * jnp.exp2(top - new_top) + jnp.dot(
                values[:, span], weights, preferred_element_type=jnp.float32
            )
            return new_top

        top = jnp.full((1, width), -1e30, jnp.float32)
        every = own_blocks(own_ref) + key_blocks(blocks)
        for group in [every[i : i + count] for i in range(0, len(every), count)]:
            load_keys(group, keys, values)
            top = lax.fori_loop(0, len(group) * (width // SHIFT_KEYS), step, top)

    attended = (total[:HD, :] / total[HD : HD + 1, :]).astype(jnp.bfloat16)
    weight = output_weight_ref[...]
    features = weight.shape[1]
    rows = out_ref.shape[2] - features
    for index in range(out_ref.shape[0]):
        out_ref[index, :, :features] = weight
        out_ref[index, :, features:] = attended[:, index * rows : (index + 1) * rows]


def block_count(arrays):
    return sum(array.shape[0] for array in arrays) // (2 * HD)


def attention_call(kernel, out_shape, operands, count, width, extra=(), aliases=None):
    specs = [pl.BlockSpec(memory_space=pltpu.VMEM)]
    return pl.pallas_call(
        kernel,
        out_shape=out_shape,
        in_specs=specs * len(operands),
        out_specs=jax.tree.map(lambda _: specs[0], out_shape),
        scratch_shapes=[
            pltpu.VMEM((count * width, 4 * HD), jnp.bfloat16),
            pltpu.VMEM((HD + HD // 2, count * width), jnp.bfloat16),
            *extra,
        ],
        input_output_aliases=aliases or {},
        compiler_params=pltpu.CompilerParams(vmem_limit_bytes=ATTENTION_VMEM),
        cost_estimate=pl.CostEstimate(
            flops=count * width * width * 1200,
            transcendentals=count * width * width,
            bytes_accessed=count * width * 4 * HD,
        ),
    )(*operands)


def near_hops(value):
    return [hop(value, "blk", lambda i, step=step: i ^ step) for step in (8, 12, 4, 2)]


def attention(projected, output_weight, expert_weights, owners):
    width = projected.shape[1]
    keys_values = projected[HD:]
    partner = hop(keys_values, "blk", lambda i: i ^ 1)
    near = near_hops(keys_values)
    total_shape = jax.ShapeDtypeStruct((HD + HD // 2, width), jnp.float32)
    wide_shape = jax.ShapeDtypeStruct((4 * HD, width), jnp.bfloat16)
    wide, total = attention_call(
        lambda *refs: first_keys_kernel(2, *refs),
        (wide_shape, total_shape),
        [projected, partner],
        2,
        width,
    )

    def more(total, group):
        count = block_count(group)
        return attention_call(
            lambda *refs: more_keys_kernel(count, *refs),
            total_shape,
            [wide, total, *group],
            count,
            width,
            aliases={1: 0},
        )

    near, total = lax.optimization_barrier((near, total))
    beyond = hop(jnp.concatenate(near[:3], axis=0), "blk", lambda i: i ^ 2)
    near_partner = hop(jnp.concatenate(near, axis=0), "blk", lambda i: i ^ 1)
    total = more(total, near)
    near_partner, expert_weights, total = lax.optimization_barrier(
        (near_partner, expert_weights, total)
    )
    beside = hop(expert_weights, "blk", lambda i: i ^ 2)
    total = more(total, [near_partner])
    beyond, beside, total = lax.optimization_barrier((beyond, beside, total))
    beyond_partner = hop(beyond, "blk", lambda i: i ^ 1)
    pair = jnp.stack([expert_weights, beside])
    lane = [pair, *[hop(pair, "blk", lambda i, step=step: i ^ step) for step in (4, 8, 12)]]
    total = more(total, [beyond])
    beyond_partner, total = lax.optimization_barrier((beyond_partner, total))
    last = [beyond_partner]
    count = block_count(last)
    features = output_weight.shape[1]
    attended = attention_call(
        lambda *refs: last_keys_kernel(count, len(last), *refs),
        jax.ShapeDtypeStruct((owners, HD, features + width // owners), jnp.bfloat16),
        [wide, total, projected, output_weight, *last, partner, *near, near_partner, beyond],
        count,
        width,
        extra=[pltpu.VMEM(total_shape.shape, jnp.float32)],
    )
    return attended, lane


def add_rows(block, rows):
    return jnp.concatenate([block.reshape(-1, block.shape[-1]), rows], axis=0)


def dot_rows(first, second):
    return lax.dot_general(
        first, second, (((1,), (1,)), ((), ())), preferred_element_type=jnp.float32
    )


def tanh_part(values):
    return jnp.tanh(TANH_SCALE * (values + CUBE * (values * values * values)))


def tile_rows(lane_ref, partner_ref):
    share, width = lane_ref.shape[1:]
    return jnp.concatenate(
        [ref[...].reshape(2 * share, width) for ref in (lane_ref, partner_ref)], axis=0
    )


def weight_specs(weights):
    _, _, _, share, width = weights.shape
    return [
        pl.BlockSpec((None, 2, None, share, width), lambda i, which=which: (i, 0, which, 0, 0))
        for which in (0, 0, 1, 1)
    ]


def expert_forward_kernel(rows_ref, lane_ref, partner_ref, result_ref):
    rows = rows_ref[...]
    total = jnp.zeros(result_ref.shape, jnp.float32)
    for step in range(lane_ref.shape[0]):
        weights = [
            tile_rows(lane_ref.at[step, :, which], partner_ref.at[step, :, which])
            for which in range(2)
        ]
        pre_act = dot_rows(rows, weights[0])
        hidden = (pre_act * (0.5 * (1.0 + tanh_part(pre_act)))).astype(jnp.bfloat16)
        total += jnp.dot(hidden, weights[1], preferred_element_type=jnp.float32)
    result_ref[...] = total.astype(result_ref.dtype)


def expert_forward(rows, lane, partner):
    count, width = rows.shape
    hidden = lane.size // width
    return pl.pallas_call(
        expert_forward_kernel,
        out_shape=jax.ShapeDtypeStruct((count, width), jnp.bfloat16),
        in_specs=[pl.BlockSpec(memory_space=pltpu.VMEM)] * 3,
        out_specs=pl.BlockSpec(memory_space=pltpu.VMEM),
        compiler_params=pltpu.CompilerParams(vmem_limit_bytes=EXPERT_VMEM),
        cost_estimate=pl.CostEstimate(
            flops=4 * count * width * hidden,
            transcendentals=count * hidden,
            bytes_accessed=4 * hidden * width,
        ),
    )(rows, lane, partner)


def expert_slopes_kernel(
    rows_ref,
    in_lane,
    in_partner,
    out_lane,
    out_partner,
    hidden_ref,
    slope_ref,
    out_weight_ref,
    in_weight_ref,
):
    weight_in = tile_rows(in_lane, in_partner)
    out_weight_ref[...] = tile_rows(out_lane, out_partner)
    in_weight_ref[...] = weight_in.T
    pre_act = dot_rows(weight_in, rows_ref[...])
    tanh = tanh_part(pre_act)
    half = 0.5 * (1.0 + tanh)
    hidden_ref[...] = (pre_act * half).astype(hidden_ref.dtype)
    slope = half + pre_act * (0.5 * (1.0 - tanh * tanh)) * (
        TANH_SCALE * (1.0 + 3.0 * CUBE * (pre_act * pre_act))
    )
    slope_ref[...] = slope.astype(slope_ref.dtype)


def expert_slopes(rows, lane, partner):
    count, width = rows.shape
    hidden = lane.size // width
    tile = hidden // lane.shape[0]
    return pl.pallas_call(
        expert_slopes_kernel,
        grid=(lane.shape[0],),
        out_shape=(
            jax.ShapeDtypeStruct((hidden, count), jnp.bfloat16),
            jax.ShapeDtypeStruct((hidden, count), jnp.bfloat16),
            jax.ShapeDtypeStruct((hidden, width), jnp.bfloat16),
            jax.ShapeDtypeStruct((width, hidden), jnp.bfloat16),
        ),
        in_specs=[pl.BlockSpec((count, width), lambda i: (0, 0)), *weight_specs(lane)],
        out_specs=(
            pl.BlockSpec((tile, count), lambda i: (i, 0)),
            pl.BlockSpec((tile, count), lambda i: (i, 0)),
            pl.BlockSpec((tile, width), lambda i: (i, 0)),
            pl.BlockSpec((width, tile), lambda i: (0, i)),
        ),
        compiler_params=pltpu.CompilerParams(vmem_limit_bytes=EXPERT_VMEM),
        cost_estimate=pl.CostEstimate(
            flops=2 * count * width * hidden,
            transcendentals=count * hidden,
            bytes_accessed=6 * count * hidden + 8 * hidden * width,
        ),
    )(rows, lane, partner, lane, partner)


def store_shares(term, mine_ref, theirs_ref):
    share = mine_ref.shape[2]
    for y in range(2):
        mine_ref[0, y] = term[y * share : (y + 1) * share]
        theirs_ref[0, y] = term[(y + 2) * share : (y + 3) * share].astype(theirs_ref.dtype)


def routed_rows(grads_ref):
    sources, rows, width = grads_ref.shape
    rows = rows - SUM_ROWS
    return grads_ref[:, :rows, :].reshape(sources * rows, width)


def expert_out_grad_kernel(scale, hidden_ref, grads_ref, mine_ref, theirs_ref):
    term = jnp.dot(hidden_ref[...], routed_rows(grads_ref), preferred_element_type=jnp.float32)
    store_shares(term * scale, mine_ref, theirs_ref)


def expert_in_grad_kernel(
    scale,
    slope_ref,
    out_weight_ref,
    rows_ref,
    grads_ref,
    mine_ref,
    theirs_ref,
    pre_grad_ref,
):
    hidden_grad = dot_rows(out_weight_ref[...], routed_rows(grads_ref))
    pre_grad = (hidden_grad * slope_ref[...].astype(jnp.float32)).astype(jnp.bfloat16)
    pre_grad_ref[...] = pre_grad
    term = jnp.dot(pre_grad, rows_ref[...], preferred_element_type=jnp.float32)
    store_shares(term * scale, mine_ref, theirs_ref)


def rows_back_kernel(pre_grad_ref, in_weight_ref, back_ref):
    total = jnp.dot(in_weight_ref[...], pre_grad_ref[...], preferred_element_type=jnp.float32)
    back_ref[...] = total.T.astype(back_ref.dtype)


def share_shapes(hidden, width):
    shape = (4, 2, hidden // 16, width)
    spec = pl.BlockSpec((1, *shape[1:]), lambda i: (i, 0, 0, 0))
    shapes = (
        jax.ShapeDtypeStruct(shape, jnp.float32),
        jax.ShapeDtypeStruct(shape, jnp.bfloat16),
    )
    return shapes, (spec, spec)


def expert_out_grad(hidden, grads, scale):
    units, count = hidden.shape
    width = grads.shape[2]
    shapes, specs = share_shapes(units, width)
    return pl.pallas_call(
        lambda *refs: expert_out_grad_kernel(scale, *refs),
        grid=(4,),
        out_shape=shapes,
        in_specs=[
            pl.BlockSpec((units // 4, count), lambda i: (i, 0)),
            pl.BlockSpec(grads.shape, lambda i: (0, 0, 0)),
        ],
        out_specs=specs,
        compiler_params=pltpu.CompilerParams(vmem_limit_bytes=EXPERT_VMEM),
        cost_estimate=pl.CostEstimate(
            flops=2 * units * count * width, transcendentals=0, bytes_accessed=2 * units * count
        ),
    )(hidden, grads)


def expert_in_grad(slopes, out_weight, rows, grads, scale):
    units, count = slopes.shape
    width = grads.shape[2]
    shapes, specs = share_shapes(units, width)
    return pl.pallas_call(
        lambda *refs: expert_in_grad_kernel(scale, *refs),
        grid=(4,),
        out_shape=(*shapes, jax.ShapeDtypeStruct((units, count), jnp.bfloat16)),
        in_specs=[
            pl.BlockSpec((units // 4, count), lambda i: (i, 0)),
            pl.BlockSpec((units // 4, width), lambda i: (i, 0)),
            pl.BlockSpec((count, width), lambda i: (0, 0)),
            pl.BlockSpec(grads.shape, lambda i: (0, 0, 0)),
        ],
        out_specs=(*specs, pl.BlockSpec((units // 4, count), lambda i: (i, 0))),
        compiler_params=pltpu.CompilerParams(vmem_limit_bytes=EXPERT_VMEM),
        cost_estimate=pl.CostEstimate(
            flops=4 * units * count * width, transcendentals=0, bytes_accessed=6 * units * count
        ),
    )(slopes, out_weight, rows, grads)


def rows_back(pre_grad, in_weight):
    units, count = pre_grad.shape
    width = in_weight.shape[0]
    return pl.pallas_call(
        rows_back_kernel,
        out_shape=jax.ShapeDtypeStruct((count, width), jnp.bfloat16),
        in_specs=[pl.BlockSpec(memory_space=pltpu.VMEM)] * 2,
        out_specs=pl.BlockSpec(memory_space=pltpu.VMEM),
        compiler_params=pltpu.CompilerParams(vmem_limit_bytes=EXPERT_VMEM),
        cost_estimate=pl.CostEstimate(
            flops=units * count, transcendentals=0, bytes_accessed=count * width
        ),
    )(pre_grad, in_weight)


def swap(block, distance):
    return hop(block.astype(jnp.bfloat16), "blk", lambda i: i ^ distance)


def swap_over_z(blocks):
    return [swap(blocks[d], 4 * d) for d in (1, 2, 3)]


def add_swapped(own, swapped):
    first, second, third = [block.astype(jnp.float32) for block in swapped]
    return own + (first + (second + third))


def local(
    nodes,
    attention_weights,
    output_weight,
    router_weight,
    gain_first,
    gain_second,
    expert_in,
    expert_out,
    routes,
    cotangent,
):
    exp_count = lax.axis_size("exp")
    blk_count = lax.axis_size("blk")
    block_rows = nodes.shape[0]
    width = nodes.shape[1]
    features = attention_weights.shape[1]
    own_rows = block_rows // exp_count
    capacity = 4 * block_rows // (exp_count * exp_count)
    experts = router_weight.shape[0]
    grad_scale = 1.0 / math.sqrt(block_rows * blk_count)
    projected = jnp.einsum(
        "fd,td->ft",
        attention_weights.reshape(3 * features, width),
        nodes,
        preferred_element_type=jnp.float32,
    ).astype(jnp.bfloat16)
    attended, lane_parts = attention(
        projected, output_weight, jnp.concatenate([expert_in, expert_out], axis=0), exp_count
    )
    flat_routes = routes.reshape(2 * own_rows)
    choose = (flat_routes[:, None] == jnp.arange(experts, dtype=jnp.int32)[None, :]).astype(
        jnp.int32
    )
    before = jnp.cumsum(choose, axis=0) - choose
    slot_index = jnp.sum(before * choose, axis=1)
    position = flat_routes * capacity + slot_index
    from_heads = exchange(attended)
    lane = jnp.stack(lane_parts)
    from_heads, lane, position = lax.optimization_barrier((from_heads, lane, position))
    attn_out = jnp.einsum(
        "hfr,hfd->rd",
        from_heads[:, :, width:],
        from_heads[:, :, :width],
        preferred_element_type=jnp.float32,
    )
    own_nodes = lax.dynamic_slice_in_dim(
        nodes, lax.axis_index("exp") * own_rows, own_rows, 0
    ).astype(jnp.float32)
    stream = rms_gain(own_nodes + attn_out, gain_first).astype(jnp.bfloat16)
    lane_partner = hop(lane, "blk", lambda i: i ^ 1)
    logits = jnp.dot(stream, router_weight.T, preferred_element_type=jnp.float32)
    dispatch_table = (
        jnp.arange(experts * capacity, dtype=jnp.int32)[:, None] == position[None, :]
    ).astype(jnp.bfloat16)
    selected = choose.reshape(own_rows, 2, experts).astype(jnp.float32)

    def gate_values(values):
        picked = jnp.sum(jax.nn.sigmoid(values)[:, None, :] * selected, axis=-1)
        return picked / jnp.sum(picked, axis=-1, keepdims=True)

    gates, gate_back = jax.vjp(gate_values, logits)
    repeated = jnp.repeat(stream, 2, axis=0)
    outgoing = jnp.dot(dispatch_table, repeated, preferred_element_type=jnp.float32).astype(
        jnp.bfloat16
    )
    outgoing = outgoing.reshape(experts, capacity, width)
    arrived = exchange(outgoing).reshape(experts * capacity, width)
    result = expert_forward(arrived, lane, lane_partner)
    returned = exchange(result.reshape(experts, capacity, width))
    kept, result = lax.optimization_barrier((arrived, result))
    hidden, slopes, out_weight, in_weight = expert_slopes(kept, lane, lane_partner)
    returned, hidden, slopes = lax.optimization_barrier((returned, hidden, slopes))
    expert_rows = jnp.einsum(
        "ps,pd->sd",
        dispatch_table,
        returned.reshape(experts * capacity, width),
        preferred_element_type=jnp.float32,
    )
    expert_rows = expert_rows.reshape(own_rows, 2, width)
    mixture = gates[:, 0:1] * expert_rows[:, 0] + gates[:, 1:2] * expert_rows[:, 1]
    stream_two = stream.astype(jnp.float32) + mixture
    normed, norm_back = jax.vjp(rms_gain, stream_two, gain_second)
    layer_out = normed.astype(jnp.bfloat16)
    grad_two, gain_part = norm_back(cotangent.astype(jnp.float32))
    gate_grads = jnp.sum(expert_rows * grad_two[:, None, :], axis=-1)
    logit_grad = gate_back(gate_grads)[0]
    router_part = jnp.dot(
        logit_grad.T, stream.astype(jnp.float32), precision=lax.Precision.HIGHEST
    )
    small = jnp.concatenate([router_part, gain_part[None, :]], axis=0) * grad_scale
    sum_rows = jnp.pad(small, ((0, SUM_ROWS - small.shape[0]), (0, 0))).astype(jnp.bfloat16)
    assigned_grads = (
        (gates[..., None] * grad_two[:, None, :]).astype(jnp.bfloat16).reshape(2 * own_rows, width)
    )
    padded = capacity + SUM_ROWS
    place = jnp.arange(experts * padded, dtype=jnp.int32)[:, None]
    row_experts = jnp.concatenate([flat_routes, jnp.full((SUM_ROWS,), -1, jnp.int32)])
    row_slots = jnp.concatenate([slot_index, capacity + jnp.arange(SUM_ROWS, dtype=jnp.int32)])
    anywhere = jnp.logical_or(place // padded == row_experts[None, :], row_experts[None, :] < 0)
    spread = jnp.logical_and(anywhere, place % padded == row_slots[None, :])
    grad_outgoing = jnp.dot(
        spread.astype(jnp.bfloat16),
        jnp.concatenate([assigned_grads, sum_rows], axis=0),
        preferred_element_type=jnp.float32,
    ).astype(jnp.bfloat16)
    grad_arrived = exchange(grad_outgoing.reshape(experts, padded, width))
    out_mine, out_theirs = expert_out_grad(hidden, grad_arrived, grad_scale)
    out_mine, out_theirs, grad_arrived = lax.optimization_barrier(
        (out_mine, out_theirs, grad_arrived)
    )
    sum_rows = jnp.sum(grad_arrived[:, capacity:].astype(jnp.float32), axis=0)
    sum_rows = sum_rows.astype(jnp.bfloat16)
    sums_swapped = swap(sum_rows, 1)
    out_swapped = swap(out_theirs, 1)
    in_mine, in_theirs, pre_grad = expert_in_grad(
        slopes, out_weight, kept, grad_arrived, grad_scale
    )
    in_swapped = swap(in_theirs, 1)
    sums_swapped, out_swapped, in_mine, pre_grad = lax.optimization_barrier(
        (sums_swapped, out_swapped, in_mine, pre_grad)
    )
    sum_rows = (sum_rows.astype(jnp.float32) + sums_swapped.astype(jnp.float32)).astype(
        jnp.bfloat16
    )
    out_sums = out_mine + out_swapped.astype(jnp.float32)
    out_sent = add_rows(out_sums[:, 1].astype(jnp.bfloat16), sum_rows)
    out_beside = swap(out_sent, 2)
    in_sums = in_mine + in_swapped.astype(jnp.float32)
    in_parts = swap_over_z(in_sums)
    out_sent, out_sums, in_sums, pre_grad = lax.optimization_barrier(
        (out_sent, out_sums, in_sums, pre_grad)
    )
    row_grads = rows_back(pre_grad, in_weight)
    back_home = exchange(row_grads.reshape(experts, capacity, width))
    out_beside, in_sums = lax.optimization_barrier((out_beside, in_sums))
    own = add_rows(out_sums[:, 0], out_sent[-SUM_ROWS:].astype(jnp.float32))
    own = own + out_beside.astype(jnp.float32)
    sum_rows = own[-SUM_ROWS:].astype(jnp.bfloat16)
    out_sums = own[:-SUM_ROWS].reshape(out_sums.shape[0], -1, width)
    out_parts = [
        swap(add_rows(out_sums[d].astype(jnp.bfloat16), sum_rows), 4 * d) for d in (1, 2, 3)
    ]
    first, second, third = [part.astype(jnp.float32) for part in out_parts]
    totals = (add_rows(out_sums[0], sum_rows.astype(jnp.float32)) + first) + (second + third)
    expert_out_grads, sums = totals[None, :-SUM_ROWS], totals[-SUM_ROWS:]
    router_grad, gain_grad = sums[:experts], sums[experts]
    in_sums = add_swapped(in_sums[0], in_parts)
    in_beside = swap(in_sums[1], 2)
    back_home, in_beside, expert_out_grads = lax.optimization_barrier(
        (back_home, in_beside, expert_out_grads)
    )
    expert_in_grads = (in_sums[0] + in_beside.astype(jnp.float32))[None]
    back_rows = jnp.einsum(
        "ps,pd->sd",
        dispatch_table,
        back_home.reshape(experts * capacity, width),
        preferred_element_type=jnp.float32,
    )
    back_rows = back_rows.reshape(own_rows, 2, width)
    router_term = jnp.dot(
        logit_grad, router_weight.astype(jnp.float32), precision=lax.Precision.HIGHEST
    )
    stream_grad = (grad_two + (back_rows[:, 0] + back_rows[:, 1]) + router_term).astype(
        jnp.bfloat16
    )
    return (layer_out, stream_grad, expert_in_grads, expert_out_grads, router_grad, gain_grad)


def solution(mesh):
    placed = (
        P("blk", None),
        P(None, "exp", None),
        P("exp", None),
        P(),
        P(),
        P(),
        P("exp", "blk", None),
        P("exp", "blk", None),
        P(("blk", "exp"), None),
        P(("blk", "exp"), None),
    )
    return jax.shard_map(
        local,
        mesh=mesh,
        in_specs=placed,
        out_specs=(
            P(("blk", "exp"), None),
            P(("blk", "exp"), None),
            P("exp", "blk", None),
            P("exp", "blk", None),
            P(),
            P(),
        ),
        check_vma=False,
    )
```
